32 devices in a mesh: rows: 2 (over x), cols: 2 (over core), imgs: 8 (over z, y).
Axes of the slice: x: 2, y: 2, z: 4, core: 2. Of those that a mesh axis runs over, the one named last changes fastest.
Arguments:
- patches: bfloat16 [8, 30, 30, 768], P('imgs', 'rows', 'cols'), may hold values from -6 to 6
- patch_mask: int32 [8, 30, 30], P('imgs'), may hold values from 0 to 1, as said below
- norm1_gain: float32 [768], replicated, may hold values from 0.1 to 1.9
- norm1_shift: float32 [768], replicated, may hold values from -3 to 3
- qkv_weight: bfloat16 [768, 2304], replicated, may hold values from -0.21875 to 0.21875
- qv_bias: float32 [768, 2], replicated, may hold values from -3 to 3
- out_weight: bfloat16 [768, 768], replicated, may hold values from -1.25 to 1.25
- out_bias: float32 [768], replicated, may hold values from -3 to 3
- norm2_gain: float32 [768], replicated, may hold values from 0.1 to 1.9
- norm2_shift: float32 [768], replicated, may hold values from -3 to 3
- fc1_weight: bfloat16 [768, 3072], replicated, may hold values from -0.21875 to 0.21875
- fc1_bias: float32 [3072], replicated, may hold values from -3 to 3
- fc2_weight: bfloat16 [3072, 768], replicated, may hold values from -0.109375 to 0.109375
- fc2_bias: float32 [768], replicated, may hold values from -3 to 3
- cotangent: bfloat16 [8, 30, 30, 768], P('imgs', 'rows', 'cols'), may hold values from -6 to 6
Outputs:
- layer_out: bfloat16 [8, 30, 30, 768], P('imgs', 'rows', 'cols')
- patches_grad: bfloat16 [8, 30, 30, 768], P('imgs', 'rows', 'cols')
- norm1_gain_grad: float32 [768], P('imgs')
- norm1_shift_grad: float32 [768], P('imgs')
- qkv_weight_grad: float32 [768, 2304], P('imgs')
- qv_bias_grad: float32 [768, 2], P('imgs')
- out_weight_grad: float32 [768, 768], P('imgs')
- out_bias_grad: float32 [768], P('imgs')
- norm2_gain_grad: float32 [768], P('imgs')
- norm2_shift_grad: float32 [768], P('imgs')
- fc1_weight_grad: float32 [768, 3072], P('imgs')
- fc1_bias_grad: float32 [3072], P('imgs')
- fc2_weight_grad: float32 [3072, 768], P('imgs')
- fc2_bias_grad: float32 [768], P('imgs')
The draws below stay inside these ranges and needn't reach their ends.
Inputs may be any that keep to these rules, and one draw needn't show every extreme that they name: For each image, patch_mask is 1 on a rectangle of h rows and w columns at the top left of the grid and 0 elsewhere, with 12 <= h, w <= 30; image 0 is whole and image 1 has h = w = 12.
All inputs are finite; a program needn't handle non-finite values.
Results may differ from the reference program's by a relative error of at most 0.012.
Values may be sent and summed in bfloat16 or wider, within the bound.
No kernel may reach another device: no remote copies, remote signals or barrier semaphores. Data moves between devices by JAX's collectives and lax.ppermute only.
A program may use at most 128 MiB of HBM per device.

```python
import jax
import jax.numpy as jnp
from jax import lax

D = 768
HEADS = 12
FF = 3072
GRID = 30
IMAGES = 8


def draw_patch_mask(key, part):
    height_key, width_key = jax.random.split(jax.random.fold_in(key, 7))
    low_edge = GRID * 2 // 5
    heights = jax.random.randint(height_key, (IMAGES,), low_edge, GRID + 1)
    widths = jax.random.randint(width_key, (IMAGES,), low_edge, GRID + 1)
    heights = heights.at[0].set(GRID).at[1].set(low_edge)
    widths = widths.at[0].set(GRID).at[1].set(low_edge)
    places = jnp.arange(GRID)
    rows_ok = places[None, :] < heights[:, None]
    cols_ok = places[None, :] < widths[:, None]
    return (rows_ok[:, :, None] & cols_ok[:, None, :]).astype(jnp.int32)


def block_levels(stream_key, dims, cuts, least, high):
    level = 1.0
    for position, blocks in cuts:
        draws = jax.random.uniform(jax.random.fold_in(jax.random.fold_in(stream_key, 6), position), (blocks,), jnp.float32, least / len(cuts), high / len(cuts))
        level = level * jnp.repeat(jnp.exp(draws), dims[position] // blocks).reshape((-1,) + (1,) * (len(dims) - 1 - position))
    return level


def noise(own_key, shape, width, most, cuts=(), held_as=jnp.bfloat16):
    values = jax.random.normal(own_key, shape, jnp.float32) * width
    if len(cuts) > 0:
        values = block_levels(own_key, shape, cuts, -0.22, 0.18) * values
    return jnp.clip(values, min=-most, max=most).astype(held_as)


def setup_inputs(seed: int = 0) -> dict:
    seeds = jax.random.split(jax.random.key(seed), 16)
    return {
        "patches": noise(seeds[0], (IMAGES, GRID, GRID, D), 1.0, 6.0, ((0, 8), (1, 2), (2, 2))),
        "patch_mask": draw_patch_mask(jax.random.fold_in(seeds[15], 71), 0),
        "norm1_gain": jnp.clip(1.0 + 0.18 * jax.random.normal(seeds[2], (D,), jnp.float32), 0.1, 1.9),
        "norm1_shift": noise(seeds[3], (D,), 0.5, 3.0, (), jnp.float32),
        "qkv_weight": noise(seeds[4], (D, 3 * D), D ** -0.5, 0.21875),
        "qv_bias": noise(seeds[5], (D, 2), 0.5, 3.0, (), jnp.float32),
        "out_weight": noise(seeds[6], (D, D), (D // 32) ** -0.5, 1.25),
        "out_bias": noise(seeds[7], (D,), 0.5, 3.0, (), jnp.float32),
        "norm2_gain": jnp.clip(1.0 + 0.18 * jax.random.normal(seeds[8], (D,), jnp.float32), 0.1, 1.9),
        "norm2_shift": noise(seeds[9], (D,), 0.5, 3.0, (), jnp.float32),
        "fc1_weight": noise(seeds[10], (D, FF), D ** -0.5, 0.21875),
        "fc1_bias": noise(seeds[11], (FF,), 0.5, 3.0, (), jnp.float32),
        "fc2_weight": noise(seeds[12], (FF, D), FF ** -0.5, 0.109375),
        "fc2_bias": noise(seeds[13], (D,), 0.5, 3.0, (), jnp.float32),
        "cotangent": noise(seeds[14], (IMAGES, GRID, GRID, D), 1.0, 6.0, ((0, 8), (1, 2), (2, 2))),
    }


@jax.custom_vjp
def low(v):
    return lax.optimization_barrier(v.astype(jnp.bfloat16)).astype(jnp.float32)

@jax.custom_vjp
def low_back(v):
    return v

def low_keep(v):
    return (low(v), None)

def low_pass(kept, grad):
    return (grad,)

def back_keep(v):
    return (v, None)

def back_low(kept, grad):
    return (low(grad),)
low.defvjp(low_keep, low_pass)
low_back.defvjp(back_keep, back_low)
NORM_EPS = 1e-06
MASKED_SCORE = -1e+30

def normalize(values, gain_vec, shift_vec):
    mean_val = lax.optimization_barrier(jnp.mean(values, axis=-1, keepdims=True))
    centred = values - mean_val
    var_val = lax.optimization_barrier(jnp.mean(centred * centred, axis=-1, keepdims=True))
    return centred * lax.rsqrt(var_val + NORM_EPS) * gain_vec + shift_vec

def matmul(left, right):
    return jnp.dot(left, right, precision=lax.Precision.HIGHEST)

def one_image(params, image_rows, keep_row):
    norm1_gain, norm1_shift, qkv_weight, qv_bias, out_weight, out_bias, norm2_gain, norm2_shift, fc1_weight, fc1_bias, fc2_weight, fc2_bias = params
    model_width = image_rows.shape[-1]
    head_width = model_width // HEADS
    score_scale = head_width ** (-0.5)
    hidden1 = low(normalize(image_rows, norm1_gain, norm1_shift))
    bias_full = jnp.concatenate([qv_bias[:, 0], jnp.zeros_like(qv_bias[:, 0]), qv_bias[:, 1]])
    mixed_all = low_back(matmul(hidden1, qkv_weight) + bias_full)
    query_heads = low(mixed_all[:, :model_width]).reshape(-1, HEADS, head_width)
    key_heads = low(mixed_all[:, model_width:2 * model_width]).reshape(-1, HEADS, head_width)
    value_heads = low(mixed_all[:, 2 * model_width:]).reshape(-1, HEADS, head_width)
    raw_scores = jnp.einsum('qhd,khd->hqk', query_heads, key_heads, precision=lax.Precision.HIGHEST)
    scores = low_back(raw_scores * score_scale)
    scores = jnp.where(keep_row[None, None, :] > 0, scores, MASKED_SCORE)
    probs_low = low(jax.nn.softmax(scores, axis=-1))
    context = jnp.einsum('hqk,khd->qhd', probs_low, value_heads, precision=lax.Precision.HIGHEST)
    context = low(low_back(context.reshape(-1, model_width)))
    branch = low_back(matmul(context, out_weight) + out_bias)
    residual = image_rows + branch
    hidden2 = low(normalize(residual, norm2_gain, norm2_shift))
    inner_pre = low_back(matmul(hidden2, fc1_weight) + fc1_bias)
    active = low(jax.nn.gelu(inner_pre, approximate=False))
    mlp_out = low_back(matmul(active, fc2_weight) + fc2_bias)
    return (residual + mlp_out) * keep_row[:, None]

def reference(patches, patch_mask, norm1_gain, norm1_shift, qkv_weight, qv_bias, out_weight, out_bias, norm2_gain, norm2_shift, fc1_weight, fc1_bias, fc2_weight, fc2_bias, cotangent):
    flat_rows = patches.astype(jnp.float32).reshape(IMAGES, GRID * GRID, D)
    keep_all = patch_mask.reshape(IMAGES, GRID * GRID).astype(jnp.float32)
    params = tuple((p.astype(jnp.float32) for p in (norm1_gain, norm1_shift, qkv_weight, qv_bias, out_weight, out_bias, norm2_gain, norm2_shift, fc1_weight, fc1_bias, fc2_weight, fc2_bias)))

    def forward(rows_in, weights):
        image_fn = jax.checkpoint(one_image)
        return lax.map(lambda pair: image_fn(weights, pair[0], pair[1]), (rows_in, keep_all))
    layer_rows, backward = jax.vjp(forward, flat_rows, params)
    upstream = cotangent.astype(jnp.float32).reshape(IMAGES, GRID * GRID, D)
    rows_grad, param_grads = backward(upstream)
    layer_out = layer_rows.reshape(IMAGES, GRID, GRID, D).astype(jnp.bfloat16)
    patches_grad = rows_grad.reshape(IMAGES, GRID, GRID, D).astype(jnp.bfloat16)
    return (layer_out, patches_grad, param_grads[0], param_grads[1], param_grads[2], param_grads[3], param_grads[4], param_grads[5], param_grads[6], param_grads[7], param_grads[8], param_grads[9], param_grads[10], param_grads[11])
```

```python
import jax
import jax.numpy as jnp
from jax import lax
from jax.sharding import PartitionSpec as P

HEADS = 12
NORM_EPS = 1e-06
MASKED_SCORE = -1e30
GROUP = ("rows", "cols")
BF = jnp.bfloat16
F32 = jnp.float32


def dot(left, right, dims):
    return lax.dot_general(left, right, (dims, ((), ())), preferred_element_type=F32)


def mm(left, right):
    return dot(left, right, ((1,), (0,)))


def mm_nt(left, right):
    return dot(left, right, ((1,), (1,)))


def mm_tn(left, right):
    return dot(left, right, ((0,), (0,)))


def to_peer(value, rel):
    if rel == 1:
        return lax.ppermute(value, "cols", [(0, 1), (1, 0)])
    if rel == 2:
        return lax.ppermute(value, "rows", [(0, 1), (1, 0)])
    return lax.ppermute(value, GROUP, [(i, i ^ 3) for i in range(4)])


def gather_tiles(value):
    across = to_peer(value, 2)
    beside = to_peer(value, 1)
    return [value, beside, across, to_peer(across, 1)]


def scatter_tiles(blocks):
    return [blocks[0], to_peer(blocks[1], 1), to_peer(blocks[2], 2), to_peer(blocks[3], 3)]


def norm_stats(values):
    mean_val = jnp.mean(values, axis=-1, keepdims=True)
    centred = values - mean_val
    var_val = jnp.mean(centred * centred, axis=-1, keepdims=True)
    inv = lax.rsqrt(var_val + NORM_EPS)
    return centred * inv, inv


def norm_back(grads, normed, inv, gain):
    g = grads * gain
    return (
        g
        - jnp.mean(g, axis=-1, keepdims=True)
        - normed * jnp.mean(g * normed, axis=-1, keepdims=True)
    ) * inv


def gelu_parts(x):
    cdf = 0.5 * (1.0 + lax.erf(x * 0.7071067811865476))
    pdf = jnp.exp(-0.5 * x * x) * 0.3989422804014327
    return x * cdf, cdf + x * pdf


def reduce_imgs(parts, imgs):
    if imgs % 2 or imgs > 8:
        return lax.psum_scatter(parts, "imgs", scatter_dimension=0, tiled=False).astype(F32)
    me = lax.axis_index("imgs")
    side = me % 2
    place = me // 2
    line = imgs // 2
    split = parts.reshape((line, 2) + parts.shape[1:])
    send = lax.dynamic_index_in_dim(split, 1 - side, 1, keepdims=False)
    keep = lax.dynamic_index_in_dim(split, side, 1, keepdims=False)
    got = lax.ppermute(send, "imgs", [(i, i ^ 1) for i in range(imgs)])
    own = keep.astype(F32) + got.astype(F32)

    def pick(index):
        return lax.dynamic_index_in_dim(own, jnp.clip(index, 0, line - 1), 0, keepdims=False)

    def hop(value, step, up):
        pairs = []
        for z in range(line):
            for y in range(2):
                if up and z <= step - 1 and z + 1 < line:
                    pairs.append((2 * z + y, 2 * (z + 1) + y))
                if not up and z >= line - step and z - 1 >= 0:
                    pairs.append((2 * z + y, 2 * (z - 1) + y))
        return lax.ppermute(value.astype(parts.dtype), "imgs", pairs).astype(F32)

    up_val = pick(place + line - 1)
    down_val = pick(place - (line - 1))
    for step in range(1, line):
        got_up = hop(up_val, step, True)
        got_down = hop(down_val, step, False)
        if step < line - 1:
            up_val = pick(place + line - 1 - step) + got_up
            down_val = pick(place - (line - 1) + step) + got_down
    return pick(place) + got_up + got_down


def own_order(blocks, tile):
    stacked = jnp.stack(blocks)
    return [lax.dynamic_index_in_dim(stacked, tile ^ k, 0, keepdims=False) for k in range(4)]


def body(
    patches,
    patch_mask,
    norm1_gain,
    norm1_shift,
    qkv_weight,
    qv_bias,
    out_weight,
    out_bias,
    norm2_gain,
    norm2_shift,
    fc1_weight,
    fc1_bias,
    fc2_weight,
    fc2_bias,
    cotangent,
):
    _, tile_rows, tile_cols, width = patches.shape
    ff = fc1_weight.shape[1]
    imgs = lax.axis_size("imgs")
    heads = HEADS // 4
    dim = width // HEADS
    part = heads * dim
    scale = dim ** (-0.5)
    row = lax.axis_index("rows")
    col = lax.axis_index("cols")
    tile = row * 2 + col
    pad_cols = 16
    toks = tile_rows * pad_cols

    def flat(block):
        return jnp.pad(block[0], ((0, 0), (0, pad_cols - tile_cols), (0, 0))).reshape(toks, -1)

    high = jnp.sum(patch_mask[0, :, 0])
    wide = jnp.sum(patch_mask[0, 0, :])

    def keep_of(rel):
        tok = jnp.arange(toks)
        place = tile ^ rel
        r = (place // 2) * tile_rows + tok // pad_cols
        c = (place % 2) * tile_cols + tok % pad_cols
        return ((tok % pad_cols < tile_cols) & (r < high) & (c < wide)).astype(F32)

    keep_blocks = [keep_of(r) for r in range(4)]
    keep_own = keep_blocks[0]
    keep_all = jnp.concatenate(keep_blocks)

    x_blocks = [flat(b) for b in gather_tiles(patches)]
    ct_blocks = [flat(b) for b in gather_tiles(cotangent)]
    x_all = jnp.concatenate(x_blocks).astype(F32)
    x_own = x_blocks[0].astype(F32)

    def own_cols(m, at):
        return lax.dynamic_slice_in_dim(m, at + tile * part, part, 1)

    w_own = jnp.concatenate([own_cols(qkv_weight, i * width) for i in range(3)], axis=1)
    q_bias = lax.dynamic_slice_in_dim(qv_bias[:, 0], tile * part, part)
    v_bias = lax.dynamic_slice_in_dim(qv_bias[:, 1], tile * part, part)
    bias_own = jnp.concatenate([q_bias, jnp.zeros_like(q_bias), v_bias])

    normed, _ = norm_stats(x_all)
    hidden1 = (normed * norm1_gain + norm1_shift).astype(BF)
    qkv = (mm(hidden1, w_own) + bias_own).astype(BF)
    ctx = []
    probs = []
    for h in range(heads):
        q = qkv[:, h * dim : (h + 1) * dim]
        k = qkv[:, part + h * dim : part + (h + 1) * dim]
        v = qkv[:, 2 * part + h * dim : 2 * part + (h + 1) * dim]
        s = jnp.where(keep_all[None, :] > 0, mm_nt(q, k) * scale, MASKED_SCORE)
        e = jnp.exp(s - jnp.max(s, axis=-1, keepdims=True))
        p = e / jnp.sum(e, axis=-1, keepdims=True)
        probs.append(p)
        ctx.append(mm(p.astype(BF), v).astype(BF))
    ctx_own = jnp.concatenate(ctx, axis=1)

    ctx_in = scatter_tiles([ctx_own[r * toks : (r + 1) * toks] for r in range(4)])

    def wo_rows(rel):
        return lax.dynamic_slice_in_dim(out_weight, (tile ^ rel) * part, part, 0)

    branch = sum(mm(ctx_in[r], wo_rows(r)) for r in range(4)) + out_bias
    residual = x_own + branch
    normed2, inv2 = norm_stats(residual)
    hidden2 = (normed2 * norm2_gain + norm2_shift).astype(BF)
    hidden2_all = jnp.concatenate(gather_tiles(hidden2))
    act, dgelu = gelu_parts(mm(hidden2, fc1_weight) + fc1_bias)
    mlp_out = mm(act.astype(BF), fc2_weight) + fc2_bias
    layer_out = (keep_own[:, None] * (residual + mlp_out)).astype(BF)
    upstream = keep_own[:, None] * ct_blocks[0].astype(F32)
    inner_low = (mm_nt(upstream.astype(BF), fc2_weight) * dgelu).astype(BF)
    n2 = mm_nt(inner_low, fc1_weight)
    norm2_gain_part = jnp.sum(n2 * normed2, axis=0)
    norm2_shift_part = jnp.sum(n2, axis=0)
    residual_grad = upstream + norm_back(n2, normed2, inv2, norm2_gain)
    branch_own = residual_grad.astype(BF)
    branch_all = jnp.concatenate(gather_tiles(branch_own))

    quarter = ff // (imgs * 4)

    def own_units(m, axis):
        shape = m.shape[:axis] + (imgs, 4, quarter) + m.shape[axis + 1 :]
        got = lax.dynamic_index_in_dim(m.reshape(shape), tile, axis + 1, keepdims=False)
        return got.reshape(m.shape[:axis] + (imgs * quarter,) + m.shape[axis + 1 :])

    fc1_own = own_units(fc1_weight, 1)
    fc1_bias_own = own_units(fc1_bias, 0)
    fc2_own = own_units(fc2_weight, 0)
    up_all = (keep_all[:, None] * jnp.concatenate(ct_blocks).astype(F32)).astype(BF)
    act_q, dgelu_q = gelu_parts(mm(hidden2_all, fc1_own) + fc1_bias_own)
    inner_q = (mm_nt(up_all, fc2_own) * dgelu_q).astype(BF)
    fc1_part = mm_tn(hidden2_all, inner_q)
    fc2_part = mm_tn(act_q.astype(BF), up_all)
    fc1_bias_part = jnp.sum(inner_q.astype(F32), axis=0)
    fc2_bias_part = jnp.sum(up_all.astype(F32), axis=0)

    wo_own = wo_rows(0)
    dctx = mm_nt(branch_all, wo_own).astype(BF)
    out_part = mm_tn(ctx_own, branch_all)
    out_bias_part = jnp.sum(branch_all.astype(F32), axis=0)
    dq, dk, dv = [], [], []
    for h in range(heads):
        q = qkv[:, h * dim : (h + 1) * dim]
        k = qkv[:, part + h * dim : part + (h + 1) * dim]
        v = qkv[:, 2 * part + h * dim : 2 * part + (h + 1) * dim]
        p = probs[h]
        do = dctx[:, h * dim : (h + 1) * dim]
        dp = mm_nt(do, v)
        ds = (p * (dp - jnp.sum(dp * p, axis=-1, keepdims=True))).astype(BF)
        dv.append(mm_tn(p.astype(BF), do))
        dq.append(mm(ds, k) * scale)
        dk.append(mm_tn(ds, q) * scale)
    mixed = jnp.concatenate(dq + dk + dv, axis=1).astype(BF)
    qkv_part = mm_tn(hidden1, mixed)
    mixed_sum = jnp.sum(mixed.astype(F32), axis=0)
    mixed_in = scatter_tiles([mixed[r * toks : (r + 1) * toks] for r in range(4)])

    qkv_cols = qkv_weight.reshape(width, 3, 4, part)

    def wq_cols(rel):
        got = lax.dynamic_index_in_dim(qkv_cols, tile ^ rel, 2, keepdims=False)
        return got.reshape(width, 3 * part)

    n1 = sum(mm_nt(mixed_in[r], wq_cols(r)) for r in range(4))
    normed1, inv1 = norm_stats(x_own)
    norm1_gain_part = jnp.sum(n1 * normed1, axis=0)
    norm1_shift_part = jnp.sum(n1, axis=0)
    patches_grad = (residual_grad + norm_back(n1, normed1, inv1, norm1_gain)).astype(BF)

    fc1_sum = reduce_imgs(fc1_part.astype(BF).reshape(imgs, width // imgs, -1), imgs)
    fc2_sum = reduce_imgs(fc2_part.astype(BF).reshape(imgs, imgs * quarter // imgs, -1), imgs)
    out_low = out_part.astype(BF)
    out_cols = [lax.dynamic_slice_in_dim(out_low, (tile ^ r) * part, part, 1) for r in range(4)]
    out_quarter = jnp.concatenate(own_order(scatter_tiles(out_cols), tile), axis=0)
    attn_part = jnp.concatenate([qkv_part.astype(BF), out_quarter], axis=1)
    attn_sum = reduce_imgs(attn_part.reshape(imgs, width // imgs, -1), imgs)

    fc1_pieces = own_order(gather_tiles(fc1_sum.astype(BF)), tile)
    fc2_pieces = own_order(gather_tiles(fc2_sum.astype(BF)), tile)
    attn_pieces = own_order(gather_tiles(attn_sum.astype(BF)), tile)
    fc1_grad = jnp.stack([p.reshape(-1, imgs, quarter) for p in fc1_pieces], axis=2)
    fc1_grad = fc1_grad.reshape(-1, ff).astype(F32)
    fc2_grad = jnp.concatenate(fc2_pieces, axis=0).astype(F32)
    qkv_grad = jnp.concatenate(
        [p[:, i * part : (i + 1) * part] for i in range(3) for p in attn_pieces], axis=1
    ).astype(F32)
    out_grad = jnp.concatenate([p[:, 3 * part :] for p in attn_pieces], axis=1).astype(F32)

    zeros_ff = jnp.zeros((imgs, 4, quarter), F32)
    fc1_bias_row = lax.dynamic_update_index_in_dim(
        zeros_ff, fc1_bias_part.reshape(imgs, quarter), tile, 1
    ).reshape(ff)
    q_row = lax.dynamic_update_slice_in_dim(
        jnp.zeros((width,), F32), mixed_sum[:part], tile * part, 0
    )
    v_row = lax.dynamic_update_slice_in_dim(
        jnp.zeros((width,), F32), mixed_sum[2 * part :], tile * part, 0
    )
    lone = (tile == 0).astype(F32)
    rows = [
        norm1_gain_part,
        norm1_shift_part,
        q_row,
        v_row,
        out_bias_part * lone,
        norm2_gain_part,
        norm2_shift_part,
        fc2_bias_part * lone,
        fc1_bias_row,
    ]
    vecs = jnp.concatenate([r.reshape(imgs, -1) for r in rows], axis=1)
    vec_own = reduce_imgs(vecs, imgs)
    vec_own = vec_own + to_peer(vec_own, 1)
    vec_own = vec_own + to_peer(vec_own, 2)
    w = width // imgs
    v = [vec_own[i * w : (i + 1) * w] for i in range(8)]

    def unflat(value):
        return value.reshape(tile_rows, pad_cols, width)[None, :, :tile_cols]

    return (
        unflat(layer_out),
        unflat(patches_grad),
        v[0],
        v[1],
        qkv_grad,
        jnp.stack([v[2], v[3]], axis=1),
        out_grad,
        v[4],
        v[5],
        v[6],
        fc1_grad,
        vec_own[8 * w :],
        fc2_grad,
        v[7],
    )


def solution(mesh):
    tiled = P("imgs", "rows", "cols", None)
    in_specs = (tiled, P("imgs", None, None)) + (P(),) * 12 + (tiled,)
    mat = P("imgs", None)
    vec = P("imgs")
    out_specs = (tiled, tiled, vec, vec, mat, mat, mat, vec, vec, vec, mat, vec, mat, vec)
    return jax.shard_map(body, mesh=mesh, in_specs=in_specs, out_specs=out_specs, check_vma=False)
```

```python
import jax
import jax.numpy as jnp
from jax import lax
from jax.experimental import pallas as pl
from jax.experimental.pallas import tpu as pltpu
from jax.sharding import PartitionSpec as P

HEADS = 12
NORM_EPS = 1e-06
MASKED_SCORE = -1e30
GROUP = ("rows", "cols")
BF = jnp.bfloat16
F32 = jnp.float32


def dot(left, right, dims):
    return lax.dot_general(left, right, (dims, ((), ())), preferred_element_type=F32)


def mm(left, right):
    return dot(left, right, ((1,), (0,)))


def mm_nt(left, right):
    return dot(left, right, ((1,), (1,)))


def mm_tn(left, right):
    return dot(left, right, ((0,), (0,)))


def to_peer(value, rel):
    if rel == 1:
        return lax.ppermute(value, "cols", [(0, 1), (1, 0)])
    if rel == 2:
        return lax.ppermute(value, "rows", [(0, 1), (1, 0)])
    return lax.ppermute(value, GROUP, [(i, i ^ 3) for i in range(4)])


def gather_tiles(value):
    across = to_peer(value, 2)
    beside = to_peer(value, 1)
    return [value, beside, across, to_peer(across, 1)]


def scatter_tiles(blocks):
    return [blocks[0], to_peer(blocks[1], 1), to_peer(blocks[2], 2), to_peer(blocks[3], 3)]


def norm_stats(values):
    mean_val = jnp.mean(values, axis=-1, keepdims=True)
    centred = values - mean_val
    var_val = jnp.mean(centred * centred, axis=-1, keepdims=True)
    inv = lax.rsqrt(var_val + NORM_EPS)
    return centred * inv, inv


def norm_back(grads, normed, inv, gain):
    g = grads * gain
    return (
        g
        - jnp.mean(g, axis=-1, keepdims=True)
        - normed * jnp.mean(g * normed, axis=-1, keepdims=True)
    ) * inv


def gelu_parts(x):
    cdf = 0.5 * (1.0 + lax.erf(x * 0.7071067811865476))
    pdf = jnp.exp(-0.5 * x * x) * 0.3989422804014327
    return x * cdf, cdf + x * pdf


def start_imgs(parts, imgs):
    if imgs % 2 or imgs > 8:
        return parts, None
    side = lax.axis_index("imgs") % 2
    split = parts.reshape((imgs // 2, 2) + parts.shape[1:])
    send = lax.dynamic_index_in_dim(split, 1 - side, 1, keepdims=False)
    keep = lax.dynamic_index_in_dim(split, side, 1, keepdims=False)
    return keep, lax.ppermute(send, "imgs", [(i, i ^ 1) for i in range(imgs)])


def finish_imgs(state, imgs, low):
    keep, got = state
    if got is None:
        return lax.psum_scatter(keep, "imgs", scatter_dimension=0, tiled=False).astype(F32)
    place = lax.axis_index("imgs") // 2
    line = imgs // 2

    def pick(index):
        at = jnp.clip(index, 0, line - 1)
        a = lax.dynamic_index_in_dim(keep, at, 0, keepdims=False)
        b = lax.dynamic_index_in_dim(got, at, 0, keepdims=False)
        return a.astype(F32) + b.astype(F32)

    def hop(value, step, up):
        pairs = []
        for z in range(line):
            for y in range(2):
                if up and z <= step - 1 and z + 1 < line:
                    pairs.append((2 * z + y, 2 * (z + 1) + y))
                if not up and z >= line - step and z - 1 >= 0:
                    pairs.append((2 * z + y, 2 * (z - 1) + y))
        return lax.ppermute(value.astype(low), "imgs", pairs).astype(F32)

    up_val = pick(place + line - 1)
    down_val = pick(place - (line - 1))
    for step in range(1, line):
        got_up = hop(up_val, step, True)
        got_down = hop(down_val, step, False)
        if step < line - 1:
            up_val = pick(place + line - 1 - step) + got_up
            down_val = pick(place - (line - 1) + step) + got_down
    return pick(place) + got_up + got_down


def own_order(blocks, tile):
    stacked = jnp.stack(blocks)
    return [lax.dynamic_index_in_dim(stacked, tile ^ k, 0, keepdims=False) for k in range(4)]


SMEM = pl.BlockSpec(memory_space=pltpu.SMEM)
VMEM = pl.BlockSpec(memory_space=pltpu.VMEM)
PAD = 16


def vec_call(kernel, outs, n_in, scratch=(), flops=0, moved=0):
    return pl.pallas_call(
        kernel,
        out_shape=outs,
        in_specs=[SMEM] + [VMEM] * n_in,
        out_specs=jax.tree.map(lambda _: VMEM, outs),
        scratch_shapes=list(scratch),
        cost_estimate=pl.CostEstimate(flops=flops, transcendentals=0, bytes_accessed=moved),
    )


def sds(shape, dtype=BF):
    return jax.ShapeDtypeStruct(shape, dtype)


def load_tile(ref, scratch, at):
    rows, cols, width = ref.shape[1:]
    scratch[at : at + rows * PAD, :] = jnp.zeros((rows * PAD, width), scratch.dtype)
    for i in range(rows):
        scratch[at + i * PAD : at + i * PAD + cols, :] = ref[0, i]


def store_tile(ref, value):
    rows, cols, _ = ref.shape[1:]
    for i in range(rows):
        ref[0, i] = value[i * PAD : i * PAD + cols, :]


def keep_tokens(scal, rel, rows, cols, axis):
    toks = rows * PAD
    shape = (toks, 1) if axis == 0 else (1, toks)
    tok = lax.broadcasted_iota(jnp.int32, shape, axis)
    place = scal[0] ^ rel
    c = tok & (PAD - 1)
    r = (tok >> 4) + (place >> 1) * rows
    ok = (c < cols) & (r < scal[1]) & (c + (place & 1) * cols < scal[2])
    return jnp.where(ok, 1.0, 0.0).astype(F32)


def prep_kernel(scal, fc1, fc1_b, qkv_w, qv_b, fc1_own, fc1_b_own, w_own, b_own):
    width = qv_b.shape[1]
    part = width // 4
    ff = fc1.shape[1]
    units = ff // 4
    quarter = prep_kernel.quarter
    for g in range(4):

        @pl.when(scal[0] == g)
        def _():
            for i in range(units // quarter):
                src = (4 * i + g) * quarter
                dst = i * quarter
                fc1_own[:, dst : dst + quarter] = fc1[:, src : src + quarter]
                fc1_b_own[:, dst : dst + quarter] = fc1_b[:, src : src + quarter]
            for i in range(3):
                src = i * width + g * part
                w_own[:, i * part : (i + 1) * part] = qkv_w[:, src : src + part]
            b_own[:, :part] = qv_b[0:1, g * part : (g + 1) * part]
            b_own[:, part : 2 * part] = jnp.zeros((1, part), F32)
            b_own[:, 2 * part :] = qv_b[1:2, g * part : (g + 1) * part]


def attn_kernel(scal, x0, x1, x2, x3, gain, shift, w, bias, hid, nrm, qkv, ctx, lse, xs):
    rows, cols, width = x0.shape[1:]
    toks = rows * PAD
    part = w.shape[1] // 3
    dim = width // HEADS
    scale = dim ** (-0.5)
    for r, ref in enumerate((x0, x1, x2, x3)):
        load_tile(ref, xs, 0)
        at = slice(r * toks, (r + 1) * toks)
        normed, _ = norm_stats(xs[...].astype(F32))
        h = (normed * gain[...] + shift[...]).astype(BF)
        hid[at, :] = h
        nrm[at, :] = normed.astype(BF)
        qkv[at, :] = (mm(h, w[...]) + bias[...]).astype(BF)
    keep = jnp.concatenate([keep_tokens(scal, r, rows, cols, 1) for r in range(4)], axis=1)
    for r in range(4):
        at = slice(r * toks, (r + 1) * toks)
        outs = []
        for h in range(part // dim):
            q = qkv[at, h * dim : (h + 1) * dim]
            k = qkv[:, part + h * dim : part + (h + 1) * dim]
            v = qkv[:, 2 * part + h * dim : 2 * part + (h + 1) * dim]
            s = jnp.where(keep > 0, mm_nt(q, k) * scale, MASKED_SCORE)
            top = jnp.max(s, axis=-1, keepdims=True)
            e = jnp.exp(s - top)
            total = jnp.sum(e, axis=-1, keepdims=True)
            outs.append(mm((e * (1.0 / total)).astype(BF), v).astype(BF))
            lse[at, h : h + 1] = top + jnp.log(total)
        ctx[r] = jnp.concatenate(outs, axis=1)


def branch_kernel(scal, c0, c1, c2, c3, wo, bo, x, gain, shift, resid, hid, xs):
    part = c0.shape[1]
    load_tile(x, xs, 0)
    acc = xs[...].astype(F32) + bo[...]
    for r, ref in enumerate((c0, c1, c2, c3)):
        at = pl.multiple_of((scal[0] ^ r) * part, part)
        acc = acc + mm(ref[...], wo[pl.ds(at, part), :])
    resid[...] = acc
    normed, _ = norm_stats(acc)
    hid[...] = (normed * gain[...] + shift[...]).astype(BF)


def mlp_kernel(
    scal, resid, hid, ct, gain, fc1, fc1_b, fc2, fc2_b, out, branch, rgrad, vecs, up, acc, nacc
):
    step = pl.program_id(0)
    rows, cols, _ = ct.shape[1:]

    @pl.when(step == 0)
    def _():
        load_tile(ct, up, 0)
        up[...] = (up[...].astype(F32) * keep_tokens(scal, 0, rows, cols, 0)).astype(BF)
        acc[...] = jnp.zeros_like(acc)
        nacc[...] = jnp.zeros_like(nacc)

    act, dgelu = gelu_parts(mm(hid[...], fc1[...]) + fc1_b[...])
    acc[...] += mm(act.astype(BF), fc2[...])
    inner = (mm_nt(up[...], fc2[...]) * dgelu).astype(BF)
    nacc[...] += mm_nt(inner, fc1[...])

    @pl.when(step == pl.num_programs(0) - 1)
    def _():
        res = resid[...]
        keep = keep_tokens(scal, 0, rows, cols, 0)
        store_tile(out, (keep * (res + acc[...] + fc2_b[...])).astype(BF))
        normed, inv = norm_stats(res)
        n = nacc[...]
        vecs[0:1, :] = jnp.sum(n * normed, axis=0, keepdims=True)
        vecs[1:2, :] = jnp.sum(n, axis=0, keepdims=True)
        grad = up[...].astype(F32) + norm_back(n, normed, inv, gain[...])
        rgrad[...] = grad
        branch[...] = grad.astype(BF)


def ffgrad_kernel(scal, h0, h1, h2, h3, t0, t1, t2, t3, fc1, fc1_b, fc2, g1, g2, b1, b2, up, a1, a2):
    rows, cols, _ = t0.shape[1:]
    hids = (h0, h1, h2, h3)
    for r, ref in enumerate((t0, t1, t2, t3)):
        load_tile(ref, up, 0)
        wide = up[...].astype(F32) * keep_tokens(scal, r, rows, cols, 0)
        low = wide.astype(BF)
        h = hids[r][...]
        act, dgelu = gelu_parts(mm(h, fc1[...]) + fc1_b[...])
        inner = (mm_nt(low, fc2[...]) * dgelu).astype(BF)
        d1 = mm_tn(h, inner)
        d2 = mm_tn(act.astype(BF), low)
        s1 = jnp.sum(inner.astype(F32), axis=0, keepdims=True)
        s2 = jnp.sum(wide, axis=0, keepdims=True)
        if r == 0:
            a1[...], a2[...], b1[...], b2[...] = d1, d2, s1, s2
        elif r < 3:
            a1[...] += d1
            a2[...] += d2
            b1[...] += s1
            b2[...] += s2
        else:
            g1[...] = (a1[...] + d1).astype(BF)
            g2[...] = (a2[...] + d2).astype(BF)
            b1[...] += s1
            b2[...] += s2


def outgrad_kernel(scal, b0, b1, b2, b3, wo, ctx, dctx, gout, bsum):
    toks, part = ctx.shape[1:]
    at = pl.multiple_of(scal[0] * part, part)
    w = wo[pl.ds(at, part), :]
    acc = None
    total = None
    for r, ref in enumerate((b0, b1, b2, b3)):
        low = ref[...]
        dctx[r * toks : (r + 1) * toks, :] = mm_nt(low, w).astype(BF)
        d = mm_tn(ctx[r], low)
        s = jnp.sum(low.astype(F32), axis=0, keepdims=True)
        acc = d if r == 0 else acc + d
        total = s if r == 0 else total + s
    gout[...] = acc.astype(BF)
    bsum[...] = total


def attnback_kernel(scal, dctx, qkv, lse, hid, nrm, w, mixed, gqkv, msum, nsum, dk, dv, mix):
    total, three = qkv.shape
    part = three // 3
    toks = total // 4
    dim = hid.shape[1] // HEADS
    rows = toks // PAD
    cols = attnback_kernel.cols
    scale = dim ** (-0.5)
    keep = jnp.concatenate([keep_tokens(scal, r, rows, cols, 1) for r in range(4)], axis=1)
    for h in range(part // dim):
        at_h = slice(h * dim, (h + 1) * dim)
        k = qkv[:, part + h * dim : part + (h + 1) * dim]
        v = qkv[:, 2 * part + h * dim : 2 * part + (h + 1) * dim]
        for r in range(4):
            at = slice(r * toks, (r + 1) * toks)
            q = qkv[at, at_h]
            do = dctx[at, at_h]
            s = jnp.where(keep > 0, mm_nt(q, k) * scale, MASKED_SCORE)
            p = jnp.exp(s - lse[at, h : h + 1])
            dp = mm_nt(do, v)
            ds = (p * (dp - jnp.sum(dp * p, axis=-1, keepdims=True))).astype(BF)
            mix[at, at_h] = (mm(ds, k) * scale).astype(BF)
            dv_r = mm_tn(p.astype(BF), do)
            dk_r = mm_tn(ds, q)
            if r == 0:
                dv[...] = dv_r
                dk[...] = dk_r
            else:
                dv[...] += dv_r
                dk[...] += dk_r
        mix[:, part + h * dim : part + (h + 1) * dim] = (dk[...] * scale).astype(BF)
        mix[:, 2 * part + h * dim : 2 * part + (h + 1) * dim] = dv[...].astype(BF)
    gqkv[...] = mm_tn(hid[...], mix[...]).astype(BF)
    for r in range(4):
        at = slice(r * toks, (r + 1) * toks)
        m = mix[at, :]
        mixed[r] = m
        n = mm_nt(m, w[...])
        a = jnp.sum(n * nrm[at, :].astype(F32), axis=0, keepdims=True)
        b = jnp.sum(n, axis=0, keepdims=True)
        c = jnp.sum(m.astype(F32), axis=0, keepdims=True)
        if r == 0:
            nsum[0:1, :] = a
            nsum[1:2, :] = b
            msum[...] = c
        else:
            nsum[0:1, :] += a
            nsum[1:2, :] += b
            msum[...] += c


def input_kernel(scal, m0, m1, m2, m3, w, x, rgrad, gain, out, ms, xs):
    part = m0.shape[1] // 3
    for r, ref in enumerate((m0, m1, m2, m3)):
        ms[r] = ref[...]
    tiles = [ms[scal[0] ^ g] for g in range(4)]
    full = jnp.concatenate(
        [m[:, i * part : (i + 1) * part] for i in range(3) for m in tiles], axis=1
    )
    n = mm_nt(full, w[...])
    load_tile(x, xs, 0)
    normed, inv = norm_stats(xs[...].astype(F32))
    store_tile(out, (rgrad[...] + norm_back(n, normed, inv, gain[...])).astype(BF))


def ffout_kernel(scal, p0, p1, p2, p3, fc1, fc2, ps):
    rows = fc1.shape[0]
    quarter = fc2.shape[0] // 4
    for r, ref in enumerate((p0, p1, p2, p3)):
        ps[r] = ref[...].astype(F32)
    for g in range(4):
        piece = ps[scal[0] ^ g]
        for i in range(fc1.shape[1] // (4 * quarter)):
            dst = (4 * i + g) * quarter
            fc1[:, dst : dst + quarter] = piece[:rows, i * quarter : (i + 1) * quarter]
        fc2[g * quarter : (g + 1) * quarter, :] = piece[rows:, :]


def attnout_kernel(scal, p0, p1, p2, p3, gqkv, gout, vecs, ps):
    rows = gqkv.shape[0]
    width = gout.shape[1]
    part = width // 4
    for r, ref in enumerate((p0, p1, p2, p3)):
        ps[r] = ref[...].astype(F32)
    total = None
    for g in range(4):
        piece = ps[scal[0] ^ g]
        for i in range(3):
            dst = i * width + g * part
            gqkv[:, dst : dst + part] = piece[:rows, i * part : (i + 1) * part]
        gout[:, g * part : (g + 1) * part] = piece[:rows, 3 * part :]
        tail = piece[rows:, :]
        total = tail if g == 0 else total + tail
    vecs[...] = total


def body(
    patches,
    patch_mask,
    norm1_gain,
    norm1_shift,
    qkv_weight,
    qv_bias,
    out_weight,
    out_bias,
    norm2_gain,
    norm2_shift,
    fc1_weight,
    fc1_bias,
    fc2_weight,
    fc2_bias,
    cotangent,
):
    _, rows, cols, width = patches.shape
    ff = fc1_weight.shape[1]
    imgs = lax.axis_size("imgs")
    part = width // 4
    units = ff // 4
    quarter = units // imgs
    share = width // imgs
    toks = rows * PAD
    total = 4 * toks
    tile = lax.axis_index("rows") * 2 + lax.axis_index("cols")
    high = jnp.sum(patch_mask[0, :, 0])
    wide = jnp.sum(patch_mask[0, 0, :])
    scal = jnp.stack([tile, high, wide]).astype(jnp.int32)

    def row(v):
        return v.reshape(1, -1)

    x_blocks = gather_tiles(patches)
    ct_blocks = gather_tiles(cotangent)

    steps = 4
    prep_kernel.quarter = quarter
    fc1_own, fc1_b_own, w_own, b_own = pl.pallas_call(
        prep_kernel,
        grid=(steps,),
        in_specs=[
            SMEM,
            pl.BlockSpec((width // steps, ff), lambda i: (i, 0)),
            pl.BlockSpec((1, ff), lambda i: (0, 0)),
            pl.BlockSpec((width // steps, 3 * width), lambda i: (i, 0)),
            pl.BlockSpec((2, width), lambda i: (0, 0)),
        ],
        out_specs=[
            pl.BlockSpec((width // steps, units), lambda i: (i, 0)),
            pl.BlockSpec((1, units), lambda i: (0, 0)),
            pl.BlockSpec((width // steps, 3 * part), lambda i: (i, 0)),
            pl.BlockSpec((1, 3 * part), lambda i: (0, 0)),
        ],
        out_shape=[
            sds((width, units)),
            sds((1, units), F32),
            sds((width, 3 * part)),
            sds((1, 3 * part), F32),
        ],
        name="prep",
    )(scal, fc1_weight, row(fc1_bias), qkv_weight, qv_bias.T)
    fc2_own = lax.dynamic_index_in_dim(
        fc2_weight.reshape(imgs, 4, quarter, width), tile, 1, keepdims=False
    ).reshape(units, width)

    hid1, nrm1, qkv, ctx, lse = vec_call(
        attn_kernel,
        [
            sds((total, width)),
            sds((total, width)),
            sds((total, 3 * part)),
            sds((4, toks, part)),
            sds((total, 128), F32),
        ],
        8,
        [pltpu.VMEM((toks, width), BF)],
        flops=3 * 10**9,
        moved=10**7,
    )(scal, *x_blocks, row(norm1_gain), row(norm1_shift), w_own, b_own)

    ctx_in = scatter_tiles([ctx[r] for r in range(4)])
    resid, hid2 = vec_call(
        branch_kernel,
        [sds((toks, width), F32), sds((toks, width))],
        9,
        [pltpu.VMEM((toks, width), BF)],
    )(
        scal,
        *ctx_in,
        out_weight,
        row(out_bias),
        patches,
        row(norm2_gain),
        row(norm2_shift),
    )
    hid2_blocks = gather_tiles(hid2)

    chunks = 4
    step = ff // chunks

    def whole(*shape):
        return pl.BlockSpec(shape, lambda i: (0,) * len(shape))

    layer_out, branch, rgrad, vec2 = pl.pallas_call(
        mlp_kernel,
        grid=(chunks,),
        in_specs=[
            SMEM,
            whole(toks, width),
            whole(toks, width),
            whole(1, rows, cols, width),
            whole(1, width),
            pl.BlockSpec((width, step), lambda i: (0, i)),
            pl.BlockSpec((1, step), lambda i: (0, i)),
            pl.BlockSpec((step, width), lambda i: (i, 0)),
            whole(1, width),
        ],
        out_specs=[
            whole(1, rows, cols, width),
            whole(toks, width),
            whole(toks, width),
            whole(2, width),
        ],
        out_shape=[
            sds((1, rows, cols, width)),
            sds((toks, width)),
            sds((toks, width), F32),
            sds((2, width), F32),
        ],
        scratch_shapes=[
            pltpu.VMEM((toks, width), BF),
            pltpu.VMEM((toks, width), F32),
            pltpu.VMEM((toks, width), F32),
        ],
        name="mlp",
    )(
        scal,
        resid,
        hid2,
        cotangent,
        row(norm2_gain),
        fc1_weight,
        row(fc1_bias),
        fc2_weight,
        row(fc2_bias),
    )
    branch_blocks = gather_tiles(branch)

    g1, g2, fb1, fb2 = vec_call(
        ffgrad_kernel,
        [sds((width, units)), sds((units, width)), sds((1, units), F32), sds((1, width), F32)],
        11,
        [
            pltpu.VMEM((toks, width), BF),
            pltpu.VMEM((width, units), F32),
            pltpu.VMEM((units, width), F32),
        ],
        flops=4 * 10**9,
        moved=10**7,
    )(scal, *hid2_blocks, *ct_blocks, fc1_own, fc1_b_own, fc2_own)

    *branch_blocks, g1, g2 = lax.optimization_barrier((*branch_blocks, g1, g2))
    dctx, gout, bsum = vec_call(
        outgrad_kernel,
        [sds((total, part)), sds((part, width)), sds((1, width), F32)],
        6,
    )(scal, *branch_blocks, out_weight, ctx)
    out_cols = [lax.dynamic_slice_in_dim(gout, (tile ^ r) * part, part, 1) for r in range(4)]
    out_rows = own_order(scatter_tiles(out_cols), tile)

    ff_bucket = jnp.concatenate(
        [g1.reshape(imgs, share, units), g2.reshape(imgs, quarter, width)], axis=1
    )
    ff_start = start_imgs(ff_bucket, imgs)

    attnback_kernel.cols = cols
    mixed, gqkv, msum, nsum = vec_call(
        attnback_kernel,
        [
            sds((4, toks, 3 * part)),
            sds((width, 3 * part)),
            sds((1, 3 * part), F32),
            sds((2, width), F32),
        ],
        6,
        [
            pltpu.VMEM((total, width // HEADS), F32),
            pltpu.VMEM((total, width // HEADS), F32),
            pltpu.VMEM((total, 3 * part), BF),
        ],
        flops=6 * 10**9,
        moved=10**7,
    )(scal, dctx, qkv, lse, hid1, nrm1, w_own)
    mixed_in = scatter_tiles([mixed[r] for r in range(4)])

    lone = (tile == 0).astype(F32)
    fb1_row = lax.dynamic_update_index_in_dim(
        jnp.zeros((imgs, 4, quarter), F32), fb1.reshape(imgs, quarter), tile, 1
    )
    heads_row = lax.dynamic_update_index_in_dim(
        jnp.zeros((3, 4, part), F32), msum.reshape(3, part), tile, 1
    ).reshape(3, width)
    vec_rows = [
        nsum,
        heads_row,
        bsum * lone,
        vec2,
        fb2 * lone,
    ]
    vecs = jnp.concatenate(vec_rows, axis=0).reshape(9, imgs, share).transpose(1, 0, 2)
    vecs = jnp.concatenate(
        [vecs.reshape(imgs, 9 * share), fb1_row.reshape(imgs, 4 * quarter)], axis=1
    ).astype(BF)
    count = vecs.shape[1]
    vec_height = -(-count // width)
    vecs = jnp.pad(vecs, ((0, 0), (0, vec_height * width - count)))
    at_bucket = jnp.concatenate(
        [
            jnp.concatenate([gqkv] + [jnp.concatenate(out_rows, axis=0)], axis=1).reshape(
                imgs, share, width
            ),
            vecs.reshape(imgs, vec_height, width),
        ],
        axis=1,
    )
    at_start = start_imgs(at_bucket, imgs)
    ff_sum = finish_imgs(ff_start, imgs, BF)
    ff_pieces = gather_tiles(ff_sum.astype(BF))

    patches_grad = vec_call(
        input_kernel,
        sds((1, rows, cols, width)),
        8,
        [pltpu.VMEM((4, toks, 3 * part), BF), pltpu.VMEM((toks, width), BF)],
    )(scal, *mixed_in, qkv_weight, patches, rgrad, row(norm1_gain))

    at_sum = finish_imgs(at_start, imgs, BF)
    at_pieces = gather_tiles(at_sum.astype(BF))
    fc1_grad, fc2_grad = vec_call(
        ffout_kernel,
        [sds((share, ff), F32), sds((4 * quarter, width), F32)],
        4,
        [pltpu.VMEM((4, share + quarter, width), F32)],
    )(scal, *ff_pieces)
    qkv_grad, out_grad, vec_sum = vec_call(
        attnout_kernel,
        [sds((share, 3 * width), F32), sds((share, width), F32), sds((vec_height, width), F32)],
        4,
        [pltpu.VMEM((4, share + vec_height, width), F32)],
    )(scal, *at_pieces)
    v = vec_sum.reshape(-1)
    piece = [v[i * share : (i + 1) * share] for i in range(9)]
    return (
        layer_out,
        patches_grad,
        piece[0],
        piece[1],
        qkv_grad,
        jnp.stack([piece[2], piece[4]], axis=1),
        out_grad,
        piece[5],
        piece[6],
        piece[7],
        fc1_grad,
        v[9 * share : count],
        fc2_grad,
        piece[8],
    )


def solution(mesh):
    tiled = P("imgs", "rows", "cols", None)
    in_specs = (tiled, P("imgs", None, None)) + (P(),) * 12 + (tiled,)
    mat = P("imgs", None)
    vec = P("imgs")
    out_specs = (tiled, tiled, vec, vec, mat, mat, mat, vec, vec, vec, mat, vec, mat, vec)
    return jax.shard_map(body, mesh=mesh, in_specs=in_specs, out_specs=out_specs, check_vma=False)
```

```python
import functools

import jax
import jax.numpy as jnp
from jax import lax
from jax.experimental import pallas as pl
from jax.experimental.pallas import tpu as pltpu
from jax.sharding import PartitionSpec as P

HEADS = 12
NORM_EPS = 1e-06
MASKED_SCORE = -1e30
GROUP = ("rows", "cols")
BF = jnp.bfloat16
F32 = jnp.float32


def dot(left, right, dims):
    return lax.dot_general(left, right, (dims, ((), ())), preferred_element_type=F32)


def mm(left, right):
    return dot(left, right, ((1,), (0,)))


def mm_nt(left, right):
    return dot(left, right, ((1,), (1,)))


def mm_tn(left, right):
    return dot(left, right, ((0,), (0,)))


def to_peer(value, rel):
    if rel == 1:
        return lax.ppermute(value, "cols", [(0, 1), (1, 0)])
    if rel == 2:
        return lax.ppermute(value, "rows", [(0, 1), (1, 0)])
    return lax.ppermute(value, GROUP, [(i, i ^ 3) for i in range(4)])


def tie(values, others):
    flat, tree = jax.tree.flatten((values, others))
    return jax.tree.unflatten(tree, lax.optimization_barrier(flat))


def gather_tiles(value, others=()):
    across = to_peer(value, 2)
    beside = to_peer(value, 1)
    across, others = tie(across, others)
    return [value, beside, across, to_peer(across, 1)], others


def scatter_tiles(blocks):
    return [blocks[0], to_peer(blocks[1], 1), to_peer(blocks[2], 2), to_peer(blocks[3], 3)]


def norm_stats(values):
    mean_val = jnp.mean(values, axis=-1, keepdims=True)
    centred = values - mean_val
    var_val = jnp.mean(centred * centred, axis=-1, keepdims=True)
    inv = lax.rsqrt(var_val + NORM_EPS)
    return centred * inv, inv


def norm_back(grads, normed, inv, gain):
    g = grads * gain
    return (
        g
        - jnp.mean(g, axis=-1, keepdims=True)
        - normed * jnp.mean(g * normed, axis=-1, keepdims=True)
    ) * inv


def gelu_parts(x):
    cdf = 0.5 * (1.0 + lax.erf(x * 0.7071067811865476))
    pdf = jnp.exp(-0.5 * x * x) * 0.3989422804014327
    return x * cdf, cdf + x * pdf


def start_imgs(parts, imgs):
    if imgs % 2 or imgs > 8:
        return parts, None
    side = lax.axis_index("imgs") % 2
    split = parts.reshape((imgs // 2, 2) + parts.shape[1:])
    send = lax.dynamic_index_in_dim(split, 1 - side, 1, keepdims=False)
    keep = lax.dynamic_index_in_dim(split, side, 1, keepdims=False)
    return keep, lax.ppermute(send, "imgs", [(i, i ^ 1) for i in range(imgs)])


def finish_imgs(state, imgs, low):
    keep, got = state
    if got is None:
        return lax.psum_scatter(keep, "imgs", scatter_dimension=0, tiled=False).astype(F32)
    place = lax.axis_index("imgs") // 2
    line = imgs // 2

    def pick(index):
        at = jnp.clip(index, 0, line - 1)
        a = lax.dynamic_index_in_dim(keep, at, 0, keepdims=False)
        b = lax.dynamic_index_in_dim(got, at, 0, keepdims=False)
        return a.astype(F32) + b.astype(F32)

    def hop(value, step, up):
        pairs = []
        for z in range(line):
            for y in range(2):
                if up and z <= step - 1 and z + 1 < line:
                    pairs.append((2 * z + y, 2 * (z + 1) + y))
                if not up and z >= line - step and z - 1 >= 0:
                    pairs.append((2 * z + y, 2 * (z - 1) + y))
        return lax.ppermute(value.astype(low), "imgs", pairs).astype(F32)

    up_val = pick(place + line - 1)
    down_val = pick(place - (line - 1))
    for step in range(1, line):
        got_up = hop(up_val, step, True)
        got_down = hop(down_val, step, False)
        if step < line - 1:
            up_val = pick(place + line - 1 - step) + got_up
            down_val = pick(place - (line - 1) + step) + got_down
    return pick(place) + got_up + got_down


def own_order(blocks, tile):
    stacked = jnp.stack(blocks)
    return [lax.dynamic_index_in_dim(stacked, tile ^ k, 0, keepdims=False) for k in range(4)]


SMEM = pl.BlockSpec(memory_space=pltpu.SMEM)
VMEM = pl.BlockSpec(memory_space=pltpu.VMEM)
PAD = 16


def vec_call(kernel, outs, n_in, scratch=(), us=5):
    return pl.pallas_call(
        kernel,
        out_shape=outs,
        in_specs=[SMEM] + [VMEM] * n_in,
        out_specs=jax.tree.map(lambda _: VMEM, outs),
        scratch_shapes=list(scratch),
        cost_estimate=cost(us),
    )


def cost(us):
    return pl.CostEstimate(flops=us * 10**9, transcendentals=0, bytes_accessed=us * 10**6)


def sds(shape, dtype=BF):
    return jax.ShapeDtypeStruct(shape, dtype)


def load_tile(ref, scratch, at):
    rows, cols, width = ref.shape[1:]
    scratch[at : at + rows * PAD, :] = jnp.zeros((rows * PAD, width), scratch.dtype)
    for i in range(rows):
        scratch[at + i * PAD : at + i * PAD + cols, :] = ref[0, i]


def store_tile(ref, value):
    rows, cols, _ = ref.shape[1:]
    for i in range(rows):
        ref[0, i] = value[i * PAD : i * PAD + cols, :]


def mask_edges(mask):
    m = mask[0].astype(F32)
    high = jnp.sum(m[:, 0:1], axis=0, keepdims=True)
    wide = jnp.sum(m[0:1, :], axis=1, keepdims=True)
    return high, wide


def keep_tokens(edges, place, rows, cols, axis):
    toks = rows * PAD
    shape = (toks, 1) if axis == 0 else (1, toks)
    tok = lax.broadcasted_iota(jnp.int32, shape, axis)
    c = tok & (PAD - 1)
    r = ((tok >> 4) + (place >> 1) * rows).astype(F32)
    at = (c + (place & 1) * cols).astype(F32)
    ok = (c < cols) & (r < edges[0]) & (at < edges[1])
    return jnp.where(ok, 1.0, 0.0).astype(F32)


def vec_row(ref):
    return ref[...].reshape(1, -1)


def heads_kernel(tile, qkv_w, qv_b, w_own, b_own):
    width = qv_b.shape[1]
    part = width // 4
    for g in range(4):

        @pl.when(tile[0] == g)
        def _():
            for i in range(3):
                src = i * width + g * part
                w_own[:, i * part : (i + 1) * part] = qkv_w[:, src : src + part]
            b_own[:, :part] = qv_b[0:1, g * part : (g + 1) * part]
            b_own[:, part : 2 * part] = jnp.zeros((1, part), F32)
            b_own[:, 2 * part :] = qv_b[1:2, g * part : (g + 1) * part]


def units_kernel(tile, fc1, fc1_b, fc1_own, fc1_b_own, *, quarter):
    for g in range(4):

        @pl.when(tile[0] == g)
        def _():
            for i in range(fc1.shape[1] // (4 * quarter)):
                src = (4 * i + g) * quarter
                dst = i * quarter
                fc1_own[:, dst : dst + quarter] = fc1[:, src : src + quarter]
                fc1_b_own[:, dst : dst + quarter] = fc1_b[:, src : src + quarter]


def attn_kernel(
    tile, mask, x0, x1, x2, x3, gain, shift, w, bias, hid, nrm, qkv, lse, c0, c1, c2, c3, xs, ctx
):
    rows, cols, width = x0.shape[1:]
    toks = rows * PAD
    part = w.shape[1] // 3
    dim = width // HEADS
    scale = dim ** (-0.5)
    for r, ref in enumerate((x0, x1, x2, x3)):
        load_tile(ref, xs, r * toks)

    def project(r, carry):
        at = pl.ds(pl.multiple_of(r * toks, toks), toks)
        normed, _ = norm_stats(xs[at, :].astype(F32))
        h = (normed * vec_row(gain) + vec_row(shift)).astype(BF)
        hid[at, :] = h
        nrm[at, :] = normed.astype(BF)
        qkv[at, :] = (mm(h, w[...]) + bias[...]).astype(BF)
        return carry

    lax.fori_loop(0, 4, project, 0)
    edges = mask_edges(mask)
    keep = jnp.concatenate(
        [keep_tokens(edges, tile[0] ^ r, rows, cols, 1) for r in range(4)], axis=1
    )

    def attend(r, carry):
        at = pl.ds(pl.multiple_of(r * toks, toks), toks)
        outs = []
        for h in range(part // dim):
            q = qkv[at, h * dim : (h + 1) * dim]
            k = qkv[:, part + h * dim : part + (h + 1) * dim]
            v = qkv[:, 2 * part + h * dim : 2 * part + (h + 1) * dim]
            s = jnp.where(keep > 0, mm_nt(q * scale, k), MASKED_SCORE)
            top = jnp.max(s, axis=-1, keepdims=True)
            e = jnp.exp(s - top)
            total = jnp.sum(e, axis=-1, keepdims=True)
            outs.append(mm((e * (1.0 / total)).astype(BF), v).astype(BF))
            lse[at, h : h + 1] = top + jnp.log(total)
        ctx[r] = jnp.concatenate(outs, axis=1)
        return carry

    lax.fori_loop(0, 4, attend, 0)
    for r, ref in enumerate((c0, c1, c2, c3)):
        ref[...] = ctx[r]


def branch_kernel(tile, c0, c1, c2, c3, wo, bo, x, gain, shift, resid, hid, xs):
    part = c0.shape[1]
    load_tile(x, xs, 0)
    acc = xs[...].astype(F32) + vec_row(bo)
    for r, ref in enumerate((c0, c1, c2, c3)):
        at = pl.multiple_of((tile[0] ^ r) * part, part)
        acc = acc + mm(ref[...], wo[pl.ds(at, part), :])
    resid[...] = acc
    normed, _ = norm_stats(acc)
    hid[...] = (normed * vec_row(gain) + vec_row(shift)).astype(BF)


def mlp_kernel(
    tile, mask, resid, hid, ct, gain, fc1, fc1_b, fc2, fc2_b, out, branch, rgrad, vecs, up, acc, nacc
):
    step = pl.program_id(0)
    rows, cols, _ = ct.shape[1:]

    @pl.when(step == 0)
    def _():
        load_tile(ct, up, 0)
        up[...] = (up[...].astype(F32) * keep_tokens(mask_edges(mask), tile[0], rows, cols, 0)).astype(BF)
        acc[...] = jnp.zeros_like(acc)
        nacc[...] = jnp.zeros_like(nacc)

    act, dgelu = gelu_parts(mm(hid[...], fc1[...]) + fc1_b[...])
    acc[...] += mm(act.astype(BF), fc2[...])
    inner = (mm_nt(up[...], fc2[...]) * dgelu).astype(BF)
    nacc[...] += mm_nt(inner, fc1[...])

    @pl.when(step == pl.num_programs(0) - 1)
    def _():
        res = resid[...]
        keep = keep_tokens(mask_edges(mask), tile[0], rows, cols, 0)
        store_tile(out, (keep * (res + acc[...] + vec_row(fc2_b))).astype(BF))
        normed, inv = norm_stats(res)
        n = nacc[...]
        vecs[0:1, :] = jnp.sum(n * normed, axis=0, keepdims=True)
        vecs[1:2, :] = jnp.sum(n, axis=0, keepdims=True)
        grad = up[...].astype(F32) + norm_back(n, normed, inv, vec_row(gain))
        rgrad[...] = grad
        branch[...] = grad.astype(BF)


def ffgrad_kernel(
    tile, mask, h0, h1, h2, h3, t0, t1, t2, t3, fc1, fc1_b, fc2, g1, g2, b1, b2, up, a1, a2
):
    rows, cols, _ = t0.shape[1:]
    edges = mask_edges(mask)
    hids = (h0, h1, h2, h3)
    for r, ref in enumerate((t0, t1, t2, t3)):
        load_tile(ref, up, 0)
        wide = up[...].astype(F32) * keep_tokens(edges, tile[0] ^ r, rows, cols, 0)
        low = wide.astype(BF)
        h = hids[r][...]
        act, dgelu = gelu_parts(mm(h, fc1[...]) + fc1_b[...])
        inner = (mm_nt(low, fc2[...]) * dgelu).astype(BF)
        d1 = mm_tn(h, inner)
        d2 = mm_tn(act.astype(BF), low)
        s1 = jnp.sum(inner.astype(F32), axis=0, keepdims=True)
        s2 = jnp.sum(wide, axis=0, keepdims=True)
        if r == 0:
            a1[...], a2[...], b1[...], b2[...] = d1, d2, s1, s2
        elif r < 3:
            a1[...] += d1
            a2[...] += d2
            b1[...] += s1
            b2[...] += s2
        else:
            g1[...] = (a1[...] + d1).astype(BF)
            g2[...] = (a2[...] + d2).astype(BF)
            b1[...] += s1
            b2[...] += s2


def outgrad_kernel(tile, b0, b1, b2, b3, wo, c0, c1, c2, c3, dctx, gout, bsum):
    toks, part = c0.shape
    at = pl.multiple_of(tile[0] * part, part)
    w = wo[pl.ds(at, part), :]
    ctx = (c0, c1, c2, c3)
    acc = None
    total = None
    for r, ref in enumerate((b0, b1, b2, b3)):
        low = ref[...]
        dctx[r * toks : (r + 1) * toks, :] = mm_nt(low, w).astype(BF)
        d = mm_tn(ctx[r][...], low)
        s = jnp.sum(low.astype(F32), axis=0, keepdims=True)
        acc = d if r == 0 else acc + d
        total = s if r == 0 else total + s
    gout[...] = acc.astype(BF)
    bsum[...] = total


def attnback_kernel(
    tile, mask, dctx, qkv, lse, hid, nrm, w, m0, m1, m2, m3, gqkv, msum, nsum, dk, dv, mix, *, cols
):
    total, three = qkv.shape
    part = three // 3
    toks = total // 4
    dim = hid.shape[1] // HEADS
    rows = toks // PAD
    scale = dim ** (-0.5)
    edges = mask_edges(mask)
    keep = jnp.concatenate(
        [keep_tokens(edges, tile[0] ^ r, rows, cols, 1) for r in range(4)], axis=1
    )
    dk[...] = jnp.zeros_like(dk)
    dv[...] = jnp.zeros_like(dv)

    def attend(r, carry):
        at = pl.ds(pl.multiple_of(r * toks, toks), toks)
        dqs = []
        for h in range(part // dim):
            at_h = slice(h * dim, (h + 1) * dim)
            k = qkv[:, part + h * dim : part + (h + 1) * dim]
            v = qkv[:, 2 * part + h * dim : 2 * part + (h + 1) * dim]
            q = qkv[at, at_h] * scale
            do = dctx[at, at_h]
            s = jnp.where(keep > 0, mm_nt(q, k), MASKED_SCORE)
            p = jnp.exp(s - lse[at, h : h + 1])
            dp = mm_nt(do, v)
            ds = (p * (dp - jnp.sum(dp * p, axis=-1, keepdims=True))).astype(BF)
            dqs.append((mm(ds, k) * scale).astype(BF))
            dv[h] += mm_tn(p.astype(BF), do)
            dk[h] += mm_tn(ds, q)
        mix[at, :part] = jnp.concatenate(dqs, axis=1)
        return carry

    lax.fori_loop(0, 4, attend, 0)
    for h in range(part // dim):
        mix[:, part + h * dim : part + (h + 1) * dim] = dk[h].astype(BF)
        mix[:, 2 * part + h * dim : 2 * part + (h + 1) * dim] = dv[h].astype(BF)
    gqkv[...] = mm_tn(hid[...], mix[...]).astype(BF)
    for r, ref in enumerate((m0, m1, m2, m3)):
        at = slice(r * toks, (r + 1) * toks)
        m = mix[at, :]
        ref[...] = m
        n = mm_nt(m, w[...])
        a = jnp.sum(n * nrm[at, :].astype(F32), axis=0, keepdims=True)
        b = jnp.sum(n, axis=0, keepdims=True)
        c = jnp.sum(m.astype(F32), axis=0, keepdims=True)
        if r == 0:
            nsum[0:1, :] = a
            nsum[1:2, :] = b
            msum[...] = c
        else:
            nsum[0:1, :] += a
            nsum[1:2, :] += b
            msum[...] += c


def input_kernel(tile, m0, m1, m2, m3, w, x, rgrad, gain, out, ms, xs):
    part = m0.shape[1] // 3
    for r, ref in enumerate((m0, m1, m2, m3)):
        ms[r] = ref[...]
    tiles = [ms[tile[0] ^ g] for g in range(4)]
    full = jnp.concatenate(
        [m[:, i * part : (i + 1) * part] for i in range(3) for m in tiles], axis=1
    )
    n = mm_nt(full, w[...])
    load_tile(x, xs, 0)
    normed, inv = norm_stats(xs[...].astype(F32))
    store_tile(out, (rgrad[...] + norm_back(n, normed, inv, vec_row(gain))).astype(BF))


def ffout_kernel(tile, p0, p1, p2, p3, fc1, fc2, ps):
    rows = fc1.shape[0]
    quarter = fc2.shape[0] // 4
    for r, ref in enumerate((p0, p1, p2, p3)):
        ps[r] = ref[...].astype(F32)
    for g in range(4):
        piece = ps[tile[0] ^ g]
        for i in range(fc1.shape[1] // (4 * quarter)):
            dst = (4 * i + g) * quarter
            fc1[:, dst : dst + quarter] = piece[:rows, i * quarter : (i + 1) * quarter]
        fc2[g * quarter : (g + 1) * quarter, :] = piece[rows:, :]


def attnout_kernel(tile, p0, p1, p2, p3, gqkv, gout, vecs, ps):
    rows = gqkv.shape[0]
    width = gout.shape[1]
    part = width // 4
    for r, ref in enumerate((p0, p1, p2, p3)):
        ps[r] = ref[...].astype(F32)
    total = None
    for g in range(4):
        piece = ps[tile[0] ^ g]
        for i in range(3):
            dst = i * width + g * part
            gqkv[:, dst : dst + part] = piece[:rows, i * part : (i + 1) * part]
        gout[:, g * part : (g + 1) * part] = piece[:rows, 3 * part :]
        tail = piece[rows:, :]
        total = tail if g == 0 else total + tail
    vecs[...] = total


def body(
    patches,
    patch_mask,
    norm1_gain,
    norm1_shift,
    qkv_weight,
    qv_bias,
    out_weight,
    out_bias,
    norm2_gain,
    norm2_shift,
    fc1_weight,
    fc1_bias,
    fc2_weight,
    fc2_bias,
    cotangent,
):
    _, rows, cols, width = patches.shape
    ff = fc1_weight.shape[1]
    imgs = lax.axis_size("imgs")
    part = width // 4
    units = ff // 4
    quarter = units // imgs
    share = width // imgs
    toks = rows * PAD
    total = 4 * toks
    tile = lax.axis_index("rows") * 2 + lax.axis_index("cols")
    at_tile = tile.reshape(1).astype(jnp.int32)

    def row(v):
        return v.reshape(1, -1)

    steps = 4
    w_own, b_own = pl.pallas_call(
        heads_kernel,
        grid=(steps,),
        in_specs=[
            SMEM,
            pl.BlockSpec((width // steps, 3 * width), lambda i: (i, 0)),
            pl.BlockSpec((2, width), lambda i: (0, 0)),
        ],
        out_specs=[
            pl.BlockSpec((width // steps, 3 * part), lambda i: (i, 0)),
            pl.BlockSpec((1, 3 * part), lambda i: (0, 0)),
        ],
        out_shape=[sds((width, 3 * part)), sds((1, 3 * part), F32)],
        cost_estimate=cost(4),
        name="heads",
    )(at_tile, qkv_weight, qv_bias.T)
    x_blocks, (w_own, b_own) = gather_tiles(patches, (w_own, b_own))

    hid1, nrm1, qkv, lse, *ctx = vec_call(
        attn_kernel,
        [
            sds((total, width)),
            sds((total, width)),
            sds((total, 3 * part)),
            sds((total, 128), F32),
        ]
        + [sds((toks, part))] * 4,
        9,
        [pltpu.VMEM((total, width), BF), pltpu.VMEM((4, toks, part), BF)],
        us=13,
    )(at_tile, patch_mask, *x_blocks, norm1_gain, norm1_shift, w_own, b_own)
    ct_blocks, ctx = gather_tiles(cotangent, ctx)

    fc1_own, fc1_b_own = pl.pallas_call(
        functools.partial(units_kernel, quarter=quarter),
        grid=(steps,),
        in_specs=[
            SMEM,
            pl.BlockSpec((width // steps, ff), lambda i: (i, 0)),
            pl.BlockSpec((1, ff), lambda i: (0, 0)),
        ],
        out_specs=[
            pl.BlockSpec((width // steps, units), lambda i: (i, 0)),
            pl.BlockSpec((1, units), lambda i: (0, 0)),
        ],
        out_shape=[sds((width, units)), sds((1, units), F32)],
        cost_estimate=cost(4),
        name="units",
    )(at_tile, fc1_weight, row(fc1_bias))
    fc2_own = lax.dynamic_index_in_dim(
        fc2_weight.reshape(imgs, 4, quarter, width), tile, 1, keepdims=False
    ).reshape(units, width)

    ctx_in = scatter_tiles(ctx)
    ctx_in, (fc1_own, fc1_b_own, fc2_own) = tie(ctx_in, (fc1_own, fc1_b_own, fc2_own))
    resid, hid2 = vec_call(
        branch_kernel,
        [sds((toks, width), F32), sds((toks, width))],
        9,
        [pltpu.VMEM((toks, width), BF)],
        us=3,
    )(at_tile, *ctx_in, out_weight, out_bias, patches, norm2_gain, norm2_shift)

    chunks = 4
    step = ff // chunks

    def whole(*shape):
        return pl.BlockSpec(shape, lambda i: (0,) * len(shape))

    layer_out, branch, rgrad, vec2 = pl.pallas_call(
        mlp_kernel,
        grid=(chunks,),
        in_specs=[
            SMEM,
            whole(*patch_mask.shape),
            whole(toks, width),
            whole(toks, width),
            whole(1, rows, cols, width),
            whole(width),
            pl.BlockSpec((width, step), lambda i: (0, i)),
            pl.BlockSpec((1, step), lambda i: (0, i)),
            pl.BlockSpec((step, width), lambda i: (i, 0)),
            whole(width),
        ],
        out_specs=[
            whole(1, rows, cols, width),
            whole(toks, width),
            whole(toks, width),
            whole(2, width),
        ],
        out_shape=[
            sds((1, rows, cols, width)),
            sds((toks, width)),
            sds((toks, width), F32),
            sds((2, width), F32),
        ],
        scratch_shapes=[
            pltpu.VMEM((toks, width), BF),
            pltpu.VMEM((toks, width), F32),
            pltpu.VMEM((toks, width), F32),
        ],
        cost_estimate=cost(11),
        name="mlp",
    )(
        at_tile,
        patch_mask,
        resid,
        hid2,
        cotangent,
        norm2_gain,
        fc1_weight,
        row(fc1_bias),
        fc2_weight,
        fc2_bias,
    )
    hid2_blocks, (branch,) = gather_tiles(hid2, (branch,))

    g1, g2, fb1, fb2 = vec_call(
        ffgrad_kernel,
        [sds((width, units)), sds((units, width)), sds((1, units), F32), sds((1, width), F32)],
        12,
        [
            pltpu.VMEM((toks, width), BF),
            pltpu.VMEM((width, units), F32),
            pltpu.VMEM((units, width), F32),
        ],
        us=9,
    )(at_tile, patch_mask, *hid2_blocks, *ct_blocks, fc1_own, fc1_b_own, fc2_own)
    branch_blocks, (g1, g2) = gather_tiles(branch, (g1, g2))

    dctx, gout, bsum = vec_call(
        outgrad_kernel,
        [sds((total, part)), sds((part, width)), sds((1, width), F32)],
        9,
        us=4,
    )(at_tile, *branch_blocks, out_weight, *ctx)
    ff_bucket = jnp.concatenate(
        [g1.reshape(imgs, share, units), g2.reshape(imgs, quarter, width)], axis=1
    )
    ff_start = start_imgs(ff_bucket, imgs)
    out_cols = [lax.dynamic_slice_in_dim(gout, (tile ^ r) * part, part, 1) for r in range(4)]
    out_rows = scatter_tiles(out_cols)

    *mixed, gqkv, msum, nsum = vec_call(
        functools.partial(attnback_kernel, cols=cols),
        [sds((toks, 3 * part))] * 4
        + [
            sds((width, 3 * part)),
            sds((1, 3 * part), F32),
            sds((2, width), F32),
        ],
        7,
        [
            pltpu.VMEM((part * HEADS // width, total, width // HEADS), F32),
            pltpu.VMEM((part * HEADS // width, total, width // HEADS), F32),
            pltpu.VMEM((total, 3 * part), BF),
        ],
        us=18,
    )(at_tile, patch_mask, dctx, qkv, lse, hid1, nrm1, w_own)
    mixed_in = scatter_tiles(mixed)
    out_rows, (gqkv,) = tie(out_rows, (gqkv,))
    out_rows = own_order(out_rows, tile)

    lone = (tile == 0).astype(F32)
    fb1_row = lax.dynamic_update_index_in_dim(
        jnp.zeros((imgs, 4, quarter), F32), fb1.reshape(imgs, quarter), tile, 1
    )
    heads_row = lax.dynamic_update_index_in_dim(
        jnp.zeros((3, 4, part), F32), msum.reshape(3, part), tile, 1
    ).reshape(3, width)
    vec_rows = [nsum, heads_row, bsum * lone, vec2, fb2 * lone]
    vecs = jnp.concatenate(vec_rows, axis=0).reshape(9, imgs, share).transpose(1, 0, 2)
    vecs = jnp.concatenate(
        [vecs.reshape(imgs, 9 * share), fb1_row.reshape(imgs, 4 * quarter)], axis=1
    ).astype(BF)
    count = vecs.shape[1]
    vec_height = -(-count // width)
    vecs = jnp.pad(vecs, ((0, 0), (0, vec_height * width - count)))
    at_bucket = jnp.concatenate(
        [
            jnp.concatenate([gqkv, jnp.concatenate(out_rows, axis=0)], axis=1).reshape(
                imgs, share, width
            ),
            vecs.reshape(imgs, vec_height, width),
        ],
        axis=1,
    )
    at_start = start_imgs(at_bucket, imgs)
    ff_start, (mixed_in[0],) = tie(ff_start, (mixed_in[0],))
    ff_sum = finish_imgs(ff_start, imgs, BF)

    patches_grad = vec_call(
        input_kernel,
        sds((1, rows, cols, width)),
        8,
        [pltpu.VMEM((4, toks, 3 * part), BF), pltpu.VMEM((toks, width), BF)],
        us=5,
    )(at_tile, *mixed_in, qkv_weight, patches, rgrad, norm1_gain)

    at_start, (patches_grad, ff_sum) = tie(at_start, (patches_grad, ff_sum))
    ff_pieces, _ = gather_tiles(ff_sum.astype(BF))
    at_sum = finish_imgs(at_start, imgs, BF)
    fc1_grad, fc2_grad = vec_call(
        ffout_kernel,
        [sds((share, ff), F32), sds((4 * quarter, width), F32)],
        4,
        [pltpu.VMEM((4, share + quarter, width), F32)],
        us=3,
    )(at_tile, *ff_pieces)
    at_pieces, (fc1_grad, fc2_grad) = gather_tiles(at_sum.astype(BF), (fc1_grad, fc2_grad))
    qkv_grad, out_grad, vec_sum = vec_call(
        attnout_kernel,
        [sds((share, 3 * width), F32), sds((share, width), F32), sds((vec_height, width), F32)],
        4,
        [pltpu.VMEM((4, share + vec_height, width), F32)],
        us=3,
    )(at_tile, *at_pieces)
    v = vec_sum.reshape(-1)
    piece = [v[i * share : (i + 1) * share] for i in range(9)]
    return (
        layer_out,
        patches_grad,
        piece[0],
        piece[1],
        qkv_grad,
        jnp.stack([piece[2], piece[4]], axis=1),
        out_grad,
        piece[5],
        piece[6],
        piece[7],
        fc1_grad,
        v[9 * share : count],
        fc2_grad,
        piece[8],
    )


def solution(mesh):
    tiled = P("imgs", "rows", "cols", None)
    in_specs = (tiled, P("imgs", None, None)) + (P(),) * 12 + (tiled,)
    mat = P("imgs", None)
    vec = P("imgs")
    out_specs = (tiled, tiled, vec, vec, mat, mat, mat, vec, vec, vec, mat, vec, mat, vec)
    return jax.shard_map(body, mesh=mesh, in_specs=in_specs, out_specs=out_specs, check_vma=False)
```

```python
import functools

import jax
import jax.numpy as jnp
from jax import lax
from jax.experimental import pallas as pl
from jax.experimental.pallas import tpu as pltpu
from jax.sharding import PartitionSpec as P

HEADS = 12
NORM_EPS = 1e-06
MASKED_SCORE = -1e30
GROUP = ("rows", "cols")
BF = jnp.bfloat16
F32 = jnp.float32


def dot(left, right, dims):
    return lax.dot_general(left, right, (dims, ((), ())), preferred_element_type=F32)


def mm(left, right):
    return dot(left, right, ((1,), (0,)))


def mm_nt(left, right):
    return dot(left, right, ((1,), (1,)))


def mm_tn(left, right):
    return dot(left, right, ((0,), (0,)))


def to_peer(value, rel):
    if rel == 1:
        return lax.ppermute(value, "cols", [(0, 1), (1, 0)])
    if rel == 2:
        return lax.ppermute(value, "rows", [(0, 1), (1, 0)])
    return lax.ppermute(value, GROUP, [(i, i ^ 3) for i in range(4)])


def tie(values, others):
    flat, tree = jax.tree.flatten((values, others))
    return jax.tree.unflatten(tree, lax.optimization_barrier(flat))


def gather_tiles(value, others=()):
    across = to_peer(value, 2)
    beside = to_peer(value, 1)
    across, others = tie(across, others)
    return [value, beside, across, to_peer(across, 1)], others


def scatter_tiles(blocks):
    return [blocks[0], to_peer(blocks[1], 1), to_peer(blocks[2], 2), to_peer(blocks[3], 3)]


def norm_stats(values):
    mean_val = jnp.mean(values, axis=-1, keepdims=True)
    centred = values - mean_val
    var_val = jnp.mean(centred * centred, axis=-1, keepdims=True)
    inv = lax.rsqrt(var_val + NORM_EPS)
    return centred * inv, inv


def norm_back(grads, normed, inv, gain):
    g = grads * gain
    return (
        g
        - jnp.mean(g, axis=-1, keepdims=True)
        - normed * jnp.mean(g * normed, axis=-1, keepdims=True)
    ) * inv


def gelu_parts(x):
    cdf = 0.5 * (1.0 + lax.erf(x * 0.7071067811865476))
    pdf = jnp.exp(-0.5 * x * x) * 0.3989422804014327
    return x * cdf, cdf + x * pdf


def exchange_near(parts):
    side = lax.axis_index("imgs") % 2
    count = lax.axis_size("imgs")
    send = lax.dynamic_index_in_dim(parts, 1 - side, 1, keepdims=False)
    keep = lax.dynamic_index_in_dim(parts, side, 1, keepdims=False)
    return keep, lax.ppermute(send, "imgs", [(i, i ^ 1) for i in range(count)])


def exchange_far(parts):
    count = lax.axis_size("imgs")
    place = lax.axis_index("imgs") // 2
    got = [lax.dynamic_index_in_dim(parts, place, 0, keepdims=False)]
    for k in range(count // 2 - 1, 0, -1):
        send = lax.dynamic_index_in_dim(parts, place ^ k, 0, keepdims=False)
        got.append(lax.ppermute(send, "imgs", [(i, i ^ (2 * k)) for i in range(count)]))
    return got


def total_of(blocks):
    return functools.reduce(jnp.add, [b.astype(F32) for b in blocks])


def direct_sum(imgs):
    return imgs <= 8 and imgs & (imgs - 1) == 0


def plain_sum(parts):
    return lax.psum_scatter(parts, "imgs", scatter_dimension=0, tiled=False)


def own_order(blocks, tile):
    stacked = jnp.stack(blocks)
    return [lax.dynamic_index_in_dim(stacked, tile ^ k, 0, keepdims=False) for k in range(4)]


SMEM = pl.BlockSpec(memory_space=pltpu.SMEM)
VMEM = pl.BlockSpec(memory_space=pltpu.VMEM)
PAD = 16


def vec_call(kernel, outs, n_in, scratch=(), us=5):
    return pl.pallas_call(
        kernel,
        out_shape=outs,
        in_specs=[SMEM] + [VMEM] * n_in,
        out_specs=jax.tree.map(lambda _: VMEM, outs),
        scratch_shapes=list(scratch),
        cost_estimate=cost(us),
    )


def cost(us):
    return pl.CostEstimate(flops=us * 10**9, transcendentals=0, bytes_accessed=us * 10**6)


def sds(shape, dtype=BF):
    return jax.ShapeDtypeStruct(shape, dtype)


def load_tile(ref, scratch, at):
    rows, cols, width = ref.shape[1:]
    scratch[at : at + rows * PAD, :] = jnp.zeros((rows * PAD, width), scratch.dtype)
    for i in range(rows):
        scratch[at + i * PAD : at + i * PAD + cols, :] = ref[0, i]


def store_tile(ref, value):
    rows, cols, _ = ref.shape[1:]
    for i in range(rows):
        ref[0, i] = value[i * PAD : i * PAD + cols, :]


def mask_edges(mask):
    m = mask[0].astype(F32)
    high = jnp.sum(m[:, 0:1], axis=0, keepdims=True)
    wide = jnp.sum(m[0:1, :], axis=1, keepdims=True)
    return high, wide


def keep_tokens(edges, place, rows, cols, axis):
    toks = rows * PAD
    shape = (toks, 1) if axis == 0 else (1, toks)
    tok = lax.broadcasted_iota(jnp.int32, shape, axis)
    c = tok & (PAD - 1)
    r = ((tok >> 4) + (place >> 1) * rows).astype(F32)
    at = (c + (place & 1) * cols).astype(F32)
    ok = (c < cols) & (r < edges[0]) & (at < edges[1])
    return jnp.where(ok, 1.0, 0.0).astype(F32)


def vec_row(ref):
    return ref[...].reshape(1, -1)


def heads_kernel(tile, qkv_w, qv_b, w_own, b_own):
    width = qv_b.shape[1]
    part = width // 4
    for g in range(4):

        @pl.when(tile[0] == g)
        def _():
            for i in range(3):
                src = i * width + g * part
                w_own[:, i * part : (i + 1) * part] = qkv_w[:, src : src + part]
            b_own[:, :part] = qv_b[0:1, g * part : (g + 1) * part]
            b_own[:, part : 2 * part] = jnp.zeros((1, part), F32)
            b_own[:, 2 * part :] = qv_b[1:2, g * part : (g + 1) * part]


def units_kernel(tile, fc1, fc1_b, fc1_own, fc1_b_own, *, quarter):
    for g in range(4):

        @pl.when(tile[0] == g)
        def _():
            for i in range(fc1.shape[1] // (4 * quarter)):
                src = (4 * i + g) * quarter
                dst = i * quarter
                fc1_own[:, dst : dst + quarter] = fc1[:, src : src + quarter]
                fc1_b_own[:, dst : dst + quarter] = fc1_b[:, src : src + quarter]


def attn_kernel(
    tile, mask, x0, x1, x2, x3, gain, shift, w, bias, hid, nrm, qkv, lse, c0, c1, c2, c3, xs, ctx
):
    rows, cols, width = x0.shape[1:]
    toks = rows * PAD
    part = w.shape[1] // 3
    dim = width // HEADS
    scale = dim ** (-0.5)
    for r, ref in enumerate((x0, x1, x2, x3)):
        load_tile(ref, xs, r * toks)

    def project(r, carry):
        at = pl.ds(pl.multiple_of(r * toks, toks), toks)
        normed, _ = norm_stats(xs[at, :].astype(F32))
        h = (normed * vec_row(gain) + vec_row(shift)).astype(BF)
        hid[at, :] = h
        nrm[at, :] = normed.astype(BF)
        qkv[at, :] = (mm(h, w[...]) + bias[...]).astype(BF)
        return carry

    lax.fori_loop(0, 4, project, 0)
    edges = mask_edges(mask)
    keep = jnp.concatenate(
        [keep_tokens(edges, tile[0] ^ r, rows, cols, 1) for r in range(4)], axis=1
    )

    def attend(r, carry):
        at = pl.ds(pl.multiple_of(r * toks, toks), toks)
        outs = []
        for h in range(part // dim):
            q = qkv[at, h * dim : (h + 1) * dim]
            k = qkv[:, part + h * dim : part + (h + 1) * dim]
            v = qkv[:, 2 * part + h * dim : 2 * part + (h + 1) * dim]
            s = jnp.where(keep > 0, mm_nt(q * scale, k), MASKED_SCORE)
            top = jnp.max(s, axis=-1, keepdims=True)
            e = jnp.exp(s - top)
            total = jnp.sum(e, axis=-1, keepdims=True)
            outs.append(mm((e * (1.0 / total)).astype(BF), v).astype(BF))
            lse[at, h : h + 1] = top + jnp.log(total)
        ctx[r] = jnp.concatenate(outs, axis=1)
        return carry

    lax.fori_loop(0, 4, attend, 0)
    for r, ref in enumerate((c0, c1, c2, c3)):
        ref[...] = ctx[r]


def branch_kernel(tile, c0, c1, c2, c3, wo, bo, x, gain, shift, resid, hid, xs):
    part = c0.shape[1]
    load_tile(x, xs, 0)
    acc = xs[...].astype(F32) + vec_row(bo)
    for r, ref in enumerate((c0, c1, c2, c3)):
        at = pl.multiple_of((tile[0] ^ r) * part, part)
        acc = acc + mm(ref[...], wo[pl.ds(at, part), :])
    resid[...] = acc
    normed, _ = norm_stats(acc)
    hid[...] = (normed * vec_row(gain) + vec_row(shift)).astype(BF)


def mlp_kernel(
    tile, mask, resid, hid, ct, gain, fc1, fc1_b, fc2, fc2_b, out, branch, rgrad, vecs, up, acc, nacc
):
    step = pl.program_id(0)
    rows, cols, _ = ct.shape[1:]

    @pl.when(step == 0)
    def _():
        load_tile(ct, up, 0)
        up[...] = (up[...].astype(F32) * keep_tokens(mask_edges(mask), tile[0], rows, cols, 0)).astype(BF)
        acc[...] = jnp.zeros_like(acc)
        nacc[...] = jnp.zeros_like(nacc)

    act, dgelu = gelu_parts(mm(hid[...], fc1[...]) + fc1_b[...])
    acc[...] += mm(act.astype(BF), fc2[...])
    inner = (mm_nt(up[...], fc2[...]) * dgelu).astype(BF)
    nacc[...] += mm_nt(inner, fc1[...])

    @pl.when(step == pl.num_programs(0) - 1)
    def _():
        res = resid[...]
        keep = keep_tokens(mask_edges(mask), tile[0], rows, cols, 0)
        store_tile(out, (keep * (res + acc[...] + vec_row(fc2_b))).astype(BF))
        normed, inv = norm_stats(res)
        n = nacc[...]
        vecs[0:1, :] = jnp.sum(n * normed, axis=0, keepdims=True)
        vecs[1:2, :] = jnp.sum(n, axis=0, keepdims=True)
        grad = up[...].astype(F32) + norm_back(n, normed, inv, vec_row(gain))
        rgrad[...] = grad
        branch[...] = grad.astype(BF)


def ffgrad_kernel(
    tile, mask, h0, h1, h2, h3, t0, t1, t2, t3, fc1, fc1_b, fc2, g1, g2, b1, b2, up, a1, a2
):
    rows, cols, _ = t0.shape[1:]
    edges = mask_edges(mask)
    hids = (h0, h1, h2, h3)
    for r, ref in enumerate((t0, t1, t2, t3)):
        load_tile(ref, up, 0)
        wide = up[...].astype(F32) * keep_tokens(edges, tile[0] ^ r, rows, cols, 0)
        low = wide.astype(BF)
        h = hids[r][...]
        act, dgelu = gelu_parts(mm(h, fc1[...]) + fc1_b[...])
        inner = (mm_nt(low, fc2[...]) * dgelu).astype(BF)
        d1 = mm_tn(h, inner)
        d2 = mm_tn(act.astype(BF), low)
        s1 = jnp.sum(inner.astype(F32), axis=0, keepdims=True)
        s2 = jnp.sum(wide, axis=0, keepdims=True)
        if r == 0:
            a1[...], a2[...], b1[...], b2[...] = d1, d2, s1, s2
        elif r < 3:
            a1[...] += d1
            a2[...] += d2
            b1[...] += s1
            b2[...] += s2
        else:
            g1[...] = (a1[...] + d1).astype(BF)
            g2[...] = (a2[...] + d2).astype(BF)
            b1[...] += s1
            b2[...] += s2


def outgrad_kernel(tile, b0, b1, b2, b3, wo, c0, c1, c2, c3, dctx, gout, bsum):
    toks, part = c0.shape
    at = pl.multiple_of(tile[0] * part, part)
    w = wo[pl.ds(at, part), :]
    ctx = (c0, c1, c2, c3)
    acc = None
    total = None
    for r, ref in enumerate((b0, b1, b2, b3)):
        low = ref[...]
        dctx[r * toks : (r + 1) * toks, :] = mm_nt(low, w).astype(BF)
        d = mm_tn(ctx[r][...], low)
        s = jnp.sum(low.astype(F32), axis=0, keepdims=True)
        acc = d if r == 0 else acc + d
        total = s if r == 0 else total + s
    gout[...] = acc.astype(BF)
    bsum[...] = total


def attnback_kernel(
    tile,
    mask,
    dctx,
    qkv,
    lse,
    hid,
    nrm,
    w,
    bsum,
    vec2,
    fb2,
    m0,
    m1,
    m2,
    m3,
    gqkv,
    vecs,
    dk,
    dv,
    mix,
    *,
    cols,
):
    total, three = qkv.shape
    part = three // 3
    toks = total // 4
    dim = hid.shape[1] // HEADS
    rows = toks // PAD
    scale = dim ** (-0.5)
    edges = mask_edges(mask)
    keep = jnp.concatenate(
        [keep_tokens(edges, tile[0] ^ r, rows, cols, 1) for r in range(4)], axis=1
    )
    dk[...] = jnp.zeros_like(dk)
    dv[...] = jnp.zeros_like(dv)

    def attend(r, carry):
        at = pl.ds(pl.multiple_of(r * toks, toks), toks)
        dqs = []
        for h in range(part // dim):
            at_h = slice(h * dim, (h + 1) * dim)
            k = qkv[:, part + h * dim : part + (h + 1) * dim]
            v = qkv[:, 2 * part + h * dim : 2 * part + (h + 1) * dim]
            q = qkv[at, at_h] * scale
            do = dctx[at, at_h]
            s = jnp.where(keep > 0, mm_nt(q, k), MASKED_SCORE)
            p = jnp.exp(s - lse[at, h : h + 1])
            dp = mm_nt(do, v)
            ds = (p * (dp - jnp.sum(dp * p, axis=-1, keepdims=True))).astype(BF)
            dqs.append((mm(ds, k) * scale).astype(BF))
            dv[h] += mm_tn(p.astype(BF), do)
            dk[h] += mm_tn(ds, q)
        mix[at, :part] = jnp.concatenate(dqs, axis=1)
        return carry

    lax.fori_loop(0, 4, attend, 0)
    for h in range(part // dim):
        mix[:, part + h * dim : part + (h + 1) * dim] = dk[h].astype(BF)
        mix[:, 2 * part + h * dim : 2 * part + (h + 1) * dim] = dv[h].astype(BF)
    gqkv[...] = mm_tn(hid[...], mix[...]).astype(BF)
    for r, ref in enumerate((m0, m1, m2, m3)):
        at = slice(r * toks, (r + 1) * toks)
        m = mix[at, :]
        ref[...] = m
        n = mm_nt(m, w[...])
        a = jnp.sum(n * nrm[at, :].astype(F32), axis=0, keepdims=True)
        b = jnp.sum(n, axis=0, keepdims=True)
        c = jnp.sum(m.astype(F32), axis=0, keepdims=True)
        sums = (a, b, c) if r == 0 else tuple(s + t for s, t in zip(sums, (a, b, c)))
    gain_sum, shift_sum, col_sum = sums
    slot = lax.broadcasted_iota(jnp.int32, (1, 4 * part), 1)
    own = (slot >= tile[0] * part) & (slot < (tile[0] + 1) * part)
    lone = jnp.where(tile[0] == 0, 1.0, 0.0).astype(F32)
    vecs[0:1, :] = gain_sum
    vecs[1:2, :] = shift_sum
    for i in range(3):
        piece = col_sum[:, i * part : (i + 1) * part]
        vecs[2 + i : 3 + i, :] = jnp.where(own, jnp.concatenate([piece] * 4, axis=1), 0.0)
    vecs[5:6, :] = bsum[...] * lone
    vecs[6:8, :] = vec2[...]
    vecs[8:9, :] = fb2[...] * lone


def input_kernel(tile, m0, m1, m2, m3, w, x, rgrad, gain, out, ms, xs):
    part = m0.shape[1] // 3
    for r, ref in enumerate((m0, m1, m2, m3)):
        ms[r] = ref[...]
    tiles = [ms[tile[0] ^ g] for g in range(4)]
    full = jnp.concatenate(
        [m[:, i * part : (i + 1) * part] for i in range(3) for m in tiles], axis=1
    )
    n = mm_nt(full, w[...])
    load_tile(x, xs, 0)
    normed, inv = norm_stats(xs[...].astype(F32))
    store_tile(out, (rgrad[...] + norm_back(n, normed, inv, vec_row(gain))).astype(BF))


def ffout_kernel(tile, a0, a1, a2, a3, b0, b1, b2, b3, fc1, fc2, ps):
    quarter = fc2.shape[0] // 4
    for r, ref in enumerate((a0, a1, a2, a3)):
        ps[r] = ref[...].astype(F32)
    for g in range(4):
        piece = ps[tile[0] ^ g]
        for i in range(fc1.shape[1] // (4 * quarter)):
            dst = (4 * i + g) * quarter
            fc1[:, dst : dst + quarter] = piece[:, i * quarter : (i + 1) * quarter]
    for r, ref in enumerate((b0, b1, b2, b3)):
        ps[r, :quarter, :] = ref[...].astype(F32)
    for g in range(4):
        fc2[g * quarter : (g + 1) * quarter, :] = ps[tile[0] ^ g][:quarter]


def attnout_kernel(tile, p0, p1, p2, p3, gqkv, gout, vecs, units, ps):
    rows, width = gout.shape
    part = width // 4
    quarter = units.shape[1] // 4
    height = ps.shape[1] - rows
    for r, ref in enumerate((p0, p1, p2, p3)):
        ps[r] = ref[...].astype(F32)
    total = None
    tails = []
    for g in range(4):
        piece = ps[tile[0] ^ g]
        for i in range(3):
            dst = i * width + g * part
            gqkv[:, dst : dst + part] = piece[:rows, i * part : (i + 1) * part]
        gout[:, g * part : (g + 1) * part] = piece[:rows, 3 * part :]
        tail = jnp.concatenate([piece[rows + j : rows + j + 1] for j in range(height)], axis=1)
        total = tail if g == 0 else total + tail
        tails.append(tail[:, 9 * rows : 9 * rows + quarter])
    for i in range(9):
        vecs[i : i + 1, :] = total[:, i * rows : (i + 1) * rows]
    units[...] = jnp.concatenate(tails, axis=1)


def body(
    patches,
    patch_mask,
    norm1_gain,
    norm1_shift,
    qkv_weight,
    qv_bias,
    out_weight,
    out_bias,
    norm2_gain,
    norm2_shift,
    fc1_weight,
    fc1_bias,
    fc2_weight,
    fc2_bias,
    cotangent,
):
    _, rows, cols, width = patches.shape
    ff = fc1_weight.shape[1]
    imgs = lax.axis_size("imgs")
    part = width // 4
    units = ff // 4
    quarter = units // imgs
    share = width // imgs
    toks = rows * PAD
    total = 4 * toks
    tile = lax.axis_index("rows") * 2 + lax.axis_index("cols")
    at_tile = tile.reshape(1).astype(jnp.int32)

    def row(v):
        return v.reshape(1, -1)

    steps = 4
    w_own, b_own = pl.pallas_call(
        heads_kernel,
        grid=(steps,),
        in_specs=[
            SMEM,
            pl.BlockSpec((width // steps, 3 * width), lambda i: (i, 0)),
            pl.BlockSpec((2, width), lambda i: (0, 0)),
        ],
        out_specs=[
            pl.BlockSpec((width // steps, 3 * part), lambda i: (i, 0)),
            pl.BlockSpec((1, 3 * part), lambda i: (0, 0)),
        ],
        out_shape=[sds((width, 3 * part)), sds((1, 3 * part), F32)],
        cost_estimate=cost(4),
        name="heads",
    )(at_tile, qkv_weight, qv_bias.T)
    x_blocks, (w_own, b_own) = gather_tiles(patches, (w_own, b_own))

    hid1, nrm1, qkv, lse, *ctx = vec_call(
        attn_kernel,
        [
            sds((total, width)),
            sds((total, width)),
            sds((total, 3 * part)),
            sds((total, 128), F32),
        ]
        + [sds((toks, part))] * 4,
        9,
        [pltpu.VMEM((total, width), BF), pltpu.VMEM((4, toks, part), BF)],
        us=13,
    )(at_tile, patch_mask, *x_blocks, norm1_gain, norm1_shift, w_own, b_own)
    ct_blocks, ctx = gather_tiles(cotangent, ctx)
    later_tile, _ = tie(at_tile, ctx)

    fc1_own, fc1_b_own = pl.pallas_call(
        functools.partial(units_kernel, quarter=quarter),
        grid=(steps,),
        in_specs=[
            SMEM,
            pl.BlockSpec((width // steps, ff), lambda i: (i, 0)),
            pl.BlockSpec((1, ff), lambda i: (0, 0)),
        ],
        out_specs=[
            pl.BlockSpec((width // steps, units), lambda i: (i, 0)),
            pl.BlockSpec((1, units), lambda i: (0, 0)),
        ],
        out_shape=[sds((width, units)), sds((1, units), F32)],
        cost_estimate=cost(4),
        name="units",
    )(later_tile, fc1_weight, row(fc1_bias))
    fc2_own = lax.dynamic_index_in_dim(
        fc2_weight.reshape(imgs, 4, quarter, width), tile, 1, keepdims=False
    ).reshape(units, width)

    ctx_in = scatter_tiles(ctx)
    ctx_in, (fc1_own, fc1_b_own, fc2_own) = tie(ctx_in, (fc1_own, fc1_b_own, fc2_own))
    resid, hid2 = vec_call(
        branch_kernel,
        [sds((toks, width), F32), sds((toks, width))],
        9,
        [pltpu.VMEM((toks, width), BF)],
        us=3,
    )(at_tile, *ctx_in, out_weight, out_bias, patches, norm2_gain, norm2_shift)

    chunks = 4
    step = ff // chunks

    def whole(*shape):
        return pl.BlockSpec(shape, lambda i: (0,) * len(shape))

    layer_out, branch, rgrad, vec2 = pl.pallas_call(
        mlp_kernel,
        grid=(chunks,),
        in_specs=[
            SMEM,
            whole(*patch_mask.shape),
            whole(toks, width),
            whole(toks, width),
            whole(1, rows, cols, width),
            whole(width),
            pl.BlockSpec((width, step), lambda i: (0, i)),
            pl.BlockSpec((1, step), lambda i: (0, i)),
            pl.BlockSpec((step, width), lambda i: (i, 0)),
            whole(width),
        ],
        out_specs=[
            whole(1, rows, cols, width),
            whole(toks, width),
            whole(toks, width),
            whole(2, width),
        ],
        out_shape=[
            sds((1, rows, cols, width)),
            sds((toks, width)),
            sds((toks, width), F32),
            sds((2, width), F32),
        ],
        scratch_shapes=[
            pltpu.VMEM((toks, width), BF),
            pltpu.VMEM((toks, width), F32),
            pltpu.VMEM((toks, width), F32),
        ],
        cost_estimate=cost(11),
        name="mlp",
    )(
        at_tile,
        patch_mask,
        resid,
        hid2,
        cotangent,
        norm2_gain,
        fc1_weight,
        row(fc1_bias),
        fc2_weight,
        fc2_bias,
    )
    hid2_blocks, (branch,) = gather_tiles(hid2, (branch,))

    g1, g2, fb1, fb2 = vec_call(
        ffgrad_kernel,
        [sds((width, units)), sds((units, width)), sds((1, units), F32), sds((1, width), F32)],
        12,
        [
            pltpu.VMEM((toks, width), BF),
            pltpu.VMEM((width, units), F32),
            pltpu.VMEM((units, width), F32),
        ],
        us=9,
    )(at_tile, patch_mask, *hid2_blocks, *ct_blocks, fc1_own, fc1_b_own, fc2_own)
    branch_blocks, (g1, g2) = gather_tiles(branch, (g1, g2))

    dctx, gout, bsum = vec_call(
        outgrad_kernel,
        [sds((total, part)), sds((part, width)), sds((1, width), F32)],
        9,
        us=4,
    )(at_tile, *branch_blocks, out_weight, *ctx)
    direct = direct_sum(imgs)
    g1 = g1.reshape(imgs, share, units)
    g2 = g2.reshape(imgs, quarter, width)
    if direct:
        line = imgs // 2
        near1 = exchange_near(g1.reshape(line, 2, share, units))
        far2 = exchange_far(g2.reshape(line, 2, quarter, width))
    out_cols = [lax.dynamic_slice_in_dim(gout, (tile ^ r) * part, part, 1) for r in range(4)]
    dctx, out_rows = tie(dctx, scatter_tiles(out_cols))
    out_rows = jnp.concatenate(own_order(out_rows, tile), axis=0)

    *mixed, gqkv, vecs = vec_call(
        functools.partial(attnback_kernel, cols=cols),
        [sds((toks, 3 * part))] * 4 + [sds((width, 3 * part)), sds((9, width), F32)],
        10,
        [
            pltpu.VMEM((part * HEADS // width, total, width // HEADS), F32),
            pltpu.VMEM((part * HEADS // width, total, width // HEADS), F32),
            pltpu.VMEM((total, 3 * part), BF),
        ],
        us=18,
    )(at_tile, patch_mask, dctx, qkv, lse, hid1, nrm1, w_own, bsum, vec2, fb2)
    mixed_in = scatter_tiles(mixed)

    vecs = vecs.reshape(9, imgs, share).transpose(1, 0, 2).reshape(imgs, 9 * share)
    count = 9 * share + quarter
    vec_height = -(-count // width)
    spare = jnp.zeros((imgs, vec_height * width - count), F32)
    vecs = jnp.concatenate([vecs, fb1.reshape(imgs, quarter), spare], axis=1).astype(BF)
    at_bucket = jnp.concatenate(
        [
            jnp.concatenate([gqkv, out_rows], axis=1).reshape(imgs, share, width),
            vecs.reshape(imgs, vec_height, width),
        ],
        axis=1,
    )
    if direct:
        near3 = exchange_near(at_bucket.reshape(line, 2, share + vec_height, width))
        (near1, far2), (at_bucket,) = tie((near1, far2), (at_bucket,))
        far1 = exchange_far(total_of(near1).astype(BF))
        near2 = exchange_near(total_of(far2).astype(BF)[None])
        near3, (far1[0],) = tie(near3, (far1[0],))
        far3 = exchange_far(total_of(near3).astype(BF))

    patches_grad = vec_call(
        input_kernel,
        sds((1, rows, cols, width)),
        8,
        [pltpu.VMEM((4, toks, 3 * part), BF), pltpu.VMEM((toks, width), BF)],
        us=5,
    )(at_tile, *mixed_in, qkv_weight, patches, rgrad, norm1_gain)

    if direct:
        fc2_sum = total_of(near2)[0].astype(BF)
        fc1_sum = total_of(far1).astype(BF)
        far3, (fc1_sum, fc2_sum, patches_grad) = tie(far3, (fc1_sum, fc2_sum, patches_grad))
        at_sum = total_of(far3).astype(BF)
    else:
        fc1_sum, fc2_sum, at_sum = (plain_sum(b) for b in (g1, g2, at_bucket))
    fc1_pieces, _ = gather_tiles(fc1_sum)
    fc2_pieces, _ = gather_tiles(fc2_sum)
    fc1_grad, fc2_grad = vec_call(
        ffout_kernel,
        [sds((share, ff), F32), sds((4 * quarter, width), F32)],
        8,
        [pltpu.VMEM((4, max(share, quarter), width), F32)],
        us=3,
    )(at_tile, *fc1_pieces, *fc2_pieces)
    at_pieces, (fc1_grad, fc2_grad) = gather_tiles(at_sum, (fc1_grad, fc2_grad))
    qkv_grad, out_grad, vec_sum, unit_sum = vec_call(
        attnout_kernel,
        [
            sds((share, 3 * width), F32),
            sds((share, width), F32),
            sds((9, share), F32),
            sds((1, 4 * quarter), F32),
        ],
        4,
        [pltpu.VMEM((4, share + vec_height, width), F32)],
        us=3,
    )(at_tile, *at_pieces)
    return (
        layer_out,
        patches_grad,
        vec_sum[0],
        vec_sum[1],
        qkv_grad,
        jnp.stack([vec_sum[2], vec_sum[4]], axis=1),
        out_grad,
        vec_sum[5],
        vec_sum[6],
        vec_sum[7],
        fc1_grad,
        unit_sum.reshape(-1),
        fc2_grad,
        vec_sum[8],
    )


def solution(mesh):
    tiled = P("imgs", "rows", "cols", None)
    in_specs = (tiled, P("imgs", None, None)) + (P(),) * 12 + (tiled,)
    mat = P("imgs", None)
    vec = P("imgs")
    out_specs = (tiled, tiled, vec, vec, mat, mat, mat, vec, vec, vec, mat, vec, mat, vec)
    return jax.shard_map(body, mesh=mesh, in_specs=in_specs, out_specs=out_specs, check_vma=False)
```

```python
import functools

import jax
import jax.numpy as jnp
from jax import lax
from jax.experimental import pallas as pl
from jax.experimental.pallas import tpu as pltpu
from jax.sharding import PartitionSpec as P

HEADS = 12
NORM_EPS = 1e-06
MASKED_SCORE = -1e30
GROUP = ("rows", "cols")
BF = jnp.bfloat16
F32 = jnp.float32


def dot(left, right, dims):
    return lax.dot_general(left, right, (dims, ((), ())), preferred_element_type=F32)


def mm(left, right):
    return dot(left, right, ((1,), (0,)))


def mm_nt(left, right):
    return dot(left, right, ((1,), (1,)))


def mm_tn(left, right):
    return dot(left, right, ((0,), (0,)))


def to_peer(value, rel):
    if rel == 1:
        return lax.ppermute(value, "cols", [(0, 1), (1, 0)])
    if rel == 2:
        return lax.ppermute(value, "rows", [(0, 1), (1, 0)])
    return lax.ppermute(value, GROUP, [(i, i ^ 3) for i in range(4)])


def tie(values, others):
    flat, tree = jax.tree.flatten((values, others))
    return jax.tree.unflatten(tree, lax.optimization_barrier(flat))


def gather_tiles(value, others=()):
    across = to_peer(value, 2)
    beside = to_peer(value, 1)
    across, others = tie(across, others)
    return [value, beside, across, to_peer(across, 1)], others


def scatter_tiles(blocks):
    return [blocks[0], to_peer(blocks[1], 1), to_peer(blocks[2], 2), to_peer(blocks[3], 3)]


def norm_stats(values):
    mean_val = jnp.mean(values, axis=-1, keepdims=True)
    centred = values - mean_val
    var_val = jnp.mean(centred * centred, axis=-1, keepdims=True)
    inv = lax.rsqrt(var_val + NORM_EPS)
    return centred * inv, inv


def norm_back(grads, normed, inv, gain):
    g = grads * gain
    return (
        g
        - jnp.mean(g, axis=-1, keepdims=True)
        - normed * jnp.mean(g * normed, axis=-1, keepdims=True)
    ) * inv


def gelu_parts(x):
    cdf = 0.5 * (1.0 + lax.erf(x * 0.7071067811865476))
    pdf = jnp.exp(-0.5 * x * x) * 0.3989422804014327
    return x * cdf, cdf + x * pdf


def exchange_near(parts):
    side = lax.axis_index("imgs") % 2
    count = lax.axis_size("imgs")
    send = lax.dynamic_index_in_dim(parts, 1 - side, 1, keepdims=False)
    keep = lax.dynamic_index_in_dim(parts, side, 1, keepdims=False)
    return keep, lax.ppermute(send, "imgs", [(i, i ^ 1) for i in range(count)])


def exchange_far(parts):
    count = lax.axis_size("imgs")
    place = lax.axis_index("imgs") // 2
    got = [lax.dynamic_index_in_dim(parts, place, 0, keepdims=False)]
    for k in range(count // 2 - 1, 0, -1):
        send = lax.dynamic_index_in_dim(parts, place ^ k, 0, keepdims=False)
        got.append(lax.ppermute(send, "imgs", [(i, i ^ (2 * k)) for i in range(count)]))
    return got


def total_of(blocks):
    return functools.reduce(jnp.add, [b.astype(F32) for b in blocks])


def direct_sum(imgs):
    return imgs <= 8 and imgs & (imgs - 1) == 0


def plain_sum(parts):
    return lax.psum_scatter(parts, "imgs", scatter_dimension=0, tiled=False)


def own_order(blocks, tile):
    stacked = jnp.stack(blocks)
    return [lax.dynamic_index_in_dim(stacked, tile ^ k, 0, keepdims=False) for k in range(4)]


SMEM = pl.BlockSpec(memory_space=pltpu.SMEM)
VMEM = pl.BlockSpec(memory_space=pltpu.VMEM)
PAD = 16


def vec_call(kernel, outs, n_in, scratch=(), us=5):
    return pl.pallas_call(
        kernel,
        out_shape=outs,
        in_specs=[SMEM] + [VMEM] * n_in,
        out_specs=jax.tree.map(lambda _: VMEM, outs),
        scratch_shapes=list(scratch),
        cost_estimate=cost(us),
    )


def cost(us):
    return pl.CostEstimate(flops=us * 10**9, transcendentals=0, bytes_accessed=us * 10**6)


def sds(shape, dtype=BF):
    return jax.ShapeDtypeStruct(shape, dtype)


def load_tile(ref, scratch, at):
    rows, cols, width = ref.shape[1:]
    scratch[at : at + rows * PAD, :] = jnp.zeros((rows * PAD, width), scratch.dtype)
    for i in range(rows):
        scratch[at + i * PAD : at + i * PAD + cols, :] = ref[0, i]


def store_tile(ref, value):
    rows, cols, _ = ref.shape[1:]
    for i in range(rows):
        ref[0, i] = value[i * PAD : i * PAD + cols, :]


def mask_edges(mask):
    m = mask[0].astype(F32)
    high = jnp.sum(m[:, 0:1], axis=0, keepdims=True)
    wide = jnp.sum(m[0:1, :], axis=1, keepdims=True)
    return high, wide


def keep_tokens(edges, place, rows, cols, axis):
    toks = rows * PAD
    shape = (toks, 1) if axis == 0 else (1, toks)
    tok = lax.broadcasted_iota(jnp.int32, shape, axis)
    c = tok & (PAD - 1)
    r = ((tok >> 4) + (place >> 1) * rows).astype(F32)
    at = (c + (place & 1) * cols).astype(F32)
    ok = (c < cols) & (r < edges[0]) & (at < edges[1])
    return jnp.where(ok, 1.0, 0.0).astype(F32)


def vec_row(ref):
    return ref[...].reshape(1, -1)


def heads_kernel(tile, qkv_w, qv_b, w_own, b_own):
    width = qv_b.shape[1]
    part = width // 4
    for g in range(4):

        @pl.when(tile[0] == g)
        def _():
            for i in range(3):
                src = i * width + g * part
                w_own[:, i * part : (i + 1) * part] = qkv_w[:, src : src + part]
            b_own[:, :part] = qv_b[0:1, g * part : (g + 1) * part]
            b_own[:, part : 2 * part] = jnp.zeros((1, part), F32)
            b_own[:, 2 * part :] = qv_b[1:2, g * part : (g + 1) * part]


def units_kernel(tile, fc1, fc1_b, fc1_own, fc1_b_own, *, quarter):
    for g in range(4):

        @pl.when(tile[0] == g)
        def _():
            for i in range(fc1.shape[1] // (4 * quarter)):
                src = (4 * i + g) * quarter
                dst = i * quarter
                fc1_own[:, dst : dst + quarter] = fc1[:, src : src + quarter]
                fc1_b_own[:, dst : dst + quarter] = fc1_b[:, src : src + quarter]


def attn_kernel(
    tile, mask, x0, x1, x2, x3, gain, shift, w, bias, hid, nrm, qkv, lse, c0, c1, c2, c3, xs, ctx
):
    rows, cols, width = x0.shape[1:]
    toks = rows * PAD
    part = w.shape[1] // 3
    dim = width // HEADS
    scale = dim ** (-0.5)
    for r, ref in enumerate((x0, x1, x2, x3)):
        load_tile(ref, xs, r * toks)

    def project(r, carry):
        at = pl.ds(pl.multiple_of(r * toks, toks), toks)
        normed, _ = norm_stats(xs[at, :].astype(F32))
        h = (normed * vec_row(gain) + vec_row(shift)).astype(BF)
        hid[at, :] = h
        nrm[at, :] = normed.astype(BF)
        qkv[at, :] = (mm(h, w[...]) + bias[...]).astype(BF)
        return carry

    lax.fori_loop(0, 4, project, 0)
    edges = mask_edges(mask)
    keep = jnp.concatenate(
        [keep_tokens(edges, tile[0] ^ r, rows, cols, 1) for r in range(4)], axis=1
    )

    def attend(r, carry):
        at = pl.ds(pl.multiple_of(r * toks, toks), toks)
        outs = []
        for h in range(part // dim):
            q = qkv[at, h * dim : (h + 1) * dim]
            k = qkv[:, part + h * dim : part + (h + 1) * dim]
            v = qkv[:, 2 * part + h * dim : 2 * part + (h + 1) * dim]
            s = jnp.where(keep > 0, mm_nt(q * scale, k), MASKED_SCORE)
            top = jnp.max(s, axis=-1, keepdims=True)
            e = jnp.exp(s - top)
            total = jnp.sum(e, axis=-1, keepdims=True)
            outs.append(mm((e * (1.0 / total)).astype(BF), v).astype(BF))
            lse[at, h : h + 1] = top + jnp.log(total)
        ctx[r] = jnp.concatenate(outs, axis=1)
        return carry

    lax.fori_loop(0, 4, attend, 0)
    for r, ref in enumerate((c0, c1, c2, c3)):
        ref[...] = ctx[r]


def branch_kernel(tile, c0, c1, c2, c3, wo, bo, x, gain, shift, resid, hid, xs):
    part = c0.shape[1]
    load_tile(x, xs, 0)
    acc = xs[...].astype(F32) + vec_row(bo)
    for r, ref in enumerate((c0, c1, c2, c3)):
        at = pl.multiple_of((tile[0] ^ r) * part, part)
        acc = acc + mm(ref[...], wo[pl.ds(at, part), :])
    resid[...] = acc
    normed, _ = norm_stats(acc)
    hid[...] = (normed * vec_row(gain) + vec_row(shift)).astype(BF)


def mlp_kernel(
    tile, mask, resid, hid, ct, gain, fc1, fc1_b, fc2, fc2_b, out, branch, rgrad, vecs, up, acc, nacc
):
    step = pl.program_id(0)
    rows, cols, _ = ct.shape[1:]

    @pl.when(step == 0)
    def _():
        load_tile(ct, up, 0)
        up[...] = (up[...].astype(F32) * keep_tokens(mask_edges(mask), tile[0], rows, cols, 0)).astype(BF)
        acc[...] = jnp.zeros_like(acc)
        nacc[...] = jnp.zeros_like(nacc)

    act, dgelu = gelu_parts(mm(hid[...], fc1[...]) + fc1_b[...])
    acc[...] += mm(act.astype(BF), fc2[...])
    inner = (mm_nt(up[...], fc2[...]) * dgelu).astype(BF)
    nacc[...] += mm_nt(inner, fc1[...])

    @pl.when(step == pl.num_programs(0) - 1)
    def _():
        res = resid[...]
        keep = keep_tokens(mask_edges(mask), tile[0], rows, cols, 0)
        store_tile(out, (keep * (res + acc[...] + vec_row(fc2_b))).astype(BF))
        normed, inv = norm_stats(res)
        n = nacc[...]
        vecs[0:1, :] = jnp.sum(n * normed, axis=0, keepdims=True)
        vecs[1:2, :] = jnp.sum(n, axis=0, keepdims=True)
        grad = up[...].astype(F32) + norm_back(n, normed, inv, vec_row(gain))
        rgrad[...] = grad
        branch[...] = grad.astype(BF)


def ffgrad_kernel(
    tile, mask, h0, h1, h2, h3, t0, t1, t2, t3, fc1, fc1_b, fc2, g1, g2, b1, b2, up, a1, a2
):
    rows, cols, _ = t0.shape[1:]
    edges = mask_edges(mask)
    hids = (h0, h1, h2, h3)
    for r, ref in enumerate((t0, t1, t2, t3)):
        load_tile(ref, up, 0)
        wide = up[...].astype(F32) * keep_tokens(edges, tile[0] ^ r, rows, cols, 0)
        low = wide.astype(BF)
        h = hids[r][...]
        act, dgelu = gelu_parts(mm(h, fc1[...]) + fc1_b[...])
        inner = (mm_nt(low, fc2[...]) * dgelu).astype(BF)
        d1 = mm_tn(h, inner)
        d2 = mm_tn(act.astype(BF), low)
        s1 = jnp.sum(inner.astype(F32), axis=0, keepdims=True)
        s2 = jnp.sum(wide, axis=0, keepdims=True)
        if r == 0:
            a1[...], a2[...], b1[...], b2[...] = d1, d2, s1, s2
        elif r < 3:
            a1[...] += d1
            a2[...] += d2
            b1[...] += s1
            b2[...] += s2
        else:
            g1[...] = (a1[...] + d1).astype(BF)
            g2[...] = (a2[...] + d2).astype(BF)
            b1[...] += s1
            b2[...] += s2


def outgrad_kernel(tile, b0, b1, b2, b3, wo, c0, c1, c2, c3, dctx, gout, bsum):
    toks, part = c0.shape
    at = pl.multiple_of(tile[0] * part, part)
    w = wo[pl.ds(at, part), :]
    ctx = (c0, c1, c2, c3)
    acc = None
    total = None
    for r, ref in enumerate((b0, b1, b2, b3)):
        low = ref[...]
        dctx[r * toks : (r + 1) * toks, :] = mm_nt(low, w).astype(BF)
        d = mm_tn(ctx[r][...], low)
        s = jnp.sum(low.astype(F32), axis=0, keepdims=True)
        acc = d if r == 0 else acc + d
        total = s if r == 0 else total + s
    gout[...] = acc.astype(BF)
    bsum[...] = total


def attnback_kernel(
    tile,
    mask,
    dctx,
    qkv,
    lse,
    hid,
    nrm,
    w,
    bsum,
    vec2,
    fb2,
    m0,
    m1,
    m2,
    m3,
    gqkv,
    vecs,
    dk,
    dv,
    mix,
    *,
    cols,
):
    total, three = qkv.shape
    part = three // 3
    toks = total // 4
    dim = hid.shape[1] // HEADS
    rows = toks // PAD
    scale = dim ** (-0.5)
    edges = mask_edges(mask)
    keep = jnp.concatenate(
        [keep_tokens(edges, tile[0] ^ r, rows, cols, 1) for r in range(4)], axis=1
    )
    dk[...] = jnp.zeros_like(dk)
    dv[...] = jnp.zeros_like(dv)

    def attend(r, carry):
        at = pl.ds(pl.multiple_of(r * toks, toks), toks)
        dqs = []
        for h in range(part // dim):
            at_h = slice(h * dim, (h + 1) * dim)
            k = qkv[:, part + h * dim : part + (h + 1) * dim]
            v = qkv[:, 2 * part + h * dim : 2 * part + (h + 1) * dim]
            q = qkv[at, at_h] * scale
            do = dctx[at, at_h]
            s = jnp.where(keep > 0, mm_nt(q, k), MASKED_SCORE)
            p = jnp.exp(s - lse[at, h : h + 1])
            dp = mm_nt(do, v)
            ds = (p * (dp - jnp.sum(dp * p, axis=-1, keepdims=True))).astype(BF)
            dqs.append((mm(ds, k) * scale).astype(BF))
            dv[h] += mm_tn(p.astype(BF), do)
            dk[h] += mm_tn(ds, q)
        mix[at, :part] = jnp.concatenate(dqs, axis=1)
        return carry

    lax.fori_loop(0, 4, attend, 0)
    for h in range(part // dim):
        mix[:, part + h * dim : part + (h + 1) * dim] = dk[h].astype(BF)
        mix[:, 2 * part + h * dim : 2 * part + (h + 1) * dim] = dv[h].astype(BF)
    gqkv[...] = mm_tn(hid[...], mix[...]).astype(BF)
    for r, ref in enumerate((m0, m1, m2, m3)):
        at = slice(r * toks, (r + 1) * toks)
        m = mix[at, :]
        ref[...] = m
        n = mm_nt(m, w[...])
        a = jnp.sum(n * nrm[at, :].astype(F32), axis=0, keepdims=True)
        b = jnp.sum(n, axis=0, keepdims=True)
        c = jnp.sum(m.astype(F32), axis=0, keepdims=True)
        sums = (a, b, c) if r == 0 else tuple(s + t for s, t in zip(sums, (a, b, c)))
    gain_sum, shift_sum, col_sum = sums
    slot = lax.broadcasted_iota(jnp.int32, (1, 4 * part), 1)
    own = (slot >= tile[0] * part) & (slot < (tile[0] + 1) * part)
    lone = jnp.where(tile[0] == 0, 1.0, 0.0).astype(F32)
    vecs[0:1, :] = gain_sum
    vecs[1:2, :] = shift_sum
    for i in range(3):
        piece = col_sum[:, i * part : (i + 1) * part]
        vecs[2 + i : 3 + i, :] = jnp.where(own, jnp.concatenate([piece] * 4, axis=1), 0.0)
    vecs[5:6, :] = bsum[...] * lone
    vecs[6:8, :] = vec2[...]
    vecs[8:9, :] = fb2[...] * lone


def input_kernel(tile, m0, m1, m2, m3, w, x, rgrad, gain, out, ms, xs):
    part = m0.shape[1] // 3
    for r, ref in enumerate((m0, m1, m2, m3)):
        ms[r] = ref[...]
    tiles = [ms[tile[0] ^ g] for g in range(4)]
    full = jnp.concatenate(
        [m[:, i * part : (i + 1) * part] for i in range(3) for m in tiles], axis=1
    )
    n = mm_nt(full, w[...])
    load_tile(x, xs, 0)
    normed, inv = norm_stats(xs[...].astype(F32))
    store_tile(out, (rgrad[...] + norm_back(n, normed, inv, vec_row(gain))).astype(BF))


def ffout_kernel(tile, a0, a1, a2, a3, b0, b1, b2, b3, fc1, fc2, ps):
    quarter = fc2.shape[0] // 4
    for r, ref in enumerate((a0, a1, a2, a3)):
        ps[r] = ref[...].astype(F32)
    for g in range(4):
        piece = ps[tile[0] ^ g]
        for i in range(fc1.shape[1] // (4 * quarter)):
            dst = (4 * i + g) * quarter
            fc1[:, dst : dst + quarter] = piece[:, i * quarter : (i + 1) * quarter]
    for r, ref in enumerate((b0, b1, b2, b3)):
        ps[r, :quarter, :] = ref[...].astype(F32)
    for g in range(4):
        fc2[g * quarter : (g + 1) * quarter, :] = ps[tile[0] ^ g][:quarter]


def attnout_kernel(
    tile, p0, p1, p2, p3, gqkv, gout, v0, v1, v5, v6, v7, v8, qv, units, ps
):
    rows, width = gout.shape
    part = width // 4
    quarter = units.shape[0] // 4
    height = ps.shape[1] - rows
    for r, ref in enumerate((p0, p1, p2, p3)):
        ps[r] = ref[...].astype(F32)
    total = None
    tails = []
    for g in range(4):
        piece = ps[tile[0] ^ g]
        for i in range(3):
            dst = i * width + g * part
            gqkv[:, dst : dst + part] = piece[:rows, i * part : (i + 1) * part]
        gout[:, g * part : (g + 1) * part] = piece[:rows, 3 * part :]
        tail = jnp.concatenate([piece[rows + j : rows + j + 1] for j in range(height)], axis=1)
        total = tail if g == 0 else total + tail
        tails.append(tail[:, 9 * rows : 9 * rows + quarter])
    for i, ref in ((0, v0), (1, v1), (5, v5), (6, v6), (7, v7), (8, v8)):
        ref[...] = total[0, i * rows : (i + 1) * rows]
    both = [total[:, i * rows : (i + 1) * rows] for i in (2, 4)]
    qv[...] = jnp.concatenate(both, axis=0).T
    units[...] = jnp.concatenate(tails, axis=1)[0]


def body(
    patches,
    patch_mask,
    norm1_gain,
    norm1_shift,
    qkv_weight,
    qv_bias,
    out_weight,
    out_bias,
    norm2_gain,
    norm2_shift,
    fc1_weight,
    fc1_bias,
    fc2_weight,
    fc2_bias,
    cotangent,
):
    _, rows, cols, width = patches.shape
    ff = fc1_weight.shape[1]
    imgs = lax.axis_size("imgs")
    part = width // 4
    units = ff // 4
    quarter = units // imgs
    share = width // imgs
    toks = rows * PAD
    total = 4 * toks
    tile = lax.axis_index("rows") * 2 + lax.axis_index("cols")
    at_tile = tile.reshape(1).astype(jnp.int32)

    def row(v):
        return v.reshape(1, -1)

    steps = 4
    w_own, b_own = pl.pallas_call(
        heads_kernel,
        grid=(steps,),
        in_specs=[
            SMEM,
            pl.BlockSpec((width // steps, 3 * width), lambda i: (i, 0)),
            pl.BlockSpec((2, width), lambda i: (0, 0)),
        ],
        out_specs=[
            pl.BlockSpec((width // steps, 3 * part), lambda i: (i, 0)),
            pl.BlockSpec((1, 3 * part), lambda i: (0, 0)),
        ],
        out_shape=[sds((width, 3 * part)), sds((1, 3 * part), F32)],
        cost_estimate=cost(4),
        name="heads",
    )(at_tile, qkv_weight, qv_bias.T)
    x_blocks, (w_own, b_own) = gather_tiles(patches, (w_own, b_own))

    hid1, nrm1, qkv, lse, *ctx = vec_call(
        attn_kernel,
        [
            sds((total, width)),
            sds((total, width)),
            sds((total, 3 * part)),
            sds((total, 128), F32),
        ]
        + [sds((toks, part))] * 4,
        9,
        [pltpu.VMEM((total, width), BF), pltpu.VMEM((4, toks, part), BF)],
        us=13,
    )(at_tile, patch_mask, *x_blocks, norm1_gain, norm1_shift, w_own, b_own)
    ct_blocks, ctx = gather_tiles(cotangent, ctx)
    later_tile, _ = tie(at_tile, ctx)

    fc1_own, fc1_b_own = pl.pallas_call(
        functools.partial(units_kernel, quarter=quarter),
        grid=(steps,),
        in_specs=[
            SMEM,
            pl.BlockSpec((width // steps, ff), lambda i: (i, 0)),
            pl.BlockSpec((1, ff), lambda i: (0, 0)),
        ],
        out_specs=[
            pl.BlockSpec((width // steps, units), lambda i: (i, 0)),
            pl.BlockSpec((1, units), lambda i: (0, 0)),
        ],
        out_shape=[sds((width, units)), sds((1, units), F32)],
        cost_estimate=cost(4),
        name="units",
    )(later_tile, fc1_weight, row(fc1_bias))
    fc2_own = lax.dynamic_index_in_dim(
        fc2_weight.reshape(imgs, 4, quarter, width), later_tile[0], 1, keepdims=False
    ).reshape(units, width)

    ctx_in = scatter_tiles(ctx)
    ctx_in, (fc1_own, fc1_b_own, fc2_own) = tie(ctx_in, (fc1_own, fc1_b_own, fc2_own))
    resid, hid2 = vec_call(
        branch_kernel,
        [sds((toks, width), F32), sds((toks, width))],
        9,
        [pltpu.VMEM((toks, width), BF)],
        us=3,
    )(at_tile, *ctx_in, out_weight, out_bias, patches, norm2_gain, norm2_shift)

    chunks = 4
    step = ff // chunks

    def whole(*shape):
        return pl.BlockSpec(shape, lambda i: (0,) * len(shape))

    layer_out, branch, rgrad, vec2 = pl.pallas_call(
        mlp_kernel,
        grid=(chunks,),
        in_specs=[
            SMEM,
            whole(*patch_mask.shape),
            whole(toks, width),
            whole(toks, width),
            whole(1, rows, cols, width),
            whole(width),
            pl.BlockSpec((width, step), lambda i: (0, i)),
            pl.BlockSpec((1, step), lambda i: (0, i)),
            pl.BlockSpec((step, width), lambda i: (i, 0)),
            whole(width),
        ],
        out_specs=[
            whole(1, rows, cols, width),
            whole(toks, width),
            whole(toks, width),
            whole(2, width),
        ],
        out_shape=[
            sds((1, rows, cols, width)),
            sds((toks, width)),
            sds((toks, width), F32),
            sds((2, width), F32),
        ],
        scratch_shapes=[
            pltpu.VMEM((toks, width), BF),
            pltpu.VMEM((toks, width), F32),
            pltpu.VMEM((toks, width), F32),
        ],
        cost_estimate=cost(11),
        name="mlp",
    )(
        at_tile,
        patch_mask,
        resid,
        hid2,
        cotangent,
        norm2_gain,
        fc1_weight,
        row(fc1_bias),
        fc2_weight,
        fc2_bias,
    )
    hid2_blocks, (branch,) = gather_tiles(hid2, (branch,))

    g1, g2, fb1, fb2 = vec_call(
        ffgrad_kernel,
        [sds((width, units)), sds((units, width)), sds((1, units), F32), sds((1, width), F32)],
        12,
        [
            pltpu.VMEM((toks, width), BF),
            pltpu.VMEM((width, units), F32),
            pltpu.VMEM((units, width), F32),
        ],
        us=9,
    )(at_tile, patch_mask, *hid2_blocks, *ct_blocks, fc1_own, fc1_b_own, fc2_own)
    branch_blocks, (g1, g2) = gather_tiles(branch, (g1, g2))

    dctx, gout, bsum = vec_call(
        outgrad_kernel,
        [sds((total, part)), sds((part, width)), sds((1, width), F32)],
        9,
        us=4,
    )(at_tile, *branch_blocks, out_weight, *ctx)
    direct = direct_sum(imgs)
    (g1, g2), (gout,) = tie((g1, g2), (gout,))
    g1 = g1.reshape(imgs, share, units)
    g2 = g2.reshape(imgs, quarter, width)
    out_cols = [lax.dynamic_slice_in_dim(gout, (tile ^ r) * part, part, 1) for r in range(4)]
    out_rows = scatter_tiles(out_cols)
    if direct:
        line = imgs // 2
        (g1, g2), out_cols = tie((g1, g2), out_cols)
        near1 = exchange_near(g1.reshape(line, 2, share, units))
        far2 = exchange_far(g2.reshape(line, 2, quarter, width))
    dctx, out_rows = tie(dctx, out_rows)
    out_rows = jnp.concatenate(own_order(out_rows, tile), axis=0)

    *mixed, gqkv, vecs = vec_call(
        functools.partial(attnback_kernel, cols=cols),
        [sds((toks, 3 * part))] * 4 + [sds((width, 3 * part)), sds((9, width), F32)],
        10,
        [
            pltpu.VMEM((part * HEADS // width, total, width // HEADS), F32),
            pltpu.VMEM((part * HEADS // width, total, width // HEADS), F32),
            pltpu.VMEM((total, 3 * part), BF),
        ],
        us=18,
    )(at_tile, patch_mask, dctx, qkv, lse, hid1, nrm1, w_own, bsum, vec2, fb2)
    mixed_in = scatter_tiles(mixed)

    vecs = vecs.reshape(9, imgs, share).transpose(1, 0, 2).reshape(imgs, 9 * share)
    count = 9 * share + quarter
    vec_height = -(-count // width)
    spare = jnp.zeros((imgs, vec_height * width - count), F32)
    vecs = jnp.concatenate([vecs, fb1.reshape(imgs, quarter), spare], axis=1).astype(BF)
    at_bucket = jnp.concatenate(
        [
            jnp.concatenate([gqkv, out_rows], axis=1).reshape(imgs, share, width),
            vecs.reshape(imgs, vec_height, width),
        ],
        axis=1,
    )
    if direct:
        near3 = exchange_near(at_bucket.reshape(line, 2, share + vec_height, width))
        (near1, far2), (at_bucket,) = tie((near1, far2), (at_bucket,))
        far1 = exchange_far(total_of(near1).astype(BF))
        near2 = exchange_near(total_of(far2).astype(BF)[None])
        near3, (far1[0],) = tie(near3, (far1[0],))
        mid3 = total_of(near3).astype(BF)
        mixed_in[0], (mid3,) = tie(mixed_in[0], (mid3,))
        far3 = exchange_far(mid3)

    patches_grad = vec_call(
        input_kernel,
        sds((1, rows, cols, width)),
        8,
        [pltpu.VMEM((4, toks, 3 * part), BF), pltpu.VMEM((toks, width), BF)],
        us=5,
    )(at_tile, *mixed_in, qkv_weight, patches, rgrad, norm1_gain)

    if direct:
        fc2_sum = total_of(near2)[0].astype(BF)
        fc1_sum = total_of(far1).astype(BF)
    else:
        fc1_sum, fc2_sum, at_sum = (plain_sum(b) for b in (g1, g2, at_bucket))
    fc2_pieces, _ = gather_tiles(fc2_sum)
    fc1_pieces, _ = gather_tiles(fc1_sum)
    if direct:
        far3, (fc1_pieces[2], fc2_pieces[2], patches_grad) = tie(
            far3, (fc1_pieces[2], fc2_pieces[2], patches_grad)
        )
        at_sum = total_of(far3).astype(BF)
    fc1_grad, fc2_grad = vec_call(
        ffout_kernel,
        [sds((share, ff), F32), sds((4 * quarter, width), F32)],
        8,
        [pltpu.VMEM((4, max(share, quarter), width), F32)],
        us=3,
    )(at_tile, *fc1_pieces, *fc2_pieces)
    at_pieces, (fc1_grad, fc2_grad) = gather_tiles(at_sum, (fc1_grad, fc2_grad))
    qkv_grad, out_grad, *vec_sums, qv_sum, unit_sum = vec_call(
        attnout_kernel,
        [
            sds((share, 3 * width), F32),
            sds((share, width), F32),
            *[sds((share,), F32)] * 6,
            sds((share, 2), F32),
            sds((4 * quarter,), F32),
        ],
        4,
        [pltpu.VMEM((4, share + vec_height, width), F32)],
        us=3,
    )(at_tile, *at_pieces)
    return (
        layer_out,
        patches_grad,
        vec_sums[0],
        vec_sums[1],
        qkv_grad,
        qv_sum,
        out_grad,
        vec_sums[2],
        vec_sums[3],
        vec_sums[4],
        fc1_grad,
        unit_sum,
        fc2_grad,
        vec_sums[5],
    )


def solution(mesh):
    tiled = P("imgs", "rows", "cols", None)
    in_specs = (tiled, P("imgs", None, None)) + (P(),) * 12 + (tiled,)
    mat = P("imgs", None)
    vec = P("imgs")
    out_specs = (tiled, tiled, vec, vec, mat, mat, mat, vec, vec, vec, mat, vec, mat, vec)
    return jax.shard_map(body, mesh=mesh, in_specs=in_specs, out_specs=out_specs, check_vma=False)
```

```python
import functools

import jax
import jax.numpy as jnp
from jax import lax
from jax.experimental import pallas as pl
from jax.experimental.pallas import tpu as pltpu
from jax.sharding import PartitionSpec as P

HEADS = 12
NORM_EPS = 1e-06
MASKED_SCORE = -1e30
GROUP = ("rows", "cols")
BF = jnp.bfloat16
F32 = jnp.float32


def dot(left, right, dims):
    return lax.dot_general(left, right, (dims, ((), ())), preferred_element_type=F32)


def mm(left, right):
    return dot(left, right, ((1,), (0,)))


def mm_nt(left, right):
    return dot(left, right, ((1,), (1,)))


def mm_tn(left, right):
    return dot(left, right, ((0,), (0,)))


def to_peer(value, rel):
    if rel == 1:
        return lax.ppermute(value, "cols", [(0, 1), (1, 0)])
    if rel == 2:
        return lax.ppermute(value, "rows", [(0, 1), (1, 0)])
    return lax.ppermute(value, GROUP, [(i, i ^ 3) for i in range(4)])


def tie(values, others):
    flat, tree = jax.tree.flatten((values, others))
    return jax.tree.unflatten(tree, lax.optimization_barrier(flat))


def gather_tiles(value, others=()):
    across = to_peer(value, 2)
    beside = to_peer(value, 1)
    across, others = tie(across, others)
    return [value, beside, across, to_peer(across, 1)], others


def scatter_tiles(blocks):
    return [blocks[0], to_peer(blocks[1], 1), to_peer(blocks[2], 2), to_peer(blocks[3], 3)]


def norm_stats(values):
    mean_val = jnp.mean(values, axis=-1, keepdims=True)
    centred = values - mean_val
    var_val = jnp.mean(centred * centred, axis=-1, keepdims=True)
    inv = lax.rsqrt(var_val + NORM_EPS)
    return centred * inv, inv


def norm_back(grads, normed, inv, gain):
    g = grads * gain
    return (
        g
        - jnp.mean(g, axis=-1, keepdims=True)
        - normed * jnp.mean(g * normed, axis=-1, keepdims=True)
    ) * inv


def gelu_parts(x):
    cdf = 0.5 * (1.0 + lax.erf(x * 0.7071067811865476))
    pdf = jnp.exp(-0.5 * x * x) * 0.3989422804014327
    return x * cdf, cdf + x * pdf


def exchange_near(parts):
    side = lax.axis_index("imgs") % 2
    count = lax.axis_size("imgs")
    send = lax.dynamic_index_in_dim(parts, 1 - side, 1, keepdims=False)
    keep = lax.dynamic_index_in_dim(parts, side, 1, keepdims=False)
    return keep, lax.ppermute(send, "imgs", [(i, i ^ 1) for i in range(count)])


def exchange_far(parts):
    count = lax.axis_size("imgs")
    place = lax.axis_index("imgs") // 2
    got = [lax.dynamic_index_in_dim(parts, place, 0, keepdims=False)]
    for k in range(count // 2 - 1, 0, -1):
        send = lax.dynamic_index_in_dim(parts, place ^ k, 0, keepdims=False)
        got.append(lax.ppermute(send, "imgs", [(i, i ^ (2 * k)) for i in range(count)]))
    return got


def total_of(blocks):
    return functools.reduce(jnp.add, [b.astype(F32) for b in blocks])


def direct_sum(imgs):
    return imgs <= 8 and imgs & (imgs - 1) == 0


def plain_sum(parts):
    return lax.psum_scatter(parts, "imgs", scatter_dimension=0, tiled=False)


def own_order(blocks, tile):
    stacked = jnp.stack(blocks)
    return [lax.dynamic_index_in_dim(stacked, tile ^ k, 0, keepdims=False) for k in range(4)]


SMEM = pl.BlockSpec(memory_space=pltpu.SMEM)
VMEM = pl.BlockSpec(memory_space=pltpu.VMEM)
PAD = 16


def vec_call(kernel, outs, n_in, scratch=(), us=5):
    return pl.pallas_call(
        kernel,
        out_shape=outs,
        in_specs=[SMEM] + [VMEM] * n_in,
        out_specs=jax.tree.map(lambda _: VMEM, outs),
        scratch_shapes=list(scratch),
        cost_estimate=cost(us),
    )


def cost(us):
    return pl.CostEstimate(flops=us * 10**9, transcendentals=0, bytes_accessed=us * 10**6)


def sds(shape, dtype=BF):
    return jax.ShapeDtypeStruct(shape, dtype)


def load_tile(ref, scratch, at):
    rows, cols, width = ref.shape[1:]
    scratch[at : at + rows * PAD, :] = jnp.zeros((rows * PAD, width), scratch.dtype)
    for i in range(rows):
        scratch[at + i * PAD : at + i * PAD + cols, :] = ref[0, i]


def store_tile(ref, value):
    rows, cols, _ = ref.shape[1:]
    for i in range(rows):
        ref[0, i] = value[i * PAD : i * PAD + cols, :]


def mask_edges(mask):
    m = mask[0].astype(F32)
    high = jnp.sum(m[:, 0:1], axis=0, keepdims=True)
    wide = jnp.sum(m[0:1, :], axis=1, keepdims=True)
    return high, wide


def keep_tokens(edges, place, rows, cols, axis):
    toks = rows * PAD
    shape = (toks, 1) if axis == 0 else (1, toks)
    tok = lax.broadcasted_iota(jnp.int32, shape, axis)
    c = tok & (PAD - 1)
    r = ((tok >> 4) + (place >> 1) * rows).astype(F32)
    at = (c + (place & 1) * cols).astype(F32)
    ok = (c < cols) & (r < edges[0]) & (at < edges[1])
    return jnp.where(ok, 1.0, 0.0).astype(F32)


def mask_row(tile, mask, rows, cols):
    edges = mask_edges(mask)
    keep = [keep_tokens(edges, tile[0] ^ r, rows, cols, 1) for r in range(4)]
    return jnp.where(jnp.concatenate(keep, axis=1) > 0, 0.0, MASKED_SCORE).astype(F32)


def vec_row(ref):
    return ref[...].reshape(1, -1)


def heads_kernel(tile, qkv_w, qv_b, w_own, b_own):
    width = qv_b.shape[1]
    part = width // 4
    for g in range(4):

        @pl.when(tile[0] == g)
        def _():
            for i in range(3):
                src = i * width + g * part
                w_own[:, i * part : (i + 1) * part] = qkv_w[:, src : src + part]
            b_own[:, :part] = qv_b[0:1, g * part : (g + 1) * part]
            b_own[:, part : 2 * part] = jnp.zeros((1, part), F32)
            b_own[:, 2 * part :] = qv_b[1:2, g * part : (g + 1) * part]


def units_kernel(tile, fc1, fc1_b, fc1_own, fc1_b_own, *, quarter):
    for g in range(4):

        @pl.when(tile[0] == g)
        def _():
            for i in range(fc1.shape[1] // (4 * quarter)):
                src = (4 * i + g) * quarter
                dst = i * quarter
                fc1_own[:, dst : dst + quarter] = fc1[:, src : src + quarter]
                fc1_b_own[:, dst : dst + quarter] = fc1_b[:, src : src + quarter]


def attn_kernel(
    tile, mask, x0, x1, x2, x3, gain, shift, w, bias, hid, nrm, qkv, lse, c0, c1, c2, c3, xs, ctx
):
    rows, cols, width = x0.shape[1:]
    toks = rows * PAD
    part = w.shape[1] // 3
    dim = width // HEADS
    scale = dim ** (-0.5)
    for r, ref in enumerate((x0, x1, x2, x3)):
        load_tile(ref, xs, r * toks)

    normed, _ = norm_stats(xs[...].astype(F32))
    nrm[...] = normed.astype(BF)
    hid[...] = (normed * vec_row(gain) + vec_row(shift)).astype(BF)
    qkv[...] = (mm(hid[...], w[...]) + bias[...]).astype(BF)
    masked = mask_row(tile, mask, rows, cols)

    def attend(r, carry):
        at = pl.ds(pl.multiple_of(r * toks, toks), toks)
        outs = []
        for h in range(part // dim):
            q = qkv[at, h * dim : (h + 1) * dim]
            k = qkv[:, part + h * dim : part + (h + 1) * dim]
            v = qkv[:, 2 * part + h * dim : 2 * part + (h + 1) * dim]
            s = mm_nt(q * scale, k) + masked
            top = jnp.max(s, axis=-1, keepdims=True)
            e = jnp.exp(s - top)
            total = jnp.sum(e, axis=-1, keepdims=True)
            outs.append((mm(e.astype(BF), v) * (1.0 / total)).astype(BF))
            lse[at, h : h + 1] = top + jnp.log(total)
        ctx[r] = jnp.concatenate(outs, axis=1)
        return carry

    lax.fori_loop(0, 4, attend, 0)
    for r, ref in enumerate((c0, c1, c2, c3)):
        ref[...] = ctx[r]


def branch_kernel(tile, c0, c1, c2, c3, wo, bo, x, gain, shift, resid, hid, xs):
    part = c0.shape[1]
    load_tile(x, xs, 0)
    acc = xs[...].astype(F32) + vec_row(bo)
    for r, ref in enumerate((c0, c1, c2, c3)):
        at = pl.multiple_of((tile[0] ^ r) * part, part)
        acc = acc + mm(ref[...], wo[pl.ds(at, part), :])
    resid[...] = acc
    normed, _ = norm_stats(acc)
    hid[...] = (normed * vec_row(gain) + vec_row(shift)).astype(BF)


def mlp_kernel(
    tile, mask, resid, hid, ct, gain, fc1, fc1_b, fc2, fc2_b, out, branch, rgrad, vecs, up, acc, nacc
):
    step = pl.program_id(0)
    rows, cols, _ = ct.shape[1:]

    @pl.when(step == 0)
    def _():
        load_tile(ct, up, 0)
        up[...] = (up[...].astype(F32) * keep_tokens(mask_edges(mask), tile[0], rows, cols, 0)).astype(BF)
        acc[...] = jnp.zeros_like(acc)
        nacc[...] = jnp.zeros_like(nacc)

    act, dgelu = gelu_parts(mm(hid[...], fc1[...]) + fc1_b[...])
    acc[...] += mm(act.astype(BF), fc2[...])
    inner = (mm_nt(up[...], fc2[...]) * dgelu).astype(BF)
    nacc[...] += mm_nt(inner, fc1[...])

    @pl.when(step == pl.num_programs(0) - 1)
    def _():
        res = resid[...]
        keep = keep_tokens(mask_edges(mask), tile[0], rows, cols, 0)
        store_tile(out, (keep * (res + acc[...] + vec_row(fc2_b))).astype(BF))
        normed, inv = norm_stats(res)
        n = nacc[...]
        vecs[0:1, :] = jnp.sum(n * normed, axis=0, keepdims=True)
        vecs[1:2, :] = jnp.sum(n, axis=0, keepdims=True)
        grad = up[...].astype(F32) + norm_back(n, normed, inv, vec_row(gain))
        rgrad[...] = grad
        branch[...] = grad.astype(BF)


def ffgrad_kernel(
    tile, mask, h0, h1, h2, h3, t0, t1, t2, t3, fc1, fc1_b, fc2, g1, g2, b1, b2, up, a1, a2
):
    rows, cols, _ = t0.shape[1:]
    edges = mask_edges(mask)
    hids = (h0, h1, h2, h3)
    for r, ref in enumerate((t0, t1, t2, t3)):
        load_tile(ref, up, 0)
        wide = up[...].astype(F32) * keep_tokens(edges, tile[0] ^ r, rows, cols, 0)
        low = wide.astype(BF)
        h = hids[r][...]
        act, dgelu = gelu_parts(mm(h, fc1[...]) + fc1_b[...])
        inner = (mm_nt(low, fc2[...]) * dgelu).astype(BF)
        d1 = mm_tn(h, inner)
        d2 = mm_tn(act.astype(BF), low)
        s1 = jnp.sum(inner.astype(F32), axis=0, keepdims=True)
        s2 = jnp.sum(wide, axis=0, keepdims=True)
        if r == 0:
            a1[...], a2[...], b1[...], b2[...] = d1, d2, s1, s2
        elif r < 3:
            a1[...] += d1
            a2[...] += d2
            b1[...] += s1
            b2[...] += s2
        else:
            g1[...] = (a1[...] + d1).astype(BF)
            g2[...] = (a2[...] + d2).astype(BF)
            b1[...] += s1
            b2[...] += s2


def outgrad_kernel(tile, b0, b1, b2, b3, wo, c0, c1, c2, c3, dctx, gout, bsum):
    toks, part = c0.shape
    at = pl.multiple_of(tile[0] * part, part)
    w = wo[pl.ds(at, part), :]
    ctx = (c0, c1, c2, c3)
    acc = None
    total = None
    for r, ref in enumerate((b0, b1, b2, b3)):
        low = ref[...]
        dctx[r * toks : (r + 1) * toks, :] = mm_nt(low, w).astype(BF)
        d = mm_tn(ctx[r][...], low)
        s = jnp.sum(low.astype(F32), axis=0, keepdims=True)
        acc = d if r == 0 else acc + d
        total = s if r == 0 else total + s
    gout[...] = acc.astype(BF)
    bsum[...] = total


def attnback_kernel(
    tile,
    mask,
    dctx,
    qkv,
    lse,
    hid,
    nrm,
    w,
    bsum,
    vec2,
    fb2,
    m0,
    m1,
    m2,
    m3,
    gqkv,
    vecs,
    dk,
    dv,
    mix,
    *,
    cols,
):
    total, three = qkv.shape
    part = three // 3
    toks = total // 4
    dim = hid.shape[1] // HEADS
    rows = toks // PAD
    scale = dim ** (-0.5)
    masked = mask_row(tile, mask, rows, cols)
    dk[...] = jnp.zeros_like(dk)
    dv[...] = jnp.zeros_like(dv)

    def attend(r, carry):
        at = pl.ds(pl.multiple_of(r * toks, toks), toks)
        dqs = []
        q_all = qkv[at, :part] * scale
        do_all = dctx[at, :]
        q_turned = q_all.T
        do_turned = do_all.T
        for h in range(part // dim):
            at_h = slice(h * dim, (h + 1) * dim)
            k = qkv[:, part + h * dim : part + (h + 1) * dim]
            v = qkv[:, 2 * part + h * dim : 2 * part + (h + 1) * dim]
            p = jnp.exp(mm_nt(q_all[:, at_h], k) + masked - lse[at, h : h + 1])
            dp = mm_nt(do_all[:, at_h], v)
            ds = (p * (dp - jnp.sum(dp * p, axis=-1, keepdims=True))).astype(BF)
            dqs.append((mm(ds, k) * scale).astype(BF))
            dv[at_h, :] += mm(do_turned[at_h], p.astype(BF))
            dk[at_h, :] += mm(q_turned[at_h], ds)
        mix[at, :part] = jnp.concatenate(dqs, axis=1)
        return carry

    lax.fori_loop(0, 4, attend, 0)
    mix[:, part : 2 * part] = dk[...].T.astype(BF)
    mix[:, 2 * part :] = dv[...].T.astype(BF)
    gqkv[...] = mm_tn(hid[...], mix[...]).astype(BF)
    for r, ref in enumerate((m0, m1, m2, m3)):
        ref[...] = mix[r * toks : (r + 1) * toks, :]
    col_sum = jnp.sum(mix[...].astype(F32), axis=0, keepdims=True)
    chunk = 256
    for i in range(w.shape[0] // chunk):
        at = slice(i * chunk, (i + 1) * chunk)
        n = mm_nt(mix[...], w[at, :])
        vecs[0:1, at] = jnp.sum(n * nrm[:, at].astype(F32), axis=0, keepdims=True)
        vecs[1:2, at] = jnp.sum(n, axis=0, keepdims=True)
    slot = lax.broadcasted_iota(jnp.int32, (1, 4 * part), 1)
    own = (slot >= tile[0] * part) & (slot < (tile[0] + 1) * part)
    lone = jnp.where(tile[0] == 0, 1.0, 0.0).astype(F32)
    for i in range(3):
        piece = col_sum[:, i * part : (i + 1) * part]
        vecs[2 + i : 3 + i, :] = jnp.where(own, jnp.concatenate([piece] * 4, axis=1), 0.0)
    vecs[5:6, :] = bsum[...] * lone
    vecs[6:8, :] = vec2[...]
    vecs[8:9, :] = fb2[...] * lone


def input_kernel(tile, m0, m1, m2, m3, w, x, rgrad, gain, out, ms, xs):
    part = m0.shape[1] // 3
    for r, ref in enumerate((m0, m1, m2, m3)):
        ms[r] = ref[...]
    tiles = [ms[tile[0] ^ g] for g in range(4)]
    full = jnp.concatenate(
        [m[:, i * part : (i + 1) * part] for i in range(3) for m in tiles], axis=1
    )
    n = mm_nt(full, w[...])
    load_tile(x, xs, 0)
    normed, inv = norm_stats(xs[...].astype(F32))
    store_tile(out, (rgrad[...] + norm_back(n, normed, inv, vec_row(gain))).astype(BF))


def ffout_kernel(tile, a0, a1, a2, a3, b0, b1, b2, b3, fc1, fc2, ps):
    quarter = fc2.shape[0] // 4
    for r, ref in enumerate((a0, a1, a2, a3)):
        ps[r] = ref[...].astype(F32)
    for g in range(4):
        piece = ps[tile[0] ^ g]
        for i in range(fc1.shape[1] // (4 * quarter)):
            dst = (4 * i + g) * quarter
            fc1[:, dst : dst + quarter] = piece[:, i * quarter : (i + 1) * quarter]
    for r, ref in enumerate((b0, b1, b2, b3)):
        ps[r, :quarter, :] = ref[...].astype(F32)
    for g in range(4):
        fc2[g * quarter : (g + 1) * quarter, :] = ps[tile[0] ^ g][:quarter]


def attnout_kernel(
    tile, p0, p1, p2, p3, gqkv, gout, v0, v1, v5, v6, v7, v8, qv, units, ps
):
    rows, width = gout.shape
    part = width // 4
    quarter = units.shape[0] // 4
    height = ps.shape[1] - rows
    for r, ref in enumerate((p0, p1, p2, p3)):
        ps[r] = ref[...].astype(F32)
    total = None
    tails = []
    for g in range(4):
        piece = ps[tile[0] ^ g]
        for i in range(3):
            dst = i * width + g * part
            gqkv[:, dst : dst + part] = piece[:rows, i * part : (i + 1) * part]
        gout[:, g * part : (g + 1) * part] = piece[:rows, 3 * part :]
        tail = jnp.concatenate([piece[rows + j : rows + j + 1] for j in range(height)], axis=1)
        total = tail if g == 0 else total + tail
        tails.append(tail[:, 9 * rows : 9 * rows + quarter])
    for i, ref in ((0, v0), (1, v1), (5, v5), (6, v6), (7, v7), (8, v8)):
        ref[...] = total[0, i * rows : (i + 1) * rows]
    both = [total[:, i * rows : (i + 1) * rows] for i in (2, 4)]
    qv[...] = jnp.concatenate(both, axis=0).T
    units[...] = jnp.concatenate(tails, axis=1)[0]


def body(
    patches,
    patch_mask,
    norm1_gain,
    norm1_shift,
    qkv_weight,
    qv_bias,
    out_weight,
    out_bias,
    norm2_gain,
    norm2_shift,
    fc1_weight,
    fc1_bias,
    fc2_weight,
    fc2_bias,
    cotangent,
):
    _, rows, cols, width = patches.shape
    ff = fc1_weight.shape[1]
    imgs = lax.axis_size("imgs")
    part = width // 4
    units = ff // 4
    quarter = units // imgs
    share = width // imgs
    toks = rows * PAD
    total = 4 * toks
    tile = lax.axis_index("rows") * 2 + lax.axis_index("cols")
    at_tile = tile.reshape(1).astype(jnp.int32)

    def row(v):
        return v.reshape(1, -1)

    steps = 4
    w_own, b_own = pl.pallas_call(
        heads_kernel,
        grid=(steps,),
        in_specs=[
            SMEM,
            pl.BlockSpec((width // steps, 3 * width), lambda i: (i, 0)),
            pl.BlockSpec((2, width), lambda i: (0, 0)),
        ],
        out_specs=[
            pl.BlockSpec((width // steps, 3 * part), lambda i: (i, 0)),
            pl.BlockSpec((1, 3 * part), lambda i: (0, 0)),
        ],
        out_shape=[sds((width, 3 * part)), sds((1, 3 * part), F32)],
        cost_estimate=cost(4),
        name="heads",
    )(at_tile, qkv_weight, qv_bias.T)
    x_blocks, (w_own, b_own) = gather_tiles(patches, (w_own, b_own))

    hid1, nrm1, qkv, lse, *ctx = vec_call(
        attn_kernel,
        [
            sds((total, width)),
            sds((total, width)),
            sds((total, 3 * part)),
            sds((total, 128), F32),
        ]
        + [sds((toks, part))] * 4,
        9,
        [pltpu.VMEM((total, width), BF), pltpu.VMEM((4, toks, part), BF)],
        us=13,
    )(at_tile, patch_mask, *x_blocks, norm1_gain, norm1_shift, w_own, b_own)
    ct_blocks, ctx = gather_tiles(cotangent, ctx)
    later_tile, _ = tie(at_tile, ctx)

    fc1_own, fc1_b_own = pl.pallas_call(
        functools.partial(units_kernel, quarter=quarter),
        grid=(steps,),
        in_specs=[
            SMEM,
            pl.BlockSpec((width // steps, ff), lambda i: (i, 0)),
            pl.BlockSpec((1, ff), lambda i: (0, 0)),
        ],
        out_specs=[
            pl.BlockSpec((width // steps, units), lambda i: (i, 0)),
            pl.BlockSpec((1, units), lambda i: (0, 0)),
        ],
        out_shape=[sds((width, units)), sds((1, units), F32)],
        cost_estimate=cost(4),
        name="units",
    )(later_tile, fc1_weight, row(fc1_bias))
    fc2_own = lax.dynamic_index_in_dim(
        fc2_weight.reshape(imgs, 4, quarter, width), later_tile[0], 1, keepdims=False
    ).reshape(units, width)

    ctx_in = scatter_tiles(ctx)
    ctx_in, (fc1_own, fc1_b_own, fc2_own) = tie(ctx_in, (fc1_own, fc1_b_own, fc2_own))
    resid, hid2 = vec_call(
        branch_kernel,
        [sds((toks, width), F32), sds((toks, width))],
        9,
        [pltpu.VMEM((toks, width), BF)],
        us=3,
    )(at_tile, *ctx_in, out_weight, out_bias, patches, norm2_gain, norm2_shift)

    chunks = 4
    step = ff // chunks

    def whole(*shape):
        return pl.BlockSpec(shape, lambda i: (0,) * len(shape))

    layer_out, branch, rgrad, vec2 = pl.pallas_call(
        mlp_kernel,
        grid=(chunks,),
        in_specs=[
            SMEM,
            whole(*patch_mask.shape),
            whole(toks, width),
            whole(toks, width),
            whole(1, rows, cols, width),
            whole(width),
            pl.BlockSpec((width, step), lambda i: (0, i)),
            pl.BlockSpec((1, step), lambda i: (0, i)),
            pl.BlockSpec((step, width), lambda i: (i, 0)),
            whole(width),
        ],
        out_specs=[
            whole(1, rows, cols, width),
            whole(toks, width),
            whole(toks, width),
            whole(2, width),
        ],
        out_shape=[
            sds((1, rows, cols, width)),
            sds((toks, width)),
            sds((toks, width), F32),
            sds((2, width), F32),
        ],
        scratch_shapes=[
            pltpu.VMEM((toks, width), BF),
            pltpu.VMEM((toks, width), F32),
            pltpu.VMEM((toks, width), F32),
        ],
        cost_estimate=cost(11),
        name="mlp",
    )(
        at_tile,
        patch_mask,
        resid,
        hid2,
        cotangent,
        norm2_gain,
        fc1_weight,
        row(fc1_bias),
        fc2_weight,
        fc2_bias,
    )
    hid2_blocks, (branch,) = gather_tiles(hid2, (branch,))

    g1, g2, fb1, fb2 = vec_call(
        ffgrad_kernel,
        [sds((width, units)), sds((units, width)), sds((1, units), F32), sds((1, width), F32)],
        12,
        [
            pltpu.VMEM((toks, width), BF),
            pltpu.VMEM((width, units), F32),
            pltpu.VMEM((units, width), F32),
        ],
        us=9,
    )(at_tile, patch_mask, *hid2_blocks, *ct_blocks, fc1_own, fc1_b_own, fc2_own)
    branch_blocks, (g1, g2) = gather_tiles(branch, (g1, g2))

    dctx, gout, bsum = vec_call(
        outgrad_kernel,
        [sds((total, part)), sds((part, width)), sds((1, width), F32)],
        9,
        us=4,
    )(at_tile, *branch_blocks, out_weight, *ctx)
    direct = direct_sum(imgs)
    (g1, g2), (gout,) = tie((g1, g2), (gout,))
    g1 = g1.reshape(imgs, share, units)
    g2 = g2.reshape(imgs, quarter, width)
    out_cols = [lax.dynamic_slice_in_dim(gout, (tile ^ r) * part, part, 1) for r in range(4)]
    out_rows = scatter_tiles(out_cols)
    if direct:
        line = imgs // 2
        (g1, g2), out_cols = tie((g1, g2), out_cols)
        near1 = exchange_near(g1.reshape(line, 2, share, units))
        far2 = exchange_far(g2.reshape(line, 2, quarter, width))
    dctx, out_rows = tie(dctx, out_rows)
    out_rows = jnp.concatenate(own_order(out_rows, tile), axis=0)

    *mixed, gqkv, vecs = vec_call(
        functools.partial(attnback_kernel, cols=cols),
        [sds((toks, 3 * part))] * 4 + [sds((width, 3 * part)), sds((9, width), F32)],
        10,
        [
            pltpu.VMEM((part, total), F32),
            pltpu.VMEM((part, total), F32),
            pltpu.VMEM((total, 3 * part), BF),
        ],
        us=18,
    )(at_tile, patch_mask, dctx, qkv, lse, hid1, nrm1, w_own, bsum, vec2, fb2)
    mixed_in = scatter_tiles(mixed)

    vecs = vecs.reshape(9, imgs, share).transpose(1, 0, 2).reshape(imgs, 9 * share)
    count = 9 * share + quarter
    vec_height = -(-count // width)
    spare = jnp.zeros((imgs, vec_height * width - count), F32)
    vecs = jnp.concatenate([vecs, fb1.reshape(imgs, quarter), spare], axis=1).astype(BF)
    at_bucket = jnp.concatenate(
        [
            jnp.concatenate([gqkv, out_rows], axis=1).reshape(imgs, share, width),
            vecs.reshape(imgs, vec_height, width),
        ],
        axis=1,
    )
    if direct:
        near3 = exchange_near(at_bucket.reshape(line, 2, share + vec_height, width))
        (near1, far2), (at_bucket,) = tie((near1, far2), (at_bucket,))
        far1 = exchange_far(total_of(near1).astype(BF))
        near2 = exchange_near(total_of(far2).astype(BF)[None])
        near3, (far1[0],) = tie(near3, (far1[0],))
        mid3 = total_of(near3).astype(BF)
        mixed_in[0], (mid3,) = tie(mixed_in[0], (mid3,))
        far3 = exchange_far(mid3)

    patches_grad = vec_call(
        input_kernel,
        sds((1, rows, cols, width)),
        8,
        [pltpu.VMEM((4, toks, 3 * part), BF), pltpu.VMEM((toks, width), BF)],
        us=5,
    )(at_tile, *mixed_in, qkv_weight, patches, rgrad, norm1_gain)

    if direct:
        fc2_sum = total_of(near2)[0].astype(BF)
        fc1_sum = total_of(far1).astype(BF)
    else:
        fc1_sum, fc2_sum, at_sum = (plain_sum(b) for b in (g1, g2, at_bucket))
    fc2_pieces, _ = gather_tiles(fc2_sum)
    fc1_pieces, _ = gather_tiles(fc1_sum)
    if direct:
        far3, (fc1_pieces[2], fc2_pieces[2], patches_grad) = tie(
            far3, (fc1_pieces[2], fc2_pieces[2], patches_grad)
        )
        at_sum = total_of(far3).astype(BF)
    fc1_grad, fc2_grad = vec_call(
        ffout_kernel,
        [sds((share, ff), F32), sds((4 * quarter, width), F32)],
        8,
        [pltpu.VMEM((4, max(share, quarter), width), F32)],
        us=3,
    )(at_tile, *fc1_pieces, *fc2_pieces)
    at_pieces, (fc1_grad, fc2_grad) = gather_tiles(at_sum, (fc1_grad, fc2_grad))
    qkv_grad, out_grad, *vec_sums, qv_sum, unit_sum = vec_call(
        attnout_kernel,
        [
            sds((share, 3 * width), F32),
            sds((share, width), F32),
            *[sds((share,), F32)] * 6,
            sds((share, 2), F32),
            sds((4 * quarter,), F32),
        ],
        4,
        [pltpu.VMEM((4, share + vec_height, width), F32)],
        us=3,
    )(at_tile, *at_pieces)
    return (
        layer_out,
        patches_grad,
        vec_sums[0],
        vec_sums[1],
        qkv_grad,
        qv_sum,
        out_grad,
        vec_sums[2],
        vec_sums[3],
        vec_sums[4],
        fc1_grad,
        unit_sum,
        fc2_grad,
        vec_sums[5],
    )


def solution(mesh):
    tiled = P("imgs", "rows", "cols", None)
    in_specs = (tiled, P("imgs", None, None)) + (P(),) * 12 + (tiled,)
    mat = P("imgs", None)
    vec = P("imgs")
    out_specs = (tiled, tiled, vec, vec, mat, mat, mat, vec, vec, vec, mat, vec, mat, vec)
    return jax.shard_map(body, mesh=mesh, in_specs=in_specs, out_specs=out_specs, check_vma=False)
```

```python
import functools

import jax
import jax.numpy as jnp
from jax import lax
from jax.experimental import pallas as pl
from jax.experimental.pallas import tpu as pltpu
from jax.sharding import PartitionSpec as P

HEADS = 12
NORM_EPS = 1e-06
MASKED_SCORE = -1e30
GROUP = ("rows", "cols")
BF = jnp.bfloat16
F32 = jnp.float32


def dot(left, right, dims):
    return lax.dot_general(left, right, (dims, ((), ())), preferred_element_type=F32)


def mm(left, right):
    return dot(left, right, ((1,), (0,)))


def mm_nt(left, right):
    return dot(left, right, ((1,), (1,)))


def mm_tn(left, right):
    return dot(left, right, ((0,), (0,)))


def to_peer(value, rel):
    if rel == 1:
        return lax.ppermute(value, "cols", [(0, 1), (1, 0)])
    if rel == 2:
        return lax.ppermute(value, "rows", [(0, 1), (1, 0)])
    return lax.ppermute(value, GROUP, [(i, i ^ 3) for i in range(4)])


def tie(values, others):
    flat, tree = jax.tree.flatten((values, others))
    return jax.tree.unflatten(tree, lax.optimization_barrier(flat))


def gather_tiles(value, others=()):
    across = to_peer(value, 2)
    beside = to_peer(value, 1)
    across, others = tie(across, others)
    return [value, beside, across, to_peer(across, 1)], others


def scatter_tiles(blocks):
    return [blocks[0], to_peer(blocks[1], 1), to_peer(blocks[2], 2), to_peer(blocks[3], 3)]


def norm_stats(values):
    mean_val = jnp.mean(values, axis=-1, keepdims=True)
    centred = values - mean_val
    var_val = jnp.mean(centred * centred, axis=-1, keepdims=True)
    inv = lax.rsqrt(var_val + NORM_EPS)
    return centred * inv, inv


def norm_back(grads, normed, inv, gain):
    g = grads * gain
    return (
        g
        - jnp.mean(g, axis=-1, keepdims=True)
        - normed * jnp.mean(g * normed, axis=-1, keepdims=True)
    ) * inv


def gelu_parts(x):
    cdf = 0.5 * (1.0 + lax.erf(x * 0.7071067811865476))
    pdf = jnp.exp(-0.5 * x * x) * 0.3989422804014327
    return x * cdf, cdf + x * pdf


def exchange_near(parts):
    side = lax.axis_index("imgs") % 2
    count = lax.axis_size("imgs")
    send = lax.dynamic_index_in_dim(parts, 1 - side, 1, keepdims=False)
    keep = lax.dynamic_index_in_dim(parts, side, 1, keepdims=False)
    return keep, lax.ppermute(send, "imgs", [(i, i ^ 1) for i in range(count)])


def exchange_far(parts):
    count = lax.axis_size("imgs")
    place = lax.axis_index("imgs") // 2
    got = [lax.dynamic_index_in_dim(parts, place, 0, keepdims=False)]
    for k in range(count // 2 - 1, 0, -1):
        send = lax.dynamic_index_in_dim(parts, place ^ k, 0, keepdims=False)
        got.append(lax.ppermute(send, "imgs", [(i, i ^ (2 * k)) for i in range(count)]))
    return got


def total_of(blocks):
    return functools.reduce(jnp.add, [b.astype(F32) for b in blocks])


def direct_sum(imgs):
    return imgs <= 8 and imgs & (imgs - 1) == 0


def plain_sum(parts):
    return lax.psum_scatter(parts, "imgs", scatter_dimension=0, tiled=False)


def own_order(blocks, tile):
    stacked = jnp.stack(blocks)
    return [lax.dynamic_index_in_dim(stacked, tile ^ k, 0, keepdims=False) for k in range(4)]


SMEM = pl.BlockSpec(memory_space=pltpu.SMEM)
VMEM = pl.BlockSpec(memory_space=pltpu.VMEM)
PAD = 16


def vec_call(kernel, outs, n_in, scratch=(), us=5):
    return pl.pallas_call(
        kernel,
        out_shape=outs,
        in_specs=[SMEM] + [VMEM] * n_in,
        out_specs=jax.tree.map(lambda _: VMEM, outs),
        scratch_shapes=list(scratch),
        cost_estimate=cost(us),
    )


def cost(us):
    return pl.CostEstimate(flops=us * 10**9, transcendentals=0, bytes_accessed=us * 10**6)


def sds(shape, dtype=BF):
    return jax.ShapeDtypeStruct(shape, dtype)


def load_tile(ref, scratch, at):
    rows, cols, width = ref.shape[1:]
    scratch[at : at + rows * PAD, :] = jnp.zeros((rows * PAD, width), scratch.dtype)
    for i in range(rows):
        scratch[at + i * PAD : at + i * PAD + cols, :] = ref[0, i]


def store_tile(ref, value):
    rows, cols, _ = ref.shape[1:]
    for i in range(rows):
        ref[0, i] = value[i * PAD : i * PAD + cols, :]


def mask_edges(mask):
    m = mask[0].astype(F32)
    high = jnp.sum(m[:, 0:1], axis=0, keepdims=True)
    wide = jnp.sum(m[0:1, :], axis=1, keepdims=True)
    return high, wide


def keep_tokens(edges, place, rows, cols, axis):
    toks = rows * PAD
    shape = (toks, 1) if axis == 0 else (1, toks)
    tok = lax.broadcasted_iota(jnp.int32, shape, axis)
    c = tok & (PAD - 1)
    r = ((tok >> 4) + (place >> 1) * rows).astype(F32)
    at = (c + (place & 1) * cols).astype(F32)
    ok = (c < cols) & (r < edges[0]) & (at < edges[1])
    return jnp.where(ok, 1.0, 0.0).astype(F32)


def mask_row(tile, mask, rows, cols):
    edges = mask_edges(mask)
    keep = [keep_tokens(edges, tile[0] ^ r, rows, cols, 1) for r in range(4)]
    return jnp.where(jnp.concatenate(keep, axis=1) > 0, 0.0, MASKED_SCORE).astype(F32)


def vec_row(ref):
    return ref[...].reshape(1, -1)


def heads_kernel(tile, qkv_w, qv_b, w_own, b_own):
    width = qv_b.shape[1]
    part = width // 4
    for g in range(4):

        @pl.when(tile[0] == g)
        def _():
            for i in range(3):
                src = i * width + g * part
                w_own[:, i * part : (i + 1) * part] = qkv_w[:, src : src + part]
            b_own[:, :part] = qv_b[0:1, g * part : (g + 1) * part]
            b_own[:, part : 2 * part] = jnp.zeros((1, part), F32)
            b_own[:, 2 * part :] = qv_b[1:2, g * part : (g + 1) * part]


def units_kernel(tile, fc1, fc1_b, fc1_own, fc1_b_own, *, quarter):
    for g in range(4):

        @pl.when(tile[0] == g)
        def _():
            for i in range(fc1.shape[1] // (4 * quarter)):
                src = (4 * i + g) * quarter
                dst = i * quarter
                fc1_own[:, dst : dst + quarter] = fc1[:, src : src + quarter]
                fc1_b_own[:, dst : dst + quarter] = fc1_b[:, src : src + quarter]


def attn_kernel(
    tile, mask, x0, x1, x2, x3, gain, shift, w, bias, hid, nrm, qkv, lse, c0, c1, c2, c3, xs, ctx
):
    rows, cols, width = x0.shape[1:]
    toks = rows * PAD
    part = w.shape[1] // 3
    dim = width // HEADS
    scale = dim ** (-0.5)
    for r, ref in enumerate((x0, x1, x2, x3)):
        load_tile(ref, xs, r * toks)

    normed, _ = norm_stats(xs[...].astype(F32))
    nrm[...] = normed.astype(BF)
    hid[...] = (normed * vec_row(gain) + vec_row(shift)).astype(BF)
    qkv[...] = (mm(hid[...], w[...]) + bias[...]).astype(BF)
    masked = mask_row(tile, mask, rows, cols)

    def attend(r, carry):
        at = pl.ds(pl.multiple_of(r * toks, toks), toks)
        outs = []
        for h in range(part // dim):
            q = qkv[at, h * dim : (h + 1) * dim]
            k = qkv[:, part + h * dim : part + (h + 1) * dim]
            v = qkv[:, 2 * part + h * dim : 2 * part + (h + 1) * dim]
            s = mm_nt(q * scale, k) + masked
            top = jnp.max(s, axis=-1, keepdims=True)
            e = jnp.exp(s - top)
            total = jnp.sum(e, axis=-1, keepdims=True)
            outs.append((mm(e.astype(BF), v) * (1.0 / total)).astype(BF))
            lse[at, h : h + 1] = top + jnp.log(total)
        ctx[r] = jnp.concatenate(outs, axis=1)
        return carry

    lax.fori_loop(0, 4, attend, 0)
    for r, ref in enumerate((c0, c1, c2, c3)):
        ref[...] = ctx[r]


def branch_kernel(tile, c0, c1, c2, c3, wo, bo, x, gain, shift, resid, hid, xs):
    part = c0.shape[1]
    load_tile(x, xs, 0)
    acc = xs[...].astype(F32) + vec_row(bo)
    for r, ref in enumerate((c0, c1, c2, c3)):
        at = pl.multiple_of((tile[0] ^ r) * part, part)
        acc = acc + mm(ref[...], wo[pl.ds(at, part), :])
    resid[...] = acc
    normed, _ = norm_stats(acc)
    hid[...] = (normed * vec_row(gain) + vec_row(shift)).astype(BF)


def mlp_kernel(
    tile, mask, resid, hid, ct, gain, fc1, fc1_b, fc2, fc2_b, out, branch, rgrad, vecs, up, acc, nacc
):
    step = pl.program_id(0)
    rows, cols, _ = ct.shape[1:]

    @pl.when(step == 0)
    def _():
        load_tile(ct, up, 0)
        up[...] = (up[...].astype(F32) * keep_tokens(mask_edges(mask), tile[0], rows, cols, 0)).astype(BF)
        acc[...] = jnp.zeros_like(acc)
        nacc[...] = jnp.zeros_like(nacc)

    act, dgelu = gelu_parts(mm(hid[...], fc1[...]) + fc1_b[...])
    acc[...] += mm(act.astype(BF), fc2[...])
    inner = (mm_nt(up[...], fc2[...]) * dgelu).astype(BF)
    nacc[...] += mm_nt(inner, fc1[...])

    @pl.when(step == pl.num_programs(0) - 1)
    def _():
        res = resid[...]
        keep = keep_tokens(mask_edges(mask), tile[0], rows, cols, 0)
        store_tile(out, (keep * (res + acc[...] + vec_row(fc2_b))).astype(BF))
        normed, inv = norm_stats(res)
        n = nacc[...]
        vecs[0:1, :] = jnp.sum(n * normed, axis=0, keepdims=True)
        vecs[1:2, :] = jnp.sum(n, axis=0, keepdims=True)
        grad = up[...].astype(F32) + norm_back(n, normed, inv, vec_row(gain))
        rgrad[...] = grad
        branch[...] = grad.astype(BF)


def ffgrad_kernel(
    tile, mask, h0, h1, h2, h3, t0, t1, t2, t3, fc1, fc1_b, fc2, g1, g2, b1, b2, up, a1, a2
):
    rows, cols, _ = t0.shape[1:]
    edges = mask_edges(mask)
    hids = (h0, h1, h2, h3)
    for r, ref in enumerate((t0, t1, t2, t3)):
        load_tile(ref, up, 0)
        wide = up[...].astype(F32) * keep_tokens(edges, tile[0] ^ r, rows, cols, 0)
        low = wide.astype(BF)
        h = hids[r][...]
        act, dgelu = gelu_parts(mm(h, fc1[...]) + fc1_b[...])
        inner = (mm_nt(low, fc2[...]) * dgelu).astype(BF)
        d1 = mm_tn(h, inner)
        d2 = mm_tn(act.astype(BF), low)
        s1 = jnp.sum(inner.astype(F32), axis=0, keepdims=True)
        s2 = jnp.sum(wide, axis=0, keepdims=True)
        if r == 0:
            a1[...], a2[...], b1[...], b2[...] = d1, d2, s1, s2
        elif r < 3:
            a1[...] += d1
            a2[...] += d2
            b1[...] += s1
            b2[...] += s2
        else:
            g1[...] = (a1[...] + d1).astype(BF)
            g2[...] = (a2[...] + d2).astype(BF)
            b1[...] += s1
            b2[...] += s2


def outgrad_kernel(tile, b0, b1, b2, b3, wo, c0, c1, c2, c3, dctx, gout, bsum):
    toks, part = c0.shape
    at = pl.multiple_of(tile[0] * part, part)
    w = wo[pl.ds(at, part), :]
    ctx = (c0, c1, c2, c3)
    acc = None
    total = None
    for r, ref in enumerate((b0, b1, b2, b3)):
        low = ref[...]
        dctx[r * toks : (r + 1) * toks, :] = mm_nt(low, w).astype(BF)
        d = mm_tn(ctx[r][...], low)
        s = jnp.sum(low.astype(F32), axis=0, keepdims=True)
        acc = d if r == 0 else acc + d
        total = s if r == 0 else total + s
    gout[...] = acc.astype(BF)
    bsum[...] = total


def attnback_kernel(
    tile,
    mask,
    dctx,
    qkv,
    lse,
    hid,
    nrm,
    w,
    bsum,
    vec2,
    fb2,
    m0,
    m1,
    m2,
    m3,
    gqkv,
    vecs,
    dk,
    dv,
    mix,
    *,
    cols,
):
    total, three = qkv.shape
    part = three // 3
    toks = total // 4
    dim = hid.shape[1] // HEADS
    rows = toks // PAD
    scale = dim ** (-0.5)
    masked = mask_row(tile, mask, rows, cols)
    dk[...] = jnp.zeros_like(dk)
    dv[...] = jnp.zeros_like(dv)

    def attend(r, carry):
        at = pl.ds(pl.multiple_of(r * toks, toks), toks)
        dqs = []
        q_all = qkv[at, :part] * scale
        do_all = dctx[at, :]
        q_turned = q_all.T
        do_turned = do_all.T
        for h in range(part // dim):
            at_h = slice(h * dim, (h + 1) * dim)
            k = qkv[:, part + h * dim : part + (h + 1) * dim]
            v = qkv[:, 2 * part + h * dim : 2 * part + (h + 1) * dim]
            p = jnp.exp(mm_nt(q_all[:, at_h], k) + masked - lse[at, h : h + 1])
            dp = mm_nt(do_all[:, at_h], v)
            ds = (p * (dp - jnp.sum(dp * p, axis=-1, keepdims=True))).astype(BF)
            dqs.append((mm(ds, k) * scale).astype(BF))
            dv[at_h, :] += mm(do_turned[at_h], p.astype(BF))
            dk[at_h, :] += mm(q_turned[at_h], ds)
        mix[at, :part] = jnp.concatenate(dqs, axis=1)
        return carry

    lax.fori_loop(0, 4, attend, 0)
    mix[:, part : 2 * part] = dk[...].T.astype(BF)
    mix[:, 2 * part :] = dv[...].T.astype(BF)
    gqkv[...] = mm_tn(hid[...], mix[...]).astype(BF)
    for r, ref in enumerate((m0, m1, m2, m3)):
        ref[...] = mix[r * toks : (r + 1) * toks, :]
    col_sum = jnp.sum(mix[...].astype(F32), axis=0, keepdims=True)
    chunk = 256
    for i in range(w.shape[0] // chunk):
        at = slice(i * chunk, (i + 1) * chunk)
        n = mm_nt(mix[...], w[at, :])
        vecs[0:1, at] = jnp.sum(n * nrm[:, at].astype(F32), axis=0, keepdims=True)
        vecs[1:2, at] = jnp.sum(n, axis=0, keepdims=True)
    slot = lax.broadcasted_iota(jnp.int32, (1, 4 * part), 1)
    own = (slot >= tile[0] * part) & (slot < (tile[0] + 1) * part)
    lone = jnp.where(tile[0] == 0, 1.0, 0.0).astype(F32)
    for i in range(3):
        piece = col_sum[:, i * part : (i + 1) * part]
        vecs[2 + i : 3 + i, :] = jnp.where(own, jnp.concatenate([piece] * 4, axis=1), 0.0)
    vecs[5:6, :] = bsum[...] * lone
    vecs[6:8, :] = vec2[...]
    vecs[8:9, :] = fb2[...] * lone


def input_kernel(tile, m0, m1, m2, m3, w, x, rgrad, gain, out, ms, xs):
    part = m0.shape[1] // 3
    for r, ref in enumerate((m0, m1, m2, m3)):
        ms[r] = ref[...]
    tiles = [ms[tile[0] ^ g] for g in range(4)]
    full = jnp.concatenate(
        [m[:, i * part : (i + 1) * part] for i in range(3) for m in tiles], axis=1
    )
    n = mm_nt(full, w[...])
    load_tile(x, xs, 0)
    normed, inv = norm_stats(xs[...].astype(F32))
    store_tile(out, (rgrad[...] + norm_back(n, normed, inv, vec_row(gain))).astype(BF))


def ffout_kernel(tile, a0, a1, a2, a3, b0, b1, b2, b3, fc1, fc2, ps):
    quarter = fc2.shape[0] // 4
    for r, ref in enumerate((a0, a1, a2, a3)):
        ps[r] = ref[...].astype(F32)
    for g in range(4):
        piece = ps[tile[0] ^ g]
        for i in range(fc1.shape[1] // (4 * quarter)):
            dst = (4 * i + g) * quarter
            fc1[:, dst : dst + quarter] = piece[:, i * quarter : (i + 1) * quarter]
    for r, ref in enumerate((b0, b1, b2, b3)):
        ps[r, :quarter, :] = ref[...].astype(F32)
    for g in range(4):
        fc2[g * quarter : (g + 1) * quarter, :] = ps[tile[0] ^ g][:quarter]


def attnout_kernel(
    tile, p0, p1, p2, p3, gqkv, gout, v0, v1, v5, v6, v7, v8, qv, units, ps
):
    rows, width = gout.shape
    part = width // 4
    quarter = units.shape[0] // 4
    height = ps.shape[1] - rows
    for r, ref in enumerate((p0, p1, p2, p3)):
        ps[r] = ref[...].astype(F32)
    total = None
    tails = []
    for g in range(4):
        piece = ps[tile[0] ^ g]
        for i in range(3):
            dst = i * width + g * part
            gqkv[:, dst : dst + part] = piece[:rows, i * part : (i + 1) * part]
        gout[:, g * part : (g + 1) * part] = piece[:rows, 3 * part :]
        tail = jnp.concatenate([piece[rows + j : rows + j + 1] for j in range(height)], axis=1)
        total = tail if g == 0 else total + tail
        tails.append(tail[:, 9 * rows : 9 * rows + quarter])
    for i, ref in ((0, v0), (1, v1), (5, v5), (6, v6), (7, v7), (8, v8)):
        ref[...] = total[0, i * rows : (i + 1) * rows]
    both = [total[:, i * rows : (i + 1) * rows] for i in (2, 4)]
    qv[...] = jnp.concatenate(both, axis=0).T
    units[...] = jnp.concatenate(tails, axis=1)[0]


def layer(
    patches,
    patch_mask,
    norm1_gain,
    norm1_shift,
    qkv_weight,
    qv_bias,
    out_weight,
    out_bias,
    norm2_gain,
    norm2_shift,
    fc1_weight,
    fc1_bias,
    fc2_weight,
    fc2_bias,
    cotangent,
):
    _, rows, cols, width = patches.shape
    ff = fc1_weight.shape[1]
    imgs = lax.axis_size("imgs")
    part = width // 4
    units = ff // 4
    quarter = units // imgs
    share = width // imgs
    toks = rows * PAD
    total = 4 * toks
    tile = lax.axis_index("rows") * 2 + lax.axis_index("cols")
    at_tile = tile.reshape(1).astype(jnp.int32)

    def row(v):
        return v.reshape(1, -1)

    steps = 4
    w_own, b_own = pl.pallas_call(
        heads_kernel,
        grid=(steps,),
        in_specs=[
            SMEM,
            pl.BlockSpec((width // steps, 3 * width), lambda i: (i, 0)),
            pl.BlockSpec((2, width), lambda i: (0, 0)),
        ],
        out_specs=[
            pl.BlockSpec((width // steps, 3 * part), lambda i: (i, 0)),
            pl.BlockSpec((1, 3 * part), lambda i: (0, 0)),
        ],
        out_shape=[sds((width, 3 * part)), sds((1, 3 * part), F32)],
        cost_estimate=cost(4),
        name="heads",
    )(at_tile, qkv_weight, qv_bias.T)
    fc1_own, fc1_b_own = pl.pallas_call(
        functools.partial(units_kernel, quarter=quarter),
        grid=(steps,),
        in_specs=[
            SMEM,
            pl.BlockSpec((width // steps, ff), lambda i: (i, 0)),
            pl.BlockSpec((1, ff), lambda i: (0, 0)),
        ],
        out_specs=[
            pl.BlockSpec((width // steps, units), lambda i: (i, 0)),
            pl.BlockSpec((1, units), lambda i: (0, 0)),
        ],
        out_shape=[sds((width, units)), sds((1, units), F32)],
        cost_estimate=cost(4),
        name="units",
    )(at_tile, fc1_weight, row(fc1_bias))
    x_blocks, (w_own, b_own, fc1_own) = gather_tiles(patches, (w_own, b_own, fc1_own))

    hid1, nrm1, qkv, lse, *ctx = vec_call(
        attn_kernel,
        [
            sds((total, width)),
            sds((total, width)),
            sds((total, 3 * part)),
            sds((total, 128), F32),
        ]
        + [sds((toks, part))] * 4,
        9,
        [pltpu.VMEM((total, width), BF), pltpu.VMEM((4, toks, part), BF)],
        us=13,
    )(at_tile, patch_mask, *x_blocks, norm1_gain, norm1_shift, w_own, b_own)
    ct_blocks, ctx = gather_tiles(cotangent, ctx)
    later_tile, _ = tie(at_tile, ctx)

    fc2_own = lax.dynamic_index_in_dim(
        fc2_weight.reshape(imgs, 4, quarter, width), later_tile[0], 1, keepdims=False
    ).reshape(units, width)

    ctx_in = scatter_tiles(ctx)
    ctx_in, (fc2_own,) = tie(ctx_in, (fc2_own,))
    resid, hid2 = vec_call(
        branch_kernel,
        [sds((toks, width), F32), sds((toks, width))],
        9,
        [pltpu.VMEM((toks, width), BF)],
        us=3,
    )(at_tile, *ctx_in, out_weight, out_bias, patches, norm2_gain, norm2_shift)

    chunks = 4
    step = ff // chunks

    def whole(*shape):
        return pl.BlockSpec(shape, lambda i: (0,) * len(shape))

    layer_out, branch, rgrad, vec2 = pl.pallas_call(
        mlp_kernel,
        grid=(chunks,),
        in_specs=[
            SMEM,
            whole(*patch_mask.shape),
            whole(toks, width),
            whole(toks, width),
            whole(1, rows, cols, width),
            whole(width),
            pl.BlockSpec((width, step), lambda i: (0, i)),
            pl.BlockSpec((1, step), lambda i: (0, i)),
            pl.BlockSpec((step, width), lambda i: (i, 0)),
            whole(width),
        ],
        out_specs=[
            whole(1, rows, cols, width),
            whole(toks, width),
            whole(toks, width),
            whole(2, width),
        ],
        out_shape=[
            sds((1, rows, cols, width)),
            sds((toks, width)),
            sds((toks, width), F32),
            sds((2, width), F32),
        ],
        scratch_shapes=[
            pltpu.VMEM((toks, width), BF),
            pltpu.VMEM((toks, width), F32),
            pltpu.VMEM((toks, width), F32),
        ],
        cost_estimate=cost(11),
        name="mlp",
    )(
        at_tile,
        patch_mask,
        resid,
        hid2,
        cotangent,
        norm2_gain,
        fc1_weight,
        row(fc1_bias),
        fc2_weight,
        fc2_bias,
    )
    hid2_blocks, (branch,) = gather_tiles(hid2, (branch,))

    g1, g2, fb1, fb2 = vec_call(
        ffgrad_kernel,
        [sds((width, units)), sds((units, width)), sds((1, units), F32), sds((1, width), F32)],
        12,
        [
            pltpu.VMEM((toks, width), BF),
            pltpu.VMEM((width, units), F32),
            pltpu.VMEM((units, width), F32),
        ],
        us=9,
    )(at_tile, patch_mask, *hid2_blocks, *ct_blocks, fc1_own, fc1_b_own, fc2_own)
    branch_blocks, (g1, g2) = gather_tiles(branch, (g1, g2))

    dctx, gout, bsum = vec_call(
        outgrad_kernel,
        [sds((total, part)), sds((part, width)), sds((1, width), F32)],
        9,
        us=4,
    )(at_tile, *branch_blocks, out_weight, *ctx)
    direct = direct_sum(imgs)
    (g1, g2), (gout,) = tie((g1, g2), (gout,))
    g1 = g1.reshape(imgs, share, units)
    g2 = g2.reshape(imgs, quarter, width)
    out_cols = [lax.dynamic_slice_in_dim(gout, (tile ^ r) * part, part, 1) for r in range(4)]
    out_rows = scatter_tiles(out_cols)
    if direct:
        line = imgs // 2
        (g1, g2), out_cols = tie((g1, g2), out_cols)
        near1 = exchange_near(g1.reshape(line, 2, share, units))
        far2 = exchange_far(g2.reshape(line, 2, quarter, width))
    dctx, out_rows = tie(dctx, out_rows)
    out_rows = jnp.concatenate(own_order(out_rows, tile), axis=0)

    *mixed, gqkv, vecs = vec_call(
        functools.partial(attnback_kernel, cols=cols),
        [sds((toks, 3 * part))] * 4 + [sds((width, 3 * part)), sds((9, width), F32)],
        10,
        [
            pltpu.VMEM((part, total), F32),
            pltpu.VMEM((part, total), F32),
            pltpu.VMEM((total, 3 * part), BF),
        ],
        us=18,
    )(at_tile, patch_mask, dctx, qkv, lse, hid1, nrm1, w_own, bsum, vec2, fb2)

    vecs = vecs.reshape(9, imgs, share).transpose(1, 0, 2).reshape(imgs, 9 * share)
    count = 9 * share + quarter
    vec_height = -(-count // width)
    spare = jnp.zeros((imgs, vec_height * width - count), F32)
    vecs = jnp.concatenate([vecs, fb1.reshape(imgs, quarter), spare], axis=1).astype(BF)
    at_bucket = jnp.concatenate(
        [
            jnp.concatenate([gqkv, out_rows], axis=1).reshape(imgs, share, width),
            vecs.reshape(imgs, vec_height, width),
        ],
        axis=1,
    )
    if direct:
        near3 = exchange_near(at_bucket.reshape(line, 2, share + vec_height, width))
        near1, (at_bucket,) = tie(near1, (at_bucket,))
        mid1 = total_of(near1).astype(BF)
        far1 = exchange_far(mid1)
        (mixed, far2), (far1[0],) = tie((mixed, far2), (far1[0],))
    mixed_in = scatter_tiles(mixed)
    if direct:
        near2 = exchange_near(total_of(far2).astype(BF)[None])
        near3, (far1[0], mixed_in[0]) = tie(near3, (far1[0], mixed_in[0]))
        mid3 = total_of(near3).astype(BF)
        mixed_in[0], (mid3,) = tie(mixed_in[0], (mid3,))
        far3 = exchange_far(mid3)

    patches_grad = vec_call(
        input_kernel,
        sds((1, rows, cols, width)),
        8,
        [pltpu.VMEM((4, toks, 3 * part), BF), pltpu.VMEM((toks, width), BF)],
        us=5,
    )(at_tile, *mixed_in, qkv_weight, patches, rgrad, norm1_gain)

    if direct:
        fc2_sum = total_of(near2)[0].astype(BF)
        far1, (patches_grad,) = tie(far1, (patches_grad,))
        fc1_sum = total_of(far1).astype(BF)
    else:
        fc1_sum, fc2_sum, at_sum = (plain_sum(b) for b in (g1, g2, at_bucket))
    fc2_pieces, _ = gather_tiles(fc2_sum)
    fc1_pieces, _ = gather_tiles(fc1_sum)
    if direct:
        far3, (fc1_pieces[2], fc2_pieces[2], patches_grad) = tie(
            far3, (fc1_pieces[2], fc2_pieces[2], patches_grad)
        )
        at_sum = total_of(far3).astype(BF)
    fc1_grad, fc2_grad = vec_call(
        ffout_kernel,
        [sds((share, ff), F32), sds((4 * quarter, width), F32)],
        8,
        [pltpu.VMEM((4, max(share, quarter), width), F32)],
        us=3,
    )(at_tile, *fc1_pieces, *fc2_pieces)
    at_pieces, (fc1_grad, fc2_grad) = gather_tiles(at_sum, (fc1_grad, fc2_grad))
    qkv_grad, out_grad, *vec_sums, qv_sum, unit_sum = vec_call(
        attnout_kernel,
        [
            sds((share, 3 * width), F32),
            sds((share, width), F32),
            *[sds((share,), F32)] * 6,
            sds((share, 2), F32),
            sds((4 * quarter,), F32),
        ],
        4,
        [pltpu.VMEM((4, share + vec_height, width), F32)],
        us=3,
    )(at_tile, *at_pieces)
    return (
        layer_out,
        patches_grad,
        vec_sums[0],
        vec_sums[1],
        qkv_grad,
        qv_sum,
        out_grad,
        vec_sums[2],
        vec_sums[3],
        vec_sums[4],
        fc1_grad,
        unit_sum,
        fc2_grad,
        vec_sums[5],
    )


def solution(mesh):
    tiled = P("imgs", "rows", "cols", None)
    in_specs = (tiled, P("imgs", None, None)) + (P(),) * 12 + (tiled,)
    mat = P("imgs", None)
    vec = P("imgs")
    out_specs = (tiled, tiled, vec, vec, mat, mat, mat, vec, vec, vec, mat, vec, mat, vec)
    return jax.shard_map(layer, mesh=mesh, in_specs=in_specs, out_specs=out_specs, check_vma=False)
```

```python
import functools

import jax
import jax.numpy as jnp
from jax import lax
from jax.experimental import pallas as pl
from jax.experimental.pallas import tpu as pltpu
from jax.sharding import PartitionSpec as P

HEADS = 12
NORM_EPS = 1e-06
MASKED_SCORE = -1e30
GROUP = ("rows", "cols")
BF = jnp.bfloat16
F32 = jnp.float32


def dot(left, right, dims):
    return lax.dot_general(left, right, (dims, ((), ())), preferred_element_type=F32)


def mm(left, right):
    return dot(left, right, ((1,), (0,)))


def mm_nt(left, right):
    return dot(left, right, ((1,), (1,)))


def mm_tn(left, right):
    return dot(left, right, ((0,), (0,)))


def to_peer(value, rel):
    if rel == 1:
        return lax.ppermute(value, "cols", [(0, 1), (1, 0)])
    if rel == 2:
        return lax.ppermute(value, "rows", [(0, 1), (1, 0)])
    return lax.ppermute(value, GROUP, [(i, i ^ 3) for i in range(4)])


def tie(values, others):
    flat, tree = jax.tree.flatten((values, others))
    return jax.tree.unflatten(tree, lax.optimization_barrier(flat))


def gather_tiles(value, others=()):
    across = to_peer(value, 2)
    beside = to_peer(value, 1)
    across, others = tie(across, others)
    return [value, beside, across, to_peer(across, 1)], others


def scatter_tiles(blocks):
    return [blocks[0], to_peer(blocks[1], 1), to_peer(blocks[2], 2), to_peer(blocks[3], 3)]


def norm_stats(values):
    mean_val = jnp.mean(values, axis=-1, keepdims=True)
    centred = values - mean_val
    var_val = jnp.mean(centred * centred, axis=-1, keepdims=True)
    inv = lax.rsqrt(var_val + NORM_EPS)
    return centred * inv, inv


def norm_back(grads, normed, inv, gain):
    g = grads * gain
    return (
        g
        - jnp.mean(g, axis=-1, keepdims=True)
        - normed * jnp.mean(g * normed, axis=-1, keepdims=True)
    ) * inv


def gelu_parts(x):
    cdf = 0.5 * (1.0 + lax.erf(x * 0.7071067811865476))
    pdf = jnp.exp(-0.5 * x * x) * 0.3989422804014327
    return x * cdf, cdf + x * pdf


def exchange_near(parts):
    side = lax.axis_index("imgs") % 2
    count = lax.axis_size("imgs")
    send = lax.dynamic_index_in_dim(parts, 1 - side, 1, keepdims=False)
    keep = lax.dynamic_index_in_dim(parts, side, 1, keepdims=False)
    return keep, lax.ppermute(send, "imgs", [(i, i ^ 1) for i in range(count)])


def exchange_far(parts):
    count = lax.axis_size("imgs")
    place = lax.axis_index("imgs") // 2
    got = [lax.dynamic_index_in_dim(parts, place, 0, keepdims=False)]
    for k in range(count // 2 - 1, 0, -1):
        send = lax.dynamic_index_in_dim(parts, place ^ k, 0, keepdims=False)
        got.append(lax.ppermute(send, "imgs", [(i, i ^ (2 * k)) for i in range(count)]))
    return got


def total_of(blocks):
    return functools.reduce(jnp.add, [b.astype(F32) for b in blocks])


def direct_sum(imgs):
    return imgs <= 8 and imgs & (imgs - 1) == 0


def plain_sum(parts):
    return lax.psum_scatter(parts, "imgs", scatter_dimension=0, tiled=False)


SMEM = pl.BlockSpec(memory_space=pltpu.SMEM)
VMEM = pl.BlockSpec(memory_space=pltpu.VMEM)
PAD = 16


def vec_call(kernel, outs, n_in, scratch=(), us=5):
    return pl.pallas_call(
        kernel,
        out_shape=outs,
        in_specs=[SMEM] + [VMEM] * n_in,
        out_specs=jax.tree.map(lambda _: VMEM, outs),
        scratch_shapes=list(scratch),
        cost_estimate=cost(us),
    )


def cost(us):
    return pl.CostEstimate(flops=us * 10**9, transcendentals=0, bytes_accessed=us * 10**6)


def sds(shape, dtype=BF):
    return jax.ShapeDtypeStruct(shape, dtype)


def load_tile(ref, scratch, at):
    rows, cols, width = ref.shape[1:]
    scratch[at : at + rows * PAD, :] = jnp.zeros((rows * PAD, width), scratch.dtype)
    for i in range(rows):
        scratch[at + i * PAD : at + i * PAD + cols, :] = ref[0, i]


def store_tile(ref, value):
    rows, cols, _ = ref.shape[1:]
    for i in range(rows):
        ref[0, i] = value[i * PAD : i * PAD + cols, :]


def mask_edges(mask):
    m = mask[0].astype(F32)
    high = jnp.sum(m[:, 0:1], axis=0, keepdims=True)
    wide = jnp.sum(m[0:1, :], axis=1, keepdims=True)
    return high, wide


def keep_tokens(edges, place, rows, cols, axis):
    toks = rows * PAD
    shape = (toks, 1) if axis == 0 else (1, toks)
    tok = lax.broadcasted_iota(jnp.int32, shape, axis)
    c = tok & (PAD - 1)
    r = ((tok >> 4) + (place >> 1) * rows).astype(F32)
    at = (c + (place & 1) * cols).astype(F32)
    ok = (c < cols) & (r < edges[0]) & (at < edges[1])
    return jnp.where(ok, 1.0, 0.0).astype(F32)


def mask_row(tile, mask, rows, cols):
    edges = mask_edges(mask)
    keep = [keep_tokens(edges, tile[0] ^ r, rows, cols, 1) for r in range(4)]
    return jnp.where(jnp.concatenate(keep, axis=1) > 0, 0.0, MASKED_SCORE).astype(F32)


def vec_row(ref):
    return ref[...].reshape(1, -1)


def heads_kernel(tile, qkv_w, qv_b, w_own, b_own):
    width = qv_b.shape[1]
    part = width // 4
    for g in range(4):

        @pl.when(tile[0] == g)
        def _():
            for i in range(3):
                src = i * width + g * part
                w_own[:, i * part : (i + 1) * part] = qkv_w[:, src : src + part]
            b_own[:, :part] = qv_b[0:1, g * part : (g + 1) * part]
            b_own[:, part : 2 * part] = jnp.zeros((1, part), F32)
            b_own[:, 2 * part :] = qv_b[1:2, g * part : (g + 1) * part]


def units_kernel(tile, fc1, fc1_b, fc1_own, fc1_b_own, *, quarter):
    for g in range(4):

        @pl.when(tile[0] == g)
        def _():
            for i in range(fc1.shape[1] // (4 * quarter)):
                src = (4 * i + g) * quarter
                dst = i * quarter
                fc1_own[:, dst : dst + quarter] = fc1[:, src : src + quarter]
                fc1_b_own[:, dst : dst + quarter] = fc1_b[:, src : src + quarter]


def attn_kernel(
    tile, mask, x0, x1, x2, x3, gain, shift, w, bias, hid, nrm, qkv, lse, c0, c1, c2, c3, xs, ctx
):
    rows, cols, width = x0.shape[1:]
    toks = rows * PAD
    part = w.shape[1] // 3
    dim = width // HEADS
    scale = dim ** (-0.5)
    for r, ref in enumerate((x0, x1, x2, x3)):
        load_tile(ref, xs, r * toks)

    normed, _ = norm_stats(xs[...].astype(F32))
    nrm[...] = normed.astype(BF)
    hid[...] = (normed * vec_row(gain) + vec_row(shift)).astype(BF)
    qkv[...] = (mm(hid[...], w[...]) + bias[...]).astype(BF)
    masked = mask_row(tile, mask, rows, cols)

    def attend(r, carry):
        at = pl.ds(pl.multiple_of(r * toks, toks), toks)
        outs = []
        for h in range(part // dim):
            q = qkv[at, h * dim : (h + 1) * dim]
            k = qkv[:, part + h * dim : part + (h + 1) * dim]
            v = qkv[:, 2 * part + h * dim : 2 * part + (h + 1) * dim]
            s = mm_nt(q * scale, k) + masked
            top = jnp.max(s, axis=-1, keepdims=True)
            e = jnp.exp(s - top)
            total = jnp.sum(e, axis=-1, keepdims=True)
            outs.append((mm(e.astype(BF), v) * (1.0 / total)).astype(BF))
            lse[at, h : h + 1] = top + jnp.log(total)
        ctx[r] = jnp.concatenate(outs, axis=1)
        return carry

    lax.fori_loop(0, 4, attend, 0)
    for r, ref in enumerate((c0, c1, c2, c3)):
        ref[...] = ctx[r]


def branch_kernel(tile, c0, c1, c2, c3, wo, bo, x, gain, shift, resid, hid, xs):
    part = c0.shape[1]
    load_tile(x, xs, 0)
    acc = xs[...].astype(F32) + vec_row(bo)
    for r, ref in enumerate((c0, c1, c2, c3)):
        at = pl.multiple_of((tile[0] ^ r) * part, part)
        acc = acc + mm(ref[...], wo[pl.ds(at, part), :])
    resid[...] = acc
    normed, _ = norm_stats(acc)
    hid[...] = (normed * vec_row(gain) + vec_row(shift)).astype(BF)


def mlp_kernel(
    tile, mask, resid, hid, ct, gain, fc1, fc1_b, fc2, fc2_b, out, branch, rgrad, vecs, up, acc, nacc
):
    step = pl.program_id(0)
    rows, cols, _ = ct.shape[1:]

    @pl.when(step == 0)
    def _():
        load_tile(ct, up, 0)
        up[...] = (up[...].astype(F32) * keep_tokens(mask_edges(mask), tile[0], rows, cols, 0)).astype(BF)
        acc[...] = jnp.zeros_like(acc)
        nacc[...] = jnp.zeros_like(nacc)

    act, dgelu = gelu_parts(mm(hid[...], fc1[...]) + fc1_b[...])
    acc[...] += mm(act.astype(BF), fc2[...])
    inner = (mm_nt(up[...], fc2[...]) * dgelu).astype(BF)
    nacc[...] += mm_nt(inner, fc1[...])

    @pl.when(step == pl.num_programs(0) - 1)
    def _():
        res = resid[...]
        keep = keep_tokens(mask_edges(mask), tile[0], rows, cols, 0)
        store_tile(out, (keep * (res + acc[...] + vec_row(fc2_b))).astype(BF))
        normed, inv = norm_stats(res)
        n = nacc[...]
        vecs[0:1, :] = jnp.sum(n * normed, axis=0, keepdims=True)
        vecs[1:2, :] = jnp.sum(n, axis=0, keepdims=True)
        grad = up[...].astype(F32) + norm_back(n, normed, inv, vec_row(gain))
        rgrad[...] = grad
        branch[...] = grad.astype(BF)


def ffgrad_kernel(
    tile, mask, h0, h1, h2, h3, t0, t1, t2, t3, fc1, fc1_b, fc2, g1, g2, b1, b2, up, a1, a2
):
    rows, cols, _ = t0.shape[1:]
    edges = mask_edges(mask)
    hids = (h0, h1, h2, h3)
    for r, ref in enumerate((t0, t1, t2, t3)):
        load_tile(ref, up, 0)
        wide = up[...].astype(F32) * keep_tokens(edges, tile[0] ^ r, rows, cols, 0)
        low = wide.astype(BF)
        h = hids[r][...]
        act, dgelu = gelu_parts(mm(h, fc1[...]) + fc1_b[...])
        inner = (mm_nt(low, fc2[...]) * dgelu).astype(BF)
        d1 = mm_tn(h, inner)
        d2 = mm_tn(act.astype(BF), low)
        s1 = jnp.sum(inner.astype(F32), axis=0, keepdims=True)
        s2 = jnp.sum(wide, axis=0, keepdims=True)
        if r == 0:
            a1[...], a2[...], b1[...], b2[...] = d1, d2, s1, s2
        elif r < 3:
            a1[...] += d1
            a2[...] += d2
            b1[...] += s1
            b2[...] += s2
        else:
            g1[...] = (a1[...] + d1).astype(BF)
            g2[...] = (a2[...] + d2).astype(BF)
            b1[...] += s1
            b2[...] += s2


def outgrad_kernel(tile, b0, b1, b2, b3, wo, c0, c1, c2, c3, dctx, gout, bsum):
    toks, part = c0.shape
    at = pl.multiple_of(tile[0] * part, part)
    w = wo[pl.ds(at, part), :]
    ctx = (c0, c1, c2, c3)
    acc = None
    total = None
    for r, ref in enumerate((b0, b1, b2, b3)):
        low = ref[...]
        dctx[r * toks : (r + 1) * toks, :] = mm_nt(low, w).astype(BF)
        d = mm_tn(ctx[r][...], low)
        s = jnp.sum(low.astype(F32), axis=0, keepdims=True)
        acc = d if r == 0 else acc + d
        total = s if r == 0 else total + s
    gout[...] = acc.astype(BF)
    bsum[...] = total


def attnback_kernel(
    tile,
    mask,
    dctx,
    qkv,
    lse,
    hid,
    nrm,
    w,
    bsum,
    vec2,
    fb2,
    o0,
    o1,
    o2,
    o3,
    m0,
    m1,
    m2,
    m3,
    grads,
    vecs,
    dk,
    dv,
    mix,
    *,
    cols,
):
    total, three = qkv.shape
    part = three // 3
    toks = total // 4
    dim = hid.shape[1] // HEADS
    rows = toks // PAD
    scale = dim ** (-0.5)
    masked = mask_row(tile, mask, rows, cols)
    dk[...] = jnp.zeros_like(dk)
    dv[...] = jnp.zeros_like(dv)

    def attend(r, carry):
        at = pl.ds(pl.multiple_of(r * toks, toks), toks)
        dqs = []
        q_all = qkv[at, :part] * scale
        do_all = dctx[at, :]
        q_turned = q_all.T
        do_turned = do_all.T
        for h in range(part // dim):
            at_h = slice(h * dim, (h + 1) * dim)
            k = qkv[:, part + h * dim : part + (h + 1) * dim]
            v = qkv[:, 2 * part + h * dim : 2 * part + (h + 1) * dim]
            p = jnp.exp(mm_nt(q_all[:, at_h], k) + masked - lse[at, h : h + 1])
            dp = mm_nt(do_all[:, at_h], v)
            ds = (p * (dp - jnp.sum(dp * p, axis=-1, keepdims=True))).astype(BF)
            dqs.append((mm(ds, k) * scale).astype(BF))
            dv[at_h, :] += mm(do_turned[at_h], p.astype(BF))
            dk[at_h, :] += mm(q_turned[at_h], ds)
        mix[at, :part] = jnp.concatenate(dqs, axis=1)
        return carry

    lax.fori_loop(0, 4, attend, 0)
    mix[:, part : 2 * part] = dk[...].T.astype(BF)
    mix[:, 2 * part :] = dv[...].T.astype(BF)
    grads[:, : 3 * part] = mm_tn(hid[...], mix[...]).astype(BF)
    for r, ref in enumerate((o0, o1, o2, o3)):
        at = pl.multiple_of((tile[0] ^ r) * part, part)
        grads[pl.ds(at, part), 3 * part :] = ref[...]
    for r, ref in enumerate((m0, m1, m2, m3)):
        ref[...] = mix[r * toks : (r + 1) * toks, :]
    col_sum = jnp.sum(mix[...].astype(F32), axis=0, keepdims=True)
    chunk = 256
    for i in range(w.shape[0] // chunk):
        at = slice(i * chunk, (i + 1) * chunk)
        n = mm_nt(mix[...], w[at, :])
        vecs[0:1, at] = jnp.sum(n * nrm[:, at].astype(F32), axis=0, keepdims=True)
        vecs[1:2, at] = jnp.sum(n, axis=0, keepdims=True)
    slot = lax.broadcasted_iota(jnp.int32, (1, 4 * part), 1)
    own = (slot >= tile[0] * part) & (slot < (tile[0] + 1) * part)
    lone = jnp.where(tile[0] == 0, 1.0, 0.0).astype(F32)
    for i in range(3):
        piece = col_sum[:, i * part : (i + 1) * part]
        vecs[2 + i : 3 + i, :] = jnp.where(own, jnp.concatenate([piece] * 4, axis=1), 0.0)
    vecs[5:6, :] = bsum[...] * lone
    vecs[6:8, :] = vec2[...]
    vecs[8:9, :] = fb2[...] * lone


def input_kernel(tile, m0, m1, m2, m3, w, x, rgrad, gain, out, ms, xs):
    part = m0.shape[1] // 3
    for r, ref in enumerate((m0, m1, m2, m3)):
        ms[r] = ref[...]
    tiles = [ms[tile[0] ^ g] for g in range(4)]
    full = jnp.concatenate(
        [m[:, i * part : (i + 1) * part] for i in range(3) for m in tiles], axis=1
    )
    n = mm_nt(full, w[...])
    load_tile(x, xs, 0)
    normed, inv = norm_stats(xs[...].astype(F32))
    store_tile(out, (rgrad[...] + norm_back(n, normed, inv, vec_row(gain))).astype(BF))


def fc1out_kernel(tile, p0, p1, p2, p3, fc1, ps, *, quarter):
    for r, ref in enumerate((p0, p1, p2, p3)):
        ps[r] = ref[...].astype(F32)
    for g in range(4):
        piece = ps[tile[0] ^ g]
        for i in range(fc1.shape[1] // (4 * quarter)):
            dst = (4 * i + g) * quarter
            fc1[:, dst : dst + quarter] = piece[:, i * quarter : (i + 1) * quarter]


def fc2out_kernel(tile, p0, p1, p2, p3, fc2, ps):
    quarter = fc2.shape[0] // 4
    for r, ref in enumerate((p0, p1, p2, p3)):
        ps[r] = ref[...].astype(F32)
    for g in range(4):
        fc2[g * quarter : (g + 1) * quarter, :] = ps[tile[0] ^ g]


def attnout_kernel(
    tile, p0, p1, p2, p3, gqkv, gout, v0, v1, v2, v4, v5, v6, v7, v8, units, ps
):
    rows, width = gout.shape
    part = width // 4
    quarter = units.shape[0] // 4
    height = ps.shape[1] - rows
    for r, ref in enumerate((p0, p1, p2, p3)):
        ps[r] = ref[...].astype(F32)
    total = None
    tails = []
    for g in range(4):
        piece = ps[tile[0] ^ g]
        for i in range(3):
            dst = i * width + g * part
            gqkv[:, dst : dst + part] = piece[:rows, i * part : (i + 1) * part]
        gout[:, g * part : (g + 1) * part] = piece[:rows, 3 * part :]
        tail = jnp.concatenate([piece[rows + j : rows + j + 1] for j in range(height)], axis=1)
        total = tail if g == 0 else total + tail
        tails.append(tail[:, 9 * rows : 9 * rows + quarter])
    places = ((0, v0), (1, v1), (2, v2), (4, v4), (5, v5), (6, v6), (7, v7), (8, v8))
    for i, ref in places:
        ref[...] = total[0, i * rows : (i + 1) * rows]
    units[...] = jnp.concatenate(tails, axis=1)[0]


def layer(
    patches,
    patch_mask,
    norm1_gain,
    norm1_shift,
    qkv_weight,
    qv_bias,
    out_weight,
    out_bias,
    norm2_gain,
    norm2_shift,
    fc1_weight,
    fc1_bias,
    fc2_weight,
    fc2_bias,
    cotangent,
):
    _, rows, cols, width = patches.shape
    ff = fc1_weight.shape[1]
    imgs = lax.axis_size("imgs")
    part = width // 4
    units = ff // 4
    quarter = units // imgs
    share = width // imgs
    toks = rows * PAD
    total = 4 * toks
    tile = lax.axis_index("rows") * 2 + lax.axis_index("cols")
    at_tile = tile.reshape(1).astype(jnp.int32)

    def row(v):
        return v.reshape(1, -1)

    steps = 4
    w_own, b_own = pl.pallas_call(
        heads_kernel,
        grid=(steps,),
        in_specs=[
            SMEM,
            pl.BlockSpec((width // steps, 3 * width), lambda i: (i, 0)),
            pl.BlockSpec((2, width), lambda i: (0, 0)),
        ],
        out_specs=[
            pl.BlockSpec((width // steps, 3 * part), lambda i: (i, 0)),
            pl.BlockSpec((1, 3 * part), lambda i: (0, 0)),
        ],
        out_shape=[sds((width, 3 * part)), sds((1, 3 * part), F32)],
        cost_estimate=cost(4),
        name="heads",
    )(at_tile, qkv_weight, qv_bias.T)
    fc1_own, fc1_b_own = pl.pallas_call(
        functools.partial(units_kernel, quarter=quarter),
        grid=(steps,),
        in_specs=[
            SMEM,
            pl.BlockSpec((width // steps, ff), lambda i: (i, 0)),
            pl.BlockSpec((1, ff), lambda i: (0, 0)),
        ],
        out_specs=[
            pl.BlockSpec((width // steps, units), lambda i: (i, 0)),
            pl.BlockSpec((1, units), lambda i: (0, 0)),
        ],
        out_shape=[sds((width, units)), sds((1, units), F32)],
        cost_estimate=cost(4),
        name="units",
    )(at_tile, fc1_weight, row(fc1_bias))
    x_blocks, (w_own, b_own, fc1_own) = gather_tiles(patches, (w_own, b_own, fc1_own))

    hid1, nrm1, qkv, lse, *ctx = vec_call(
        attn_kernel,
        [
            sds((total, width)),
            sds((total, width)),
            sds((total, 3 * part)),
            sds((total, 128), F32),
        ]
        + [sds((toks, part))] * 4,
        9,
        [pltpu.VMEM((total, width), BF), pltpu.VMEM((4, toks, part), BF)],
        us=13,
    )(at_tile, patch_mask, *x_blocks, norm1_gain, norm1_shift, w_own, b_own)
    ct_blocks, ctx = gather_tiles(cotangent, ctx)
    later_tile, _ = tie(at_tile, ctx)

    fc2_own = lax.dynamic_index_in_dim(
        fc2_weight.reshape(imgs, 4, quarter, width), later_tile[0], 1, keepdims=False
    ).reshape(units, width)

    ctx_in = scatter_tiles(ctx)
    ctx_in, (fc2_own,) = tie(ctx_in, (fc2_own,))
    resid, hid2 = vec_call(
        branch_kernel,
        [sds((toks, width), F32), sds((toks, width))],
        9,
        [pltpu.VMEM((toks, width), BF)],
        us=3,
    )(at_tile, *ctx_in, out_weight, out_bias, patches, norm2_gain, norm2_shift)

    chunks = 4
    step = ff // chunks

    def whole(*shape):
        return pl.BlockSpec(shape, lambda i: (0,) * len(shape))

    layer_out, branch, rgrad, vec2 = pl.pallas_call(
        mlp_kernel,
        grid=(chunks,),
        in_specs=[
            SMEM,
            whole(*patch_mask.shape),
            whole(toks, width),
            whole(toks, width),
            whole(1, rows, cols, width),
            whole(width),
            pl.BlockSpec((width, step), lambda i: (0, i)),
            pl.BlockSpec((1, step), lambda i: (0, i)),
            pl.BlockSpec((step, width), lambda i: (i, 0)),
            whole(width),
        ],
        out_specs=[
            whole(1, rows, cols, width),
            whole(toks, width),
            whole(toks, width),
            whole(2, width),
        ],
        out_shape=[
            sds((1, rows, cols, width)),
            sds((toks, width)),
            sds((toks, width), F32),
            sds((2, width), F32),
        ],
        scratch_shapes=[
            pltpu.VMEM((toks, width), BF),
            pltpu.VMEM((toks, width), F32),
            pltpu.VMEM((toks, width), F32),
        ],
        cost_estimate=cost(11),
        name="mlp",
    )(
        at_tile,
        patch_mask,
        resid,
        hid2,
        cotangent,
        norm2_gain,
        fc1_weight,
        row(fc1_bias),
        fc2_weight,
        fc2_bias,
    )
    hid2_blocks, (branch,) = gather_tiles(hid2, (branch,))

    g1, g2, fb1, fb2 = vec_call(
        ffgrad_kernel,
        [sds((width, units)), sds((units, width)), sds((1, units), F32), sds((1, width), F32)],
        12,
        [
            pltpu.VMEM((toks, width), BF),
            pltpu.VMEM((width, units), F32),
            pltpu.VMEM((units, width), F32),
        ],
        us=9,
    )(at_tile, patch_mask, *hid2_blocks, *ct_blocks, fc1_own, fc1_b_own, fc2_own)
    branch_blocks, (g1, g2) = gather_tiles(branch, (g1, g2))

    dctx, gout, bsum = vec_call(
        outgrad_kernel,
        [sds((total, part)), sds((part, width)), sds((1, width), F32)],
        9,
        us=4,
    )(at_tile, *branch_blocks, out_weight, *ctx)
    direct = direct_sum(imgs)
    (g1, g2), (gout,) = tie((g1, g2), (gout,))
    g1 = g1.reshape(imgs, share, units)
    g2 = g2.reshape(imgs, quarter, width)
    out_cols = [lax.dynamic_slice_in_dim(gout, (tile ^ r) * part, part, 1) for r in range(4)]
    out_rows = scatter_tiles(out_cols)
    if direct:
        line = imgs // 2
        (g1, g2), out_cols = tie((g1, g2), out_cols)
        near1 = exchange_near(g1.reshape(line, 2, share, units))
        far2 = exchange_far(g2.reshape(line, 2, quarter, width))
    dctx, out_rows = tie(dctx, out_rows)

    *mixed, grads, vecs = vec_call(
        functools.partial(attnback_kernel, cols=cols),
        [sds((toks, 3 * part))] * 4 + [sds((width, width)), sds((9, width), F32)],
        14,
        [
            pltpu.VMEM((part, total), F32),
            pltpu.VMEM((part, total), F32),
            pltpu.VMEM((total, 3 * part), BF),
        ],
        us=18,
    )(at_tile, patch_mask, dctx, qkv, lse, hid1, nrm1, w_own, bsum, vec2, fb2, *out_rows)

    vecs = vecs.reshape(9, imgs, share).transpose(1, 0, 2).reshape(imgs, 9 * share)
    count = 9 * share + quarter
    vec_height = -(-count // width)
    spare = jnp.zeros((imgs, vec_height * width - count), F32)
    vecs = jnp.concatenate([vecs, fb1.reshape(imgs, quarter), spare], axis=1).astype(BF)
    at_bucket = jnp.concatenate(
        [grads.reshape(imgs, share, width), vecs.reshape(imgs, vec_height, width)], axis=1
    )
    if direct:
        near3 = exchange_near(at_bucket.reshape(line, 2, share + vec_height, width))
        near1, (at_bucket,) = tie(near1, (at_bucket,))
        mid1 = total_of(near1).astype(BF)
        far1 = exchange_far(mid1)
        far2, (far1[0],) = tie(far2, (far1[0],))
    mixed_in = scatter_tiles(mixed)
    if direct:
        near2 = exchange_near(total_of(far2).astype(BF)[None])
        near3, (far1[0], mixed_in[0]) = tie(near3, (far1[0], mixed_in[0]))
        mid3 = total_of(near3).astype(BF)
        mixed_in[0], (mid3,) = tie(mixed_in[0], (mid3,))
        far3 = exchange_far(mid3)

    patches_grad = vec_call(
        input_kernel,
        sds((1, rows, cols, width)),
        8,
        [pltpu.VMEM((4, toks, 3 * part), BF), pltpu.VMEM((toks, width), BF)],
        us=5,
    )(at_tile, *mixed_in, qkv_weight, patches, rgrad, norm1_gain)

    if direct:
        fc2_sum = total_of(near2)[0].astype(BF)
        far1, (patches_grad,) = tie(far1, (patches_grad,))
        fc1_sum = total_of(far1).astype(BF)
    else:
        fc1_sum, fc2_sum, at_sum = (plain_sum(b) for b in (g1, g2, at_bucket))
    fc2_pieces, _ = gather_tiles(fc2_sum)
    fc1_pieces, _ = gather_tiles(fc1_sum)
    if direct:
        far3, (patches_grad, fc2_pieces[2]) = tie(far3, (patches_grad, fc2_pieces[2]))
        at_sum = total_of(far3).astype(BF)
    fc2_grad = vec_call(
        fc2out_kernel,
        sds((4 * quarter, width), F32),
        4,
        [pltpu.VMEM((4, quarter, width), F32)],
        us=2,
    )(at_tile, *fc2_pieces)
    fc1_grad = vec_call(
        functools.partial(fc1out_kernel, quarter=quarter),
        sds((share, ff), F32),
        4,
        [pltpu.VMEM((4, share, units), F32)],
        us=2,
    )(at_tile, *fc1_pieces)
    at_pieces, (fc1_grad, fc2_grad) = gather_tiles(at_sum, (fc1_grad, fc2_grad))
    qkv_grad, out_grad, *vec_sums, unit_sum = vec_call(
        attnout_kernel,
        [
            sds((share, 3 * width), F32),
            sds((share, width), F32),
            *[sds((share,), F32)] * 8,
            sds((4 * quarter,), F32),
        ],
        4,
        [pltpu.VMEM((4, share + vec_height, width), F32)],
        us=3,
    )(at_tile, *at_pieces)
    return (
        layer_out,
        patches_grad,
        vec_sums[0],
        vec_sums[1],
        qkv_grad,
        jnp.stack([vec_sums[2], vec_sums[3]], axis=1),
        out_grad,
        vec_sums[4],
        vec_sums[5],
        vec_sums[6],
        fc1_grad,
        unit_sum,
        fc2_grad,
        vec_sums[7],
    )


def solution(mesh):
    tiled = P("imgs", "rows", "cols", None)
    in_specs = (tiled, P("imgs", None, None)) + (P(),) * 12 + (tiled,)
    mat = P("imgs", None)
    vec = P("imgs")
    out_specs = (tiled, tiled, vec, vec, mat, mat, mat, vec, vec, vec, mat, vec, mat, vec)
    return jax.shard_map(layer, mesh=mesh, in_specs=in_specs, out_specs=out_specs, check_vma=False)
```

```python
import functools

import jax
import jax.numpy as jnp
from jax import lax
from jax.experimental import pallas as pl
from jax.experimental.pallas import tpu as pltpu
from jax.sharding import PartitionSpec as P

HEADS = 12
NORM_EPS = 1e-06
MASKED_SCORE = -1e30
GROUP = ("rows", "cols")
BF = jnp.bfloat16
F32 = jnp.float32


def dot(left, right, dims):
    return lax.dot_general(left, right, (dims, ((), ())), preferred_element_type=F32)


def mm(left, right):
    return dot(left, right, ((1,), (0,)))


def mm_nt(left, right):
    return dot(left, right, ((1,), (1,)))


def mm_tn(left, right):
    return dot(left, right, ((0,), (0,)))


def to_peer(value, rel):
    if rel == 1:
        return lax.ppermute(value, "cols", [(0, 1), (1, 0)])
    if rel == 2:
        return lax.ppermute(value, "rows", [(0, 1), (1, 0)])
    return lax.ppermute(value, GROUP, [(i, i ^ 3) for i in range(4)])


def tie(values, others):
    flat, tree = jax.tree.flatten((values, others))
    return jax.tree.unflatten(tree, lax.optimization_barrier(flat))


def gather_tiles(value, others=()):
    across = to_peer(value, 2)
    beside = to_peer(value, 1)
    across, others = tie(across, others)
    return [value, beside, across, to_peer(across, 1)], others


def scatter_tiles(blocks):
    return [blocks[0], to_peer(blocks[1], 1), to_peer(blocks[2], 2), to_peer(blocks[3], 3)]


def norm_stats(values):
    mean_val = jnp.mean(values, axis=-1, keepdims=True)
    centred = values - mean_val
    var_val = jnp.mean(centred * centred, axis=-1, keepdims=True)
    inv = lax.rsqrt(var_val + NORM_EPS)
    return centred * inv, inv


def norm_back(grads, normed, inv, gain):
    g = grads * gain
    return (
        g
        - jnp.mean(g, axis=-1, keepdims=True)
        - normed * jnp.mean(g * normed, axis=-1, keepdims=True)
    ) * inv


def gelu_parts(x):
    cdf = 0.5 * (1.0 + lax.erf(x * 0.7071067811865476))
    pdf = jnp.exp(-0.5 * x * x) * 0.3989422804014327
    return x * cdf, cdf + x * pdf


def exchange_near(parts):
    side = lax.axis_index("imgs") % 2
    count = lax.axis_size("imgs")
    send = lax.dynamic_index_in_dim(parts, 1 - side, 1, keepdims=False)
    keep = lax.dynamic_index_in_dim(parts, side, 1, keepdims=False)
    return keep, lax.ppermute(send, "imgs", [(i, i ^ 1) for i in range(count)])


def exchange_far(parts):
    count = lax.axis_size("imgs")
    place = lax.axis_index("imgs") // 2
    got = [lax.dynamic_index_in_dim(parts, place, 0, keepdims=False)]
    for k in range(count // 2 - 1, 0, -1):
        send = lax.dynamic_index_in_dim(parts, place ^ k, 0, keepdims=False)
        got.append(lax.ppermute(send, "imgs", [(i, i ^ (2 * k)) for i in range(count)]))
    return got


def total_of(blocks):
    return functools.reduce(jnp.add, [b.astype(F32) for b in blocks])


def direct_sum(imgs):
    return imgs <= 8 and imgs & (imgs - 1) == 0


def plain_sum(parts):
    return lax.psum_scatter(parts, "imgs", scatter_dimension=0, tiled=False)


SMEM = pl.BlockSpec(memory_space=pltpu.SMEM)
VMEM = pl.BlockSpec(memory_space=pltpu.VMEM)
PAD = 16


def vec_call(kernel, outs, n_in, scratch=(), us=5):
    return pl.pallas_call(
        kernel,
        out_shape=outs,
        in_specs=[SMEM] + [VMEM] * n_in,
        out_specs=jax.tree.map(lambda _: VMEM, outs),
        scratch_shapes=list(scratch),
        cost_estimate=cost(us),
    )


def cost(us):
    return pl.CostEstimate(flops=us * 10**9, transcendentals=0, bytes_accessed=us * 10**6)


def sds(shape, dtype=BF):
    return jax.ShapeDtypeStruct(shape, dtype)


def load_tile(ref, scratch, at):
    rows, cols, width = ref.shape[1:]
    scratch[at : at + rows * PAD, :] = jnp.zeros((rows * PAD, width), scratch.dtype)
    for i in range(rows):
        scratch[at + i * PAD : at + i * PAD + cols, :] = ref[0, i]


def store_tile(ref, value):
    rows, cols, _ = ref.shape[1:]
    for i in range(rows):
        ref[0, i] = value[i * PAD : i * PAD + cols, :]


def mask_edges(mask):
    m = mask[0].astype(F32)
    high = jnp.sum(m[:, 0:1], axis=0, keepdims=True)
    wide = jnp.sum(m[0:1, :], axis=1, keepdims=True)
    return high, wide


def keep_tokens(edges, place, rows, cols, axis):
    toks = rows * PAD
    shape = (toks, 1) if axis == 0 else (1, toks)
    tok = lax.broadcasted_iota(jnp.int32, shape, axis)
    c = tok & (PAD - 1)
    r = ((tok >> 4) + (place >> 1) * rows).astype(F32)
    at = (c + (place & 1) * cols).astype(F32)
    ok = (c < cols) & (r < edges[0]) & (at < edges[1])
    return jnp.where(ok, 1.0, 0.0).astype(F32)


def mask_row(tile, mask, rows, cols):
    edges = mask_edges(mask)
    keep = [keep_tokens(edges, tile[0] ^ r, rows, cols, 1) for r in range(4)]
    return jnp.where(jnp.concatenate(keep, axis=1) > 0, 0.0, MASKED_SCORE).astype(F32)


def vec_row(ref):
    return ref[...].reshape(1, -1)


def heads_kernel(tile, qkv_w, qv_b, w_own, b_own):
    width = qv_b.shape[1]
    part = width // 4
    for g in range(4):

        @pl.when(tile[0] == g)
        def _():
            for i in range(3):
                src = i * width + g * part
                w_own[:, i * part : (i + 1) * part] = qkv_w[:, src : src + part]
            b_own[:, :part] = qv_b[0:1, g * part : (g + 1) * part]
            b_own[:, part : 2 * part] = jnp.zeros((1, part), F32)
            b_own[:, 2 * part :] = qv_b[1:2, g * part : (g + 1) * part]


def units_kernel(tile, fc1, fc1_b, fc1_own, fc1_b_own, *, quarter):
    for g in range(4):

        @pl.when(tile[0] == g)
        def _():
            for i in range(fc1.shape[1] // (4 * quarter)):
                src = (4 * i + g) * quarter
                dst = i * quarter
                fc1_own[:, dst : dst + quarter] = fc1[:, src : src + quarter]
                fc1_b_own[:, dst : dst + quarter] = fc1_b[:, src : src + quarter]


def attn_kernel(
    tile, mask, x0, x1, x2, x3, gain, shift, w, bias, hid, nrm, qkv, lse, c0, c1, c2, c3, xs, ctx
):
    rows, cols, width = x0.shape[1:]
    toks = rows * PAD
    part = w.shape[1] // 3
    dim = width // HEADS
    scale = dim ** (-0.5)
    for r, ref in enumerate((x0, x1, x2, x3)):
        load_tile(ref, xs, r * toks)

    normed, _ = norm_stats(xs[...].astype(F32))
    nrm[...] = normed.astype(BF)
    hid[...] = (normed * vec_row(gain) + vec_row(shift)).astype(BF)
    qkv[...] = (mm(hid[...], w[...]) + bias[...]).astype(BF)
    masked = mask_row(tile, mask, rows, cols)

    def attend(r, carry):
        at = pl.ds(pl.multiple_of(r * toks, toks), toks)
        outs = []
        for h in range(part // dim):
            q = qkv[at, h * dim : (h + 1) * dim]
            k = qkv[:, part + h * dim : part + (h + 1) * dim]
            v = qkv[:, 2 * part + h * dim : 2 * part + (h + 1) * dim]
            s = mm_nt(q * scale, k) + masked
            top = jnp.max(s, axis=-1, keepdims=True)
            e = jnp.exp(s - top)
            total = jnp.sum(e, axis=-1, keepdims=True)
            outs.append((mm(e.astype(BF), v) * (1.0 / total)).astype(BF))
            lse[at, h : h + 1] = top + jnp.log(total)
        ctx[r] = jnp.concatenate(outs, axis=1)
        return carry

    lax.fori_loop(0, 4, attend, 0)
    for r, ref in enumerate((c0, c1, c2, c3)):
        ref[...] = ctx[r]


def branch_kernel(tile, c0, c1, c2, c3, wo, bo, x, gain, shift, resid, hid, xs):
    part = c0.shape[1]
    load_tile(x, xs, 0)
    acc = xs[...].astype(F32) + vec_row(bo)
    for r, ref in enumerate((c0, c1, c2, c3)):
        at = pl.multiple_of((tile[0] ^ r) * part, part)
        acc = acc + mm(ref[...], wo[pl.ds(at, part), :])
    resid[...] = acc
    normed, _ = norm_stats(acc)
    hid[...] = (normed * vec_row(gain) + vec_row(shift)).astype(BF)


def mlp_kernel(
    tile, mask, resid, hid, ct, gain, fc1, fc1_b, fc2, fc2_b, out, branch, rgrad, vecs, up, acc, nacc
):
    step = pl.program_id(0)
    rows, cols, _ = ct.shape[1:]

    @pl.when(step == 0)
    def _():
        load_tile(ct, up, 0)
        up[...] = (up[...].astype(F32) * keep_tokens(mask_edges(mask), tile[0], rows, cols, 0)).astype(BF)
        acc[...] = jnp.zeros_like(acc)
        nacc[...] = jnp.zeros_like(nacc)

    act, dgelu = gelu_parts(mm(hid[...], fc1[...]) + fc1_b[...])
    acc[...] += mm(act.astype(BF), fc2[...])
    inner = (mm_nt(up[...], fc2[...]) * dgelu).astype(BF)
    nacc[...] += mm_nt(inner, fc1[...])

    @pl.when(step == pl.num_programs(0) - 1)
    def _():
        res = resid[...]
        keep = keep_tokens(mask_edges(mask), tile[0], rows, cols, 0)
        store_tile(out, (keep * (res + acc[...] + vec_row(fc2_b))).astype(BF))
        normed, inv = norm_stats(res)
        n = nacc[...]
        vecs[0:1, :] = jnp.sum(n * normed, axis=0, keepdims=True)
        vecs[1:2, :] = jnp.sum(n, axis=0, keepdims=True)
        grad = up[...].astype(F32) + norm_back(n, normed, inv, vec_row(gain))
        rgrad[...] = grad
        branch[...] = grad.astype(BF)


def ffgrad_kernel(
    tile, mask, h0, h1, h2, h3, t0, t1, t2, t3, fc1, fc1_b, fc2, g1, g2, b1, b2, up, a1, a2
):
    rows, cols, _ = t0.shape[1:]
    edges = mask_edges(mask)
    hids = (h0, h1, h2, h3)
    for r, ref in enumerate((t0, t1, t2, t3)):
        load_tile(ref, up, 0)
        wide = up[...].astype(F32) * keep_tokens(edges, tile[0] ^ r, rows, cols, 0)
        low = wide.astype(BF)
        h = hids[r][...]
        act, dgelu = gelu_parts(mm(h, fc1[...]) + fc1_b[...])
        inner = (mm_nt(low, fc2[...]) * dgelu).astype(BF)
        d1 = mm_tn(h, inner)
        d2 = mm_tn(act.astype(BF), low)
        s1 = jnp.sum(inner.astype(F32), axis=0, keepdims=True)
        s2 = jnp.sum(wide, axis=0, keepdims=True)
        if r == 0:
            a1[...], a2[...], b1[...], b2[...] = d1, d2, s1, s2
        elif r < 3:
            a1[...] += d1
            a2[...] += d2
            b1[...] += s1
            b2[...] += s2
        else:
            g1[...] = (a1[...] + d1).astype(BF)
            g2[...] = (a2[...] + d2).astype(BF)
            b1[...] += s1
            b2[...] += s2


def outgrad_kernel(tile, b0, b1, b2, b3, wo, c0, c1, c2, c3, dctx, gout, bsum):
    toks, part = c0.shape
    at = pl.multiple_of(tile[0] * part, part)
    w = wo[pl.ds(at, part), :]
    ctx = (c0, c1, c2, c3)
    acc = None
    total = None
    for r, ref in enumerate((b0, b1, b2, b3)):
        low = ref[...]
        dctx[r * toks : (r + 1) * toks, :] = mm_nt(low, w).astype(BF)
        d = mm_tn(ctx[r][...], low)
        s = jnp.sum(low.astype(F32), axis=0, keepdims=True)
        acc = d if r == 0 else acc + d
        total = s if r == 0 else total + s
    gout[...] = acc.astype(BF)
    bsum[...] = total


def attnback_kernel(
    tile,
    mask,
    dctx,
    qkv,
    lse,
    hid,
    nrm,
    w,
    bsum,
    vec2,
    fb1,
    fb2,
    o0,
    o1,
    o2,
    o3,
    m0,
    m1,
    m2,
    m3,
    grads,
    rows_out,
    dk,
    dv,
    mix,
    vecs,
    *,
    cols,
):
    total, three = qkv.shape
    part = three // 3
    toks = total // 4
    dim = hid.shape[1] // HEADS
    rows = toks // PAD
    scale = dim ** (-0.5)
    masked = mask_row(tile, mask, rows, cols)
    dk[...] = jnp.zeros_like(dk)
    dv[...] = jnp.zeros_like(dv)

    def attend(r, carry):
        at = pl.ds(pl.multiple_of(r * toks, toks), toks)
        dqs = []
        q_all = qkv[at, :part] * scale
        do_all = dctx[at, :]
        q_turned = q_all.T
        do_turned = do_all.T
        for h in range(part // dim):
            at_h = slice(h * dim, (h + 1) * dim)
            k = qkv[:, part + h * dim : part + (h + 1) * dim]
            v = qkv[:, 2 * part + h * dim : 2 * part + (h + 1) * dim]
            p = jnp.exp(mm_nt(q_all[:, at_h], k) + masked - lse[at, h : h + 1])
            dp = mm_nt(do_all[:, at_h], v)
            ds = (p * (dp - jnp.sum(dp * p, axis=-1, keepdims=True))).astype(BF)
            dqs.append((mm(ds, k) * scale).astype(BF))
            dv[at_h, :] += mm(do_turned[at_h], p.astype(BF))
            dk[at_h, :] += mm(q_turned[at_h], ds)
        mix[at, :part] = jnp.concatenate(dqs, axis=1)
        return carry

    lax.fori_loop(0, 4, attend, 0)
    mix[:, part : 2 * part] = dk[...].T.astype(BF)
    mix[:, 2 * part :] = dv[...].T.astype(BF)
    grads[:, : 3 * part] = mm_tn(hid[...], mix[...]).astype(BF)
    for r, ref in enumerate((o0, o1, o2, o3)):
        at = pl.multiple_of((tile[0] ^ r) * part, part)
        grads[pl.ds(at, part), 3 * part :] = ref[...]
    for r, ref in enumerate((m0, m1, m2, m3)):
        ref[...] = mix[r * toks : (r + 1) * toks, :]
    col_sum = jnp.sum(mix[...].astype(F32), axis=0, keepdims=True)
    chunk = 256
    for i in range(w.shape[0] // chunk):
        at = slice(i * chunk, (i + 1) * chunk)
        n = mm_nt(mix[...], w[at, :])
        vecs[0:1, at] = jnp.sum(n * nrm[:, at].astype(F32), axis=0, keepdims=True)
        vecs[1:2, at] = jnp.sum(n, axis=0, keepdims=True)
    slot = lax.broadcasted_iota(jnp.int32, (1, 4 * part), 1)
    own = (slot >= tile[0] * part) & (slot < (tile[0] + 1) * part)
    lone = jnp.where(tile[0] == 0, 1.0, 0.0).astype(F32)
    for i in range(3):
        piece = col_sum[:, i * part : (i + 1) * part]
        vecs[2 + i : 3 + i, :] = jnp.where(own, jnp.concatenate([piece] * 4, axis=1), 0.0)
    vecs[5:6, :] = bsum[...] * lone
    vecs[6:8, :] = vec2[...]
    vecs[8:9, :] = fb2[...] * lone
    imgs, height, width = rows_out.shape
    share = width // imgs
    quarter = fb1.shape[1] // imgs
    spare = jnp.zeros((1, height * width - 9 * share - quarter), F32)
    for i in range(imgs):
        pieces = [vecs[j : j + 1, i * share : (i + 1) * share] for j in range(9)]
        pieces += [fb1[:, i * quarter : (i + 1) * quarter], spare]
        line = jnp.concatenate(pieces, axis=1).astype(BF)
        for j in range(height):
            rows_out[i, j : j + 1, :] = line[:, j * width : (j + 1) * width]


def input_kernel(tile, m0, m1, m2, m3, w, x, rgrad, gain, out, ms, xs):
    part = m0.shape[1] // 3
    for r, ref in enumerate((m0, m1, m2, m3)):
        ms[r] = ref[...]
    tiles = [ms[tile[0] ^ g] for g in range(4)]
    full = jnp.concatenate(
        [m[:, i * part : (i + 1) * part] for i in range(3) for m in tiles], axis=1
    )
    n = mm_nt(full, w[...])
    load_tile(x, xs, 0)
    normed, inv = norm_stats(xs[...].astype(F32))
    store_tile(out, (rgrad[...] + norm_back(n, normed, inv, vec_row(gain))).astype(BF))


def fc1out_kernel(tile, p0, p1, p2, p3, fc1, ps, *, quarter):
    for r, ref in enumerate((p0, p1, p2, p3)):
        ps[r] = ref[...].astype(F32)
    for g in range(4):
        piece = ps[tile[0] ^ g]
        for i in range(fc1.shape[1] // (4 * quarter)):
            dst = (4 * i + g) * quarter
            fc1[:, dst : dst + quarter] = piece[:, i * quarter : (i + 1) * quarter]


def fc2out_kernel(tile, p0, p1, p2, p3, fc2, ps):
    quarter = fc2.shape[0] // 4
    for r, ref in enumerate((p0, p1, p2, p3)):
        ps[r] = ref[...].astype(F32)
    for g in range(4):
        fc2[g * quarter : (g + 1) * quarter, :] = ps[tile[0] ^ g]


def attnout_kernel(
    tile, p0, p1, p2, p3, gqkv, gout, v0, v1, v2, v4, v5, v6, v7, v8, units, ps
):
    rows, width = gout.shape
    part = width // 4
    quarter = units.shape[0] // 4
    height = ps.shape[1] - rows
    for r, ref in enumerate((p0, p1, p2, p3)):
        ps[r] = ref[...].astype(F32)
    total = None
    tails = []
    for g in range(4):
        piece = ps[tile[0] ^ g]
        for i in range(3):
            dst = i * width + g * part
            gqkv[:, dst : dst + part] = piece[:rows, i * part : (i + 1) * part]
        gout[:, g * part : (g + 1) * part] = piece[:rows, 3 * part :]
        tail = jnp.concatenate([piece[rows + j : rows + j + 1] for j in range(height)], axis=1)
        total = tail if g == 0 else total + tail
        tails.append(tail[:, 9 * rows : 9 * rows + quarter])
    places = ((0, v0), (1, v1), (2, v2), (4, v4), (5, v5), (6, v6), (7, v7), (8, v8))
    for i, ref in places:
        ref[...] = total[0, i * rows : (i + 1) * rows]
    units[...] = jnp.concatenate(tails, axis=1)[0]


def layer(
    patches,
    patch_mask,
    norm1_gain,
    norm1_shift,
    qkv_weight,
    qv_bias,
    out_weight,
    out_bias,
    norm2_gain,
    norm2_shift,
    fc1_weight,
    fc1_bias,
    fc2_weight,
    fc2_bias,
    cotangent,
):
    _, rows, cols, width = patches.shape
    ff = fc1_weight.shape[1]
    imgs = lax.axis_size("imgs")
    part = width // 4
    units = ff // 4
    quarter = units // imgs
    share = width // imgs
    toks = rows * PAD
    total = 4 * toks
    tile = lax.axis_index("rows") * 2 + lax.axis_index("cols")
    at_tile = tile.reshape(1).astype(jnp.int32)

    def row(v):
        return v.reshape(1, -1)

    steps = 4
    w_own, b_own = pl.pallas_call(
        heads_kernel,
        grid=(steps,),
        in_specs=[
            SMEM,
            pl.BlockSpec((width // steps, 3 * width), lambda i: (i, 0)),
            pl.BlockSpec((2, width), lambda i: (0, 0)),
        ],
        out_specs=[
            pl.BlockSpec((width // steps, 3 * part), lambda i: (i, 0)),
            pl.BlockSpec((1, 3 * part), lambda i: (0, 0)),
        ],
        out_shape=[sds((width, 3 * part)), sds((1, 3 * part), F32)],
        cost_estimate=cost(4),
        name="heads",
    )(at_tile, qkv_weight, qv_bias.T)
    fc1_own, fc1_b_own = pl.pallas_call(
        functools.partial(units_kernel, quarter=quarter),
        grid=(steps,),
        in_specs=[
            SMEM,
            pl.BlockSpec((width // steps, ff), lambda i: (i, 0)),
            pl.BlockSpec((1, ff), lambda i: (0, 0)),
        ],
        out_specs=[
            pl.BlockSpec((width // steps, units), lambda i: (i, 0)),
            pl.BlockSpec((1, units), lambda i: (0, 0)),
        ],
        out_shape=[sds((width, units)), sds((1, units), F32)],
        cost_estimate=cost(4),
        name="units",
    )(at_tile, fc1_weight, row(fc1_bias))
    x_blocks, (w_own, b_own, fc1_own) = gather_tiles(patches, (w_own, b_own, fc1_own))

    hid1, nrm1, qkv, lse, *ctx = vec_call(
        attn_kernel,
        [
            sds((total, width)),
            sds((total, width)),
            sds((total, 3 * part)),
            sds((total, 128), F32),
        ]
        + [sds((toks, part))] * 4,
        9,
        [pltpu.VMEM((total, width), BF), pltpu.VMEM((4, toks, part), BF)],
        us=13,
    )(at_tile, patch_mask, *x_blocks, norm1_gain, norm1_shift, w_own, b_own)
    ct_blocks, ctx = gather_tiles(cotangent, ctx)
    later_tile, _ = tie(at_tile, ctx)

    fc2_own = lax.dynamic_index_in_dim(
        fc2_weight.reshape(imgs, 4, quarter, width), later_tile[0], 1, keepdims=False
    ).reshape(units, width)

    ctx_in = scatter_tiles(ctx)
    ctx_in, (fc2_own,) = tie(ctx_in, (fc2_own,))
    resid, hid2 = vec_call(
        branch_kernel,
        [sds((toks, width), F32), sds((toks, width))],
        9,
        [pltpu.VMEM((toks, width), BF)],
        us=3,
    )(at_tile, *ctx_in, out_weight, out_bias, patches, norm2_gain, norm2_shift)

    chunks = 4
    step = ff // chunks

    def whole(*shape):
        return pl.BlockSpec(shape, lambda i: (0,) * len(shape))

    layer_out, branch, rgrad, vec2 = pl.pallas_call(
        mlp_kernel,
        grid=(chunks,),
        in_specs=[
            SMEM,
            whole(*patch_mask.shape),
            whole(toks, width),
            whole(toks, width),
            whole(1, rows, cols, width),
            whole(width),
            pl.BlockSpec((width, step), lambda i: (0, i)),
            pl.BlockSpec((1, step), lambda i: (0, i)),
            pl.BlockSpec((step, width), lambda i: (i, 0)),
            whole(width),
        ],
        out_specs=[
            whole(1, rows, cols, width),
            whole(toks, width),
            whole(toks, width),
            whole(2, width),
        ],
        out_shape=[
            sds((1, rows, cols, width)),
            sds((toks, width)),
            sds((toks, width), F32),
            sds((2, width), F32),
        ],
        scratch_shapes=[
            pltpu.VMEM((toks, width), BF),
            pltpu.VMEM((toks, width), F32),
            pltpu.VMEM((toks, width), F32),
        ],
        cost_estimate=cost(11),
        name="mlp",
    )(
        at_tile,
        patch_mask,
        resid,
        hid2,
        cotangent,
        norm2_gain,
        fc1_weight,
        row(fc1_bias),
        fc2_weight,
        fc2_bias,
    )
    hid2_blocks, (branch,) = gather_tiles(hid2, (branch,))

    g1, g2, fb1, fb2 = vec_call(
        ffgrad_kernel,
        [sds((width, units)), sds((units, width)), sds((1, units), F32), sds((1, width), F32)],
        12,
        [
            pltpu.VMEM((toks, width), BF),
            pltpu.VMEM((width, units), F32),
            pltpu.VMEM((units, width), F32),
        ],
        us=9,
    )(at_tile, patch_mask, *hid2_blocks, *ct_blocks, fc1_own, fc1_b_own, fc2_own)
    branch_blocks, (g1, g2) = gather_tiles(branch, (g1, g2))

    dctx, gout, bsum = vec_call(
        outgrad_kernel,
        [sds((total, part)), sds((part, width)), sds((1, width), F32)],
        9,
        us=4,
    )(at_tile, *branch_blocks, out_weight, *ctx)
    direct = direct_sum(imgs)
    (g1, g2), (gout,) = tie((g1, g2), (gout,))
    g1 = g1.reshape(imgs, share, units)
    g2 = g2.reshape(imgs, quarter, width)
    out_cols = [lax.dynamic_slice_in_dim(gout, (tile ^ r) * part, part, 1) for r in range(4)]
    out_rows = scatter_tiles(out_cols)
    if direct:
        line = imgs // 2
        (g1, g2), out_cols = tie((g1, g2), out_cols)
        near1 = exchange_near(g1.reshape(line, 2, share, units))
        far2 = exchange_far(g2.reshape(line, 2, quarter, width))
    dctx, out_rows = tie(dctx, out_rows)

    count = 9 * share + quarter
    vec_height = -(-count // width)
    *mixed, grads, vecs = vec_call(
        functools.partial(attnback_kernel, cols=cols),
        [sds((toks, 3 * part))] * 4 + [sds((width, width)), sds((imgs, vec_height, width))],
        15,
        [
            pltpu.VMEM((part, total), F32),
            pltpu.VMEM((part, total), F32),
            pltpu.VMEM((total, 3 * part), BF),
            pltpu.VMEM((9, width), F32),
        ],
        us=18,
    )(at_tile, patch_mask, dctx, qkv, lse, hid1, nrm1, w_own, bsum, vec2, fb1, fb2, *out_rows)

    at_bucket = jnp.concatenate(
        [grads.reshape(imgs, share, width), vecs], axis=1
    )
    if direct:
        near3 = exchange_near(at_bucket.reshape(line, 2, share + vec_height, width))
        near1, (at_bucket,) = tie(near1, (at_bucket,))
        mid1 = total_of(near1).astype(BF)
        far1 = exchange_far(mid1)
        far2, (far1[0],) = tie(far2, (far1[0],))
    mixed_in = scatter_tiles(mixed)
    if direct:
        near2 = exchange_near(total_of(far2).astype(BF)[None])
        near3, (far1[0], mixed_in[0]) = tie(near3, (far1[0], mixed_in[0]))
        mid3 = total_of(near3).astype(BF)
        mixed_in[0], (mid3,) = tie(mixed_in[0], (mid3,))
        far3 = exchange_far(mid3)

    patches_grad = vec_call(
        input_kernel,
        sds((1, rows, cols, width)),
        8,
        [pltpu.VMEM((4, toks, 3 * part), BF), pltpu.VMEM((toks, width), BF)],
        us=5,
    )(at_tile, *mixed_in, qkv_weight, patches, rgrad, norm1_gain)

    if direct:
        fc2_sum = total_of(near2)[0].astype(BF)
        far1, (patches_grad,) = tie(far1, (patches_grad,))
        fc1_sum = total_of(far1).astype(BF)
    else:
        fc1_sum, fc2_sum, at_sum = (plain_sum(b) for b in (g1, g2, at_bucket))
    fc2_pieces, _ = gather_tiles(fc2_sum)
    fc1_pieces, _ = gather_tiles(fc1_sum)
    if direct:
        far3, (patches_grad, fc2_pieces[2]) = tie(far3, (patches_grad, fc2_pieces[2]))
        at_sum = total_of(far3).astype(BF)
    fc2_grad = vec_call(
        fc2out_kernel,
        sds((4 * quarter, width), F32),
        4,
        [pltpu.VMEM((4, quarter, width), F32)],
        us=2,
    )(at_tile, *fc2_pieces)
    fc1_grad = vec_call(
        functools.partial(fc1out_kernel, quarter=quarter),
        sds((share, ff), F32),
        4,
        [pltpu.VMEM((4, share, units), F32)],
        us=2,
    )(at_tile, *fc1_pieces)
    at_pieces, (fc1_grad, fc2_grad) = gather_tiles(at_sum, (fc1_grad, fc2_grad))
    qkv_grad, out_grad, *vec_sums, unit_sum = vec_call(
        attnout_kernel,
        [
            sds((share, 3 * width), F32),
            sds((share, width), F32),
            *[sds((share,), F32)] * 8,
            sds((4 * quarter,), F32),
        ],
        4,
        [pltpu.VMEM((4, share + vec_height, width), F32)],
        us=3,
    )(at_tile, *at_pieces)
    return (
        layer_out,
        patches_grad,
        vec_sums[0],
        vec_sums[1],
        qkv_grad,
        jnp.stack([vec_sums[2], vec_sums[3]], axis=1),
        out_grad,
        vec_sums[4],
        vec_sums[5],
        vec_sums[6],
        fc1_grad,
        unit_sum,
        fc2_grad,
        vec_sums[7],
    )


def solution(mesh):
    tiled = P("imgs", "rows", "cols", None)
    in_specs = (tiled, P("imgs", None, None)) + (P(),) * 12 + (tiled,)
    mat = P("imgs", None)
    vec = P("imgs")
    out_specs = (tiled, tiled, vec, vec, mat, mat, mat, vec, vec, vec, mat, vec, mat, vec)
    return jax.shard_map(layer, mesh=mesh, in_specs=in_specs, out_specs=out_specs, check_vma=False)
```

```python
import functools

import jax
import jax.numpy as jnp
from jax import lax
from jax.experimental import pallas as pl
from jax.experimental.pallas import tpu as pltpu
from jax.sharding import PartitionSpec as P

HEADS = 12
NORM_EPS = 1e-06
MASKED_SCORE = -1e30
GROUP = ("rows", "cols")
BF = jnp.bfloat16
F32 = jnp.float32


def dot(left, right, dims):
    return lax.dot_general(left, right, (dims, ((), ())), preferred_element_type=F32)


def mm(left, right):
    return dot(left, right, ((1,), (0,)))


def mm_nt(left, right):
    return dot(left, right, ((1,), (1,)))


def mm_tn(left, right):
    return dot(left, right, ((0,), (0,)))


def to_peer(value, rel):
    if rel == 1:
        return lax.ppermute(value, "cols", [(0, 1), (1, 0)])
    if rel == 2:
        return lax.ppermute(value, "rows", [(0, 1), (1, 0)])
    return lax.ppermute(value, GROUP, [(i, i ^ 3) for i in range(4)])


def tie(values, others):
    flat, tree = jax.tree.flatten((values, others))
    return jax.tree.unflatten(tree, lax.optimization_barrier(flat))


def gather_tiles(value, others=()):
    across = to_peer(value, 2)
    beside = to_peer(value, 1)
    across, others = tie(across, others)
    return [value, beside, across, to_peer(across, 1)], others


def scatter_tiles(blocks):
    return [blocks[0], to_peer(blocks[1], 1), to_peer(blocks[2], 2), to_peer(blocks[3], 3)]


def norm_stats(values):
    mean_val = jnp.mean(values, axis=-1, keepdims=True)
    centred = values - mean_val
    var_val = jnp.mean(centred * centred, axis=-1, keepdims=True)
    inv = lax.rsqrt(var_val + NORM_EPS)
    return centred * inv, inv


def norm_back(grads, normed, inv, gain):
    g = grads * gain
    return (
        g
        - jnp.mean(g, axis=-1, keepdims=True)
        - normed * jnp.mean(g * normed, axis=-1, keepdims=True)
    ) * inv


def gelu_parts(x):
    cdf = 0.5 * (1.0 + lax.erf(x * 0.7071067811865476))
    pdf = jnp.exp(-0.5 * x * x) * 0.3989422804014327
    return x * cdf, cdf + x * pdf


def exchange_near(parts):
    side = lax.axis_index("imgs") % 2
    count = lax.axis_size("imgs")
    send = lax.dynamic_index_in_dim(parts, 1 - side, 1, keepdims=False)
    keep = lax.dynamic_index_in_dim(parts, side, 1, keepdims=False)
    return keep, lax.ppermute(send, "imgs", [(i, i ^ 1) for i in range(count)])


def exchange_far(parts):
    count = lax.axis_size("imgs")
    place = lax.axis_index("imgs") // 2
    got = [lax.dynamic_index_in_dim(parts, place, 0, keepdims=False)]
    for k in range(count // 2 - 1, 0, -1):
        send = lax.dynamic_index_in_dim(parts, place ^ k, 0, keepdims=False)
        got.append(lax.ppermute(send, "imgs", [(i, i ^ (2 * k)) for i in range(count)]))
    return got


def total_of(blocks):
    return functools.reduce(jnp.add, [b.astype(F32) for b in blocks])


def direct_sum(imgs):
    return imgs <= 8 and imgs & (imgs - 1) == 0


def plain_sum(parts):
    return lax.psum_scatter(parts, "imgs", scatter_dimension=0, tiled=False)


SMEM = pl.BlockSpec(memory_space=pltpu.SMEM)
VMEM = pl.BlockSpec(memory_space=pltpu.VMEM)
PAD = 16


def vec_call(kernel, outs, n_in, scratch=(), us=5, near=()):
    call = pl.pallas_call(
        kernel,
        out_shape=outs,
        in_specs=[SMEM] + [VMEM] * n_in,
        out_specs=jax.tree.map(lambda _: VMEM, outs),
        scratch_shapes=list(scratch),
        cost_estimate=cost(us),
    )

    def run(*args):
        placed = [
            pltpu.with_memory_space_constraint(a, pltpu.VMEM) if i in near else a
            for i, a in enumerate(args)
        ]
        return call(*placed)

    return run


def cost(us):
    return pl.CostEstimate(flops=us * 10**9, transcendentals=0, bytes_accessed=us * 10**6)


def sds(shape, dtype=BF):
    return jax.ShapeDtypeStruct(shape, dtype)


def load_tile(ref, scratch, at):
    rows, cols, width = ref.shape[1:]
    scratch[at : at + rows * PAD, :] = jnp.zeros((rows * PAD, width), scratch.dtype)
    for i in range(rows):
        scratch[at + i * PAD : at + i * PAD + cols, :] = ref[0, i]


def store_tile(ref, value):
    rows, cols, _ = ref.shape[1:]
    for i in range(rows):
        ref[0, i] = value[i * PAD : i * PAD + cols, :]


def mask_edges(mask):
    m = mask[0].astype(F32)
    high = jnp.sum(m[:, 0:1], axis=0, keepdims=True)
    wide = jnp.sum(m[0:1, :], axis=1, keepdims=True)
    return high, wide


def keep_tokens(edges, place, rows, cols, axis):
    toks = rows * PAD
    shape = (toks, 1) if axis == 0 else (1, toks)
    tok = lax.broadcasted_iota(jnp.int32, shape, axis)
    c = tok & (PAD - 1)
    r = ((tok >> 4) + (place >> 1) * rows).astype(F32)
    at = (c + (place & 1) * cols).astype(F32)
    ok = (c < cols) & (r < edges[0]) & (at < edges[1])
    return jnp.where(ok, 1.0, 0.0).astype(F32)


def mask_row(tile, mask, rows, cols):
    edges = mask_edges(mask)
    keep = [keep_tokens(edges, tile[0] ^ r, rows, cols, 1) for r in range(4)]
    return jnp.where(jnp.concatenate(keep, axis=1) > 0, 0.0, MASKED_SCORE).astype(F32)


def vec_row(ref):
    return ref[...].reshape(1, -1)


def heads_kernel(tile, qkv_w, qv_b, w_own, b_own):
    width = qv_b.shape[1]
    part = width // 4
    for g in range(4):

        @pl.when(tile[0] == g)
        def _():
            for i in range(3):
                src = i * width + g * part
                w_own[:, i * part : (i + 1) * part] = qkv_w[:, src : src + part]
            b_own[:, :part] = qv_b[0:1, g * part : (g + 1) * part]
            b_own[:, part : 2 * part] = jnp.zeros((1, part), F32)
            b_own[:, 2 * part :] = qv_b[1:2, g * part : (g + 1) * part]


def units_kernel(tile, fc1, fc1_b, fc1_own, fc1_b_own, *, quarter):
    for g in range(4):

        @pl.when(tile[0] == g)
        def _():
            for i in range(fc1.shape[1] // (4 * quarter)):
                src = (4 * i + g) * quarter
                dst = i * quarter
                fc1_own[:, dst : dst + quarter] = fc1[:, src : src + quarter]
                fc1_b_own[:, dst : dst + quarter] = fc1_b[:, src : src + quarter]


def attn_kernel(
    tile, mask, x0, x1, x2, x3, gain, shift, w, bias, hid, nrm, qkv, lse, c0, c1, c2, c3, xs, ctx
):
    rows, cols, width = x0.shape[1:]
    toks = rows * PAD
    part = w.shape[1] // 3
    dim = width // HEADS
    scale = dim ** (-0.5)
    for r, ref in enumerate((x0, x1, x2, x3)):
        load_tile(ref, xs, r * toks)

    normed, _ = norm_stats(xs[...].astype(F32))
    nrm[...] = normed.astype(BF)
    hid[...] = (normed * vec_row(gain) + vec_row(shift)).astype(BF)
    qkv[...] = (mm(hid[...], w[...]) + bias[...]).astype(BF)
    masked = mask_row(tile, mask, rows, cols)

    def attend(r, carry):
        at = pl.ds(pl.multiple_of(r * toks, toks), toks)
        outs = []
        for h in range(part // dim):
            q = qkv[at, h * dim : (h + 1) * dim]
            k = qkv[:, part + h * dim : part + (h + 1) * dim]
            v = qkv[:, 2 * part + h * dim : 2 * part + (h + 1) * dim]
            s = mm_nt(q * scale, k) + masked
            top = jnp.max(s, axis=-1, keepdims=True)
            e = jnp.exp(s - top)
            total = jnp.sum(e, axis=-1, keepdims=True)
            outs.append((mm(e.astype(BF), v) * (1.0 / total)).astype(BF))
            lse[at, h : h + 1] = top + jnp.log(total)
        ctx[r] = jnp.concatenate(outs, axis=1)
        return carry

    lax.fori_loop(0, 4, attend, 0)
    for r, ref in enumerate((c0, c1, c2, c3)):
        ref[...] = ctx[r]


def branch_kernel(tile, c0, c1, c2, c3, wo, bo, x, gain, shift, resid, hid, xs):
    part = c0.shape[1]
    load_tile(x, xs, 0)
    acc = xs[...].astype(F32) + vec_row(bo)
    for r, ref in enumerate((c0, c1, c2, c3)):
        at = pl.multiple_of((tile[0] ^ r) * part, part)
        acc = acc + mm(ref[...], wo[pl.ds(at, part), :])
    resid[...] = acc
    normed, _ = norm_stats(acc)
    hid[...] = (normed * vec_row(gain) + vec_row(shift)).astype(BF)


def mlp_kernel(
    tile, mask, resid, hid, ct, gain, fc1, fc1_b, fc2, fc2_b, out, branch, rgrad, vecs, up, acc, nacc
):
    step = pl.program_id(0)
    rows, cols, _ = ct.shape[1:]

    @pl.when(step == 0)
    def _():
        load_tile(ct, up, 0)
        up[...] = (up[...].astype(F32) * keep_tokens(mask_edges(mask), tile[0], rows, cols, 0)).astype(BF)
        acc[...] = jnp.zeros_like(acc)
        nacc[...] = jnp.zeros_like(nacc)

    act, dgelu = gelu_parts(mm(hid[...], fc1[...]) + fc1_b[...])
    acc[...] += mm(act.astype(BF), fc2[...])
    inner = (mm_nt(up[...], fc2[...]) * dgelu).astype(BF)
    nacc[...] += mm_nt(inner, fc1[...])

    @pl.when(step == pl.num_programs(0) - 1)
    def _():
        res = resid[...]
        keep = keep_tokens(mask_edges(mask), tile[0], rows, cols, 0)
        store_tile(out, (keep * (res + acc[...] + vec_row(fc2_b))).astype(BF))
        normed, inv = norm_stats(res)
        n = nacc[...]
        vecs[0:1, :] = jnp.sum(n * normed, axis=0, keepdims=True)
        vecs[1:2, :] = jnp.sum(n, axis=0, keepdims=True)
        grad = up[...].astype(F32) + norm_back(n, normed, inv, vec_row(gain))
        rgrad[...] = grad
        branch[...] = grad.astype(BF)


def ffgrad_kernel(
    tile, mask, h0, h1, h2, h3, t0, t1, t2, t3, fc1, fc1_b, fc2, g1, g2, b1, b2, up, a1, a2
):
    rows, cols, _ = t0.shape[1:]
    edges = mask_edges(mask)
    hids = (h0, h1, h2, h3)
    for r, ref in enumerate((t0, t1, t2, t3)):
        load_tile(ref, up, 0)
        wide = up[...].astype(F32) * keep_tokens(edges, tile[0] ^ r, rows, cols, 0)
        low = wide.astype(BF)
        h = hids[r][...]
        act, dgelu = gelu_parts(mm(h, fc1[...]) + fc1_b[...])
        inner = (mm_nt(low, fc2[...]) * dgelu).astype(BF)
        d1 = mm_tn(h, inner)
        d2 = mm_tn(act.astype(BF), low)
        s1 = jnp.sum(inner.astype(F32), axis=0, keepdims=True)
        s2 = jnp.sum(wide, axis=0, keepdims=True)
        if r == 0:
            a1[...], a2[...], b1[...], b2[...] = d1, d2, s1, s2
        elif r < 3:
            a1[...] += d1
            a2[...] += d2
            b1[...] += s1
            b2[...] += s2
        else:
            g1[...] = (a1[...] + d1).astype(BF)
            g2[...] = (a2[...] + d2).astype(BF)
            b1[...] += s1
            b2[...] += s2


def outgrad_kernel(tile, b0, b1, b2, b3, wo, c0, c1, c2, c3, dctx, gout, bsum):
    toks, part = c0.shape
    at = pl.multiple_of(tile[0] * part, part)
    w = wo[pl.ds(at, part), :]
    ctx = (c0, c1, c2, c3)
    acc = None
    total = None
    for r, ref in enumerate((b0, b1, b2, b3)):
        low = ref[...]
        dctx[r * toks : (r + 1) * toks, :] = mm_nt(low, w).astype(BF)
        d = mm_tn(ctx[r][...], low)
        s = jnp.sum(low.astype(F32), axis=0, keepdims=True)
        acc = d if r == 0 else acc + d
        total = s if r == 0 else total + s
    gout[...] = acc.astype(BF)
    bsum[...] = total


def attnback_kernel(
    tile,
    mask,
    dctx,
    qkv,
    lse,
    hid,
    nrm,
    w,
    bsum,
    vec2,
    fb1,
    fb2,
    o0,
    o1,
    o2,
    o3,
    m0,
    m1,
    m2,
    m3,
    grads,
    rows_out,
    dk,
    dv,
    mix,
    vecs,
    *,
    cols,
):
    total, three = qkv.shape
    part = three // 3
    toks = total // 4
    dim = hid.shape[1] // HEADS
    rows = toks // PAD
    scale = dim ** (-0.5)
    masked = mask_row(tile, mask, rows, cols)
    dk[...] = jnp.zeros_like(dk)
    dv[...] = jnp.zeros_like(dv)

    def attend(r, carry):
        at = pl.ds(pl.multiple_of(r * toks, toks), toks)
        dqs = []
        q_all = qkv[at, :part] * scale
        do_all = dctx[at, :]
        q_turned = q_all.T
        do_turned = do_all.T
        for h in range(part // dim):
            at_h = slice(h * dim, (h + 1) * dim)
            k = qkv[:, part + h * dim : part + (h + 1) * dim]
            v = qkv[:, 2 * part + h * dim : 2 * part + (h + 1) * dim]
            p = jnp.exp(mm_nt(q_all[:, at_h], k) + masked - lse[at, h : h + 1])
            dp = mm_nt(do_all[:, at_h], v)
            ds = (p * (dp - jnp.sum(dp * p, axis=-1, keepdims=True))).astype(BF)
            dqs.append((mm(ds, k) * scale).astype(BF))
            dv[at_h, :] += mm(do_turned[at_h], p.astype(BF))
            dk[at_h, :] += mm(q_turned[at_h], ds)
        mix[at, :part] = jnp.concatenate(dqs, axis=1)
        return carry

    lax.fori_loop(0, 4, attend, 0)
    mix[:, part : 2 * part] = dk[...].T.astype(BF)
    mix[:, 2 * part :] = dv[...].T.astype(BF)
    grads[:, : 3 * part] = mm_tn(hid[...], mix[...]).astype(BF)
    for r, ref in enumerate((o0, o1, o2, o3)):
        at = pl.multiple_of((tile[0] ^ r) * part, part)
        grads[pl.ds(at, part), 3 * part :] = ref[...]
    for r, ref in enumerate((m0, m1, m2, m3)):
        ref[...] = mix[r * toks : (r + 1) * toks, :]
    col_sum = jnp.sum(mix[...].astype(F32), axis=0, keepdims=True)
    chunk = 256
    for i in range(w.shape[0] // chunk):
        at = slice(i * chunk, (i + 1) * chunk)
        n = mm_nt(mix[...], w[at, :])
        vecs[0:1, at] = jnp.sum(n * nrm[:, at].astype(F32), axis=0, keepdims=True)
        vecs[1:2, at] = jnp.sum(n, axis=0, keepdims=True)
    slot = lax.broadcasted_iota(jnp.int32, (1, 4 * part), 1)
    own = (slot >= tile[0] * part) & (slot < (tile[0] + 1) * part)
    lone = jnp.where(tile[0] == 0, 1.0, 0.0).astype(F32)
    for i in range(3):
        piece = col_sum[:, i * part : (i + 1) * part]
        vecs[2 + i : 3 + i, :] = jnp.where(own, jnp.concatenate([piece] * 4, axis=1), 0.0)
    vecs[5:6, :] = bsum[...] * lone
    vecs[6:8, :] = vec2[...]
    vecs[8:9, :] = fb2[...] * lone
    imgs, height, width = rows_out.shape
    share = width // imgs
    quarter = fb1.shape[1] // imgs
    spare = jnp.zeros((1, height * width - 9 * share - quarter), F32)
    for i in range(imgs):
        pieces = [vecs[j : j + 1, i * share : (i + 1) * share] for j in range(9)]
        pieces += [fb1[:, i * quarter : (i + 1) * quarter], spare]
        line = jnp.concatenate(pieces, axis=1).astype(BF)
        for j in range(height):
            rows_out[i, j : j + 1, :] = line[:, j * width : (j + 1) * width]


def input_kernel(tile, m0, m1, m2, m3, w, x, rgrad, gain, out, ms, xs):
    part = m0.shape[1] // 3
    for r, ref in enumerate((m0, m1, m2, m3)):
        ms[r] = ref[...]
    tiles = [ms[tile[0] ^ g] for g in range(4)]
    full = jnp.concatenate(
        [m[:, i * part : (i + 1) * part] for i in range(3) for m in tiles], axis=1
    )
    n = mm_nt(full, w[...])
    load_tile(x, xs, 0)
    normed, inv = norm_stats(xs[...].astype(F32))
    store_tile(out, (rgrad[...] + norm_back(n, normed, inv, vec_row(gain))).astype(BF))


def fc1out_kernel(tile, p0, p1, p2, p3, fc1, ps, *, quarter):
    for r, ref in enumerate((p0, p1, p2, p3)):
        ps[r] = ref[...].astype(F32)
    for g in range(4):
        piece = ps[tile[0] ^ g]
        for i in range(fc1.shape[1] // (4 * quarter)):
            dst = (4 * i + g) * quarter
            fc1[:, dst : dst + quarter] = piece[:, i * quarter : (i + 1) * quarter]


def fc2out_kernel(tile, p0, p1, p2, p3, fc2, ps):
    quarter = fc2.shape[0] // 4
    for r, ref in enumerate((p0, p1, p2, p3)):
        ps[r] = ref[...].astype(F32)
    for g in range(4):
        fc2[g * quarter : (g + 1) * quarter, :] = ps[tile[0] ^ g]


def attnout_kernel(
    tile, p0, p1, p2, p3, gqkv, gout, v0, v1, v2, v4, v5, v6, v7, v8, units, ps
):
    rows, width = gout.shape
    part = width // 4
    quarter = units.shape[0] // 4
    height = ps.shape[1] - rows
    for r, ref in enumerate((p0, p1, p2, p3)):
        ps[r] = ref[...].astype(F32)
    total = None
    tails = []
    for g in range(4):
        piece = ps[tile[0] ^ g]
        for i in range(3):
            dst = i * width + g * part
            gqkv[:, dst : dst + part] = piece[:rows, i * part : (i + 1) * part]
        gout[:, g * part : (g + 1) * part] = piece[:rows, 3 * part :]
        tail = jnp.concatenate([piece[rows + j : rows + j + 1] for j in range(height)], axis=1)
        total = tail if g == 0 else total + tail
        tails.append(tail[:, 9 * rows : 9 * rows + quarter])
    places = ((0, v0), (1, v1), (2, v2), (4, v4), (5, v5), (6, v6), (7, v7), (8, v8))
    for i, ref in places:
        ref[...] = total[0, i * rows : (i + 1) * rows]
    units[...] = jnp.concatenate(tails, axis=1)[0]


def layer(
    patches,
    patch_mask,
    norm1_gain,
    norm1_shift,
    qkv_weight,
    qv_bias,
    out_weight,
    out_bias,
    norm2_gain,
    norm2_shift,
    fc1_weight,
    fc1_bias,
    fc2_weight,
    fc2_bias,
    cotangent,
):
    _, rows, cols, width = patches.shape
    ff = fc1_weight.shape[1]
    imgs = lax.axis_size("imgs")
    part = width // 4
    units = ff // 4
    quarter = units // imgs
    share = width // imgs
    toks = rows * PAD
    total = 4 * toks
    tile = lax.axis_index("rows") * 2 + lax.axis_index("cols")
    at_tile = tile.reshape(1).astype(jnp.int32)

    def row(v):
        return v.reshape(1, -1)

    steps = 4
    w_own, b_own = pl.pallas_call(
        heads_kernel,
        grid=(steps,),
        in_specs=[
            SMEM,
            pl.BlockSpec((width // steps, 3 * width), lambda i: (i, 0)),
            pl.BlockSpec((2, width), lambda i: (0, 0)),
        ],
        out_specs=[
            pl.BlockSpec((width // steps, 3 * part), lambda i: (i, 0)),
            pl.BlockSpec((1, 3 * part), lambda i: (0, 0)),
        ],
        out_shape=[sds((width, 3 * part)), sds((1, 3 * part), F32)],
        cost_estimate=cost(4),
        name="heads",
    )(at_tile, qkv_weight, qv_bias.T)
    fc1_own, fc1_b_own = pl.pallas_call(
        functools.partial(units_kernel, quarter=quarter),
        grid=(steps,),
        in_specs=[
            SMEM,
            pl.BlockSpec((width // steps, ff), lambda i: (i, 0)),
            pl.BlockSpec((1, ff), lambda i: (0, 0)),
        ],
        out_specs=[
            pl.BlockSpec((width // steps, units), lambda i: (i, 0)),
            pl.BlockSpec((1, units), lambda i: (0, 0)),
        ],
        out_shape=[sds((width, units)), sds((1, units), F32)],
        cost_estimate=cost(4),
        name="units",
    )(at_tile, fc1_weight, row(fc1_bias))
    x_blocks, (w_own, b_own, fc1_own) = gather_tiles(patches, (w_own, b_own, fc1_own))

    hid1, nrm1, qkv, lse, *ctx = vec_call(
        attn_kernel,
        [
            sds((total, width)),
            sds((total, width)),
            sds((total, 3 * part)),
            sds((total, 128), F32),
        ]
        + [sds((toks, part))] * 4,
        9,
        [pltpu.VMEM((total, width), BF), pltpu.VMEM((4, toks, part), BF)],
        us=13,
        near=(3, 4, 5),
    )(at_tile, patch_mask, *x_blocks, norm1_gain, norm1_shift, w_own, b_own)
    ct_blocks, ctx = gather_tiles(cotangent, ctx)
    later_tile, _ = tie(at_tile, ctx)

    fc2_own = lax.dynamic_index_in_dim(
        fc2_weight.reshape(imgs, 4, quarter, width), later_tile[0], 1, keepdims=False
    ).reshape(units, width)

    ctx_in = scatter_tiles(ctx)
    ctx_in, (fc2_own,) = tie(ctx_in, (fc2_own,))
    resid, hid2 = vec_call(
        branch_kernel,
        [sds((toks, width), F32), sds((toks, width))],
        9,
        [pltpu.VMEM((toks, width), BF)],
        us=3,
        near=(2, 3, 4),
    )(at_tile, *ctx_in, out_weight, out_bias, patches, norm2_gain, norm2_shift)

    chunks = 4
    step = ff // chunks

    def whole(*shape):
        return pl.BlockSpec(shape, lambda i: (0,) * len(shape))

    layer_out, branch, rgrad, vec2 = pl.pallas_call(
        mlp_kernel,
        grid=(chunks,),
        in_specs=[
            SMEM,
            whole(*patch_mask.shape),
            whole(toks, width),
            whole(toks, width),
            whole(1, rows, cols, width),
            whole(width),
            pl.BlockSpec((width, step), lambda i: (0, i)),
            pl.BlockSpec((1, step), lambda i: (0, i)),
            pl.BlockSpec((step, width), lambda i: (i, 0)),
            whole(width),
        ],
        out_specs=[
            whole(1, rows, cols, width),
            whole(toks, width),
            whole(toks, width),
            whole(2, width),
        ],
        out_shape=[
            sds((1, rows, cols, width)),
            sds((toks, width)),
            sds((toks, width), F32),
            sds((2, width), F32),
        ],
        scratch_shapes=[
            pltpu.VMEM((toks, width), BF),
            pltpu.VMEM((toks, width), F32),
            pltpu.VMEM((toks, width), F32),
        ],
        cost_estimate=cost(11),
        name="mlp",
    )(
        at_tile,
        patch_mask,
        resid,
        hid2,
        cotangent,
        norm2_gain,
        fc1_weight,
        row(fc1_bias),
        fc2_weight,
        fc2_bias,
    )
    hid2_blocks, (branch,) = gather_tiles(hid2, (branch,))

    g1, g2, fb1, fb2 = vec_call(
        ffgrad_kernel,
        [sds((width, units)), sds((units, width)), sds((1, units), F32), sds((1, width), F32)],
        12,
        [
            pltpu.VMEM((toks, width), BF),
            pltpu.VMEM((width, units), F32),
            pltpu.VMEM((units, width), F32),
        ],
        us=9,
        near=(3, 4, 5),
    )(at_tile, patch_mask, *hid2_blocks, *ct_blocks, fc1_own, fc1_b_own, fc2_own)
    branch_blocks, (g1, g2) = gather_tiles(branch, (g1, g2))

    dctx, gout, bsum = vec_call(
        outgrad_kernel,
        [sds((total, part)), sds((part, width)), sds((1, width), F32)],
        9,
        us=4,
        near=(2, 3, 4),
    )(at_tile, *branch_blocks, out_weight, *ctx)
    direct = direct_sum(imgs)
    (g1, g2), (gout,) = tie((g1, g2), (gout,))
    g1 = g1.reshape(imgs, share, units)
    g2 = g2.reshape(imgs, quarter, width)
    out_cols = [lax.dynamic_slice_in_dim(gout, (tile ^ r) * part, part, 1) for r in range(4)]
    out_rows = scatter_tiles(out_cols)
    if direct:
        line = imgs // 2
        (g1, g2), out_cols = tie((g1, g2), out_cols)
        near1 = exchange_near(g1.reshape(line, 2, share, units))
        far2 = exchange_far(g2.reshape(line, 2, quarter, width))
    dctx, out_rows = tie(dctx, out_rows)

    count = 9 * share + quarter
    vec_height = -(-count // width)
    *mixed, grads, vecs = vec_call(
        functools.partial(attnback_kernel, cols=cols),
        [sds((toks, 3 * part))] * 4 + [sds((width, width)), sds((imgs, vec_height, width))],
        15,
        [
            pltpu.VMEM((part, total), F32),
            pltpu.VMEM((part, total), F32),
            pltpu.VMEM((total, 3 * part), BF),
            pltpu.VMEM((9, width), F32),
        ],
        us=18,
    )(at_tile, patch_mask, dctx, qkv, lse, hid1, nrm1, w_own, bsum, vec2, fb1, fb2, *out_rows)

    at_bucket = jnp.concatenate(
        [grads.reshape(imgs, share, width), vecs], axis=1
    )
    if direct:
        near3 = exchange_near(at_bucket.reshape(line, 2, share + vec_height, width))
        near1, (at_bucket,) = tie(near1, (at_bucket,))
        mid1 = total_of(near1).astype(BF)
        far1 = exchange_far(mid1)
        far2, (far1[0],) = tie(far2, (far1[0],))
    mixed_in = scatter_tiles(mixed)
    if direct:
        near2 = exchange_near(total_of(far2).astype(BF)[None])
        near3, (far1[0], mixed_in[0]) = tie(near3, (far1[0], mixed_in[0]))
        mid3 = total_of(near3).astype(BF)
        mixed_in[0], (mid3,) = tie(mixed_in[0], (mid3,))
        far3 = exchange_far(mid3)

    patches_grad = vec_call(
        input_kernel,
        sds((1, rows, cols, width)),
        8,
        [pltpu.VMEM((4, toks, 3 * part), BF), pltpu.VMEM((toks, width), BF)],
        us=5,
        near=(2, 3, 4),
    )(at_tile, *mixed_in, qkv_weight, patches, rgrad, norm1_gain)

    if direct:
        fc2_sum = total_of(near2)[0].astype(BF)
        far1, (patches_grad,) = tie(far1, (patches_grad,))
        fc1_sum = total_of(far1).astype(BF)
    else:
        fc1_sum, fc2_sum, at_sum = (plain_sum(b) for b in (g1, g2, at_bucket))
    fc2_pieces, _ = gather_tiles(fc2_sum)
    fc1_pieces, _ = gather_tiles(fc1_sum)
    if direct:
        far3, (patches_grad, fc2_pieces[2]) = tie(far3, (patches_grad, fc2_pieces[2]))
        at_sum = total_of(far3).astype(BF)
    fc2_grad = vec_call(
        fc2out_kernel,
        sds((4 * quarter, width), F32),
        4,
        [pltpu.VMEM((4, quarter, width), F32)],
        us=2,
        near=(2, 3, 4),
    )(at_tile, *fc2_pieces)
    fc1_grad = vec_call(
        functools.partial(fc1out_kernel, quarter=quarter),
        sds((share, ff), F32),
        4,
        [pltpu.VMEM((4, share, units), F32)],
        us=2,
        near=(2, 3, 4),
    )(at_tile, *fc1_pieces)
    at_pieces, (fc1_grad, fc2_grad) = gather_tiles(at_sum, (fc1_grad, fc2_grad))
    qkv_grad, out_grad, *vec_sums, unit_sum = vec_call(
        attnout_kernel,
        [
            sds((share, 3 * width), F32),
            sds((share, width), F32),
            *[sds((share,), F32)] * 8,
            sds((4 * quarter,), F32),
        ],
        4,
        [pltpu.VMEM((4, share + vec_height, width), F32)],
        us=3,
        near=(2, 3, 4),
    )(at_tile, *at_pieces)
    return (
        layer_out,
        patches_grad,
        vec_sums[0],
        vec_sums[1],
        qkv_grad,
        jnp.stack([vec_sums[2], vec_sums[3]], axis=1),
        out_grad,
        vec_sums[4],
        vec_sums[5],
        vec_sums[6],
        fc1_grad,
        unit_sum,
        fc2_grad,
        vec_sums[7],
    )


def solution(mesh):
    tiled = P("imgs", "rows", "cols", None)
    in_specs = (tiled, P("imgs", None, None)) + (P(),) * 12 + (tiled,)
    mat = P("imgs", None)
    vec = P("imgs")
    out_specs = (tiled, tiled, vec, vec, mat, mat, mat, vec, vec, vec, mat, vec, mat, vec)
    return jax.shard_map(layer, mesh=mesh, in_specs=in_specs, out_specs=out_specs, check_vma=False)
```
